32 devices in a mesh: section: 2 (over core), ctx: 4 (over y, x), wt: 4 (over z).
Axes of the slice: x: 2, y: 2, z: 4, core: 2. Of those that a mesh axis runs over, the one named last changes fastest.
Arguments:
- layer_input: bfloat16 [2, 1024, 2048], P(None, 'ctx'), may hold values from -6 to 6
- cotangent: bfloat16 [2, 1024, 2048], P(None, 'ctx'), may hold values from -6 to 6
- seq_lengths: int32 [2], replicated, may hold values from 256 to 1024, as said below
- adapter_ids: int32 [2], replicated, may hold values from 0 to 7
- mixer_gain: bfloat16 [2, 2048], P('section'), may hold values from 0.5 to 1.5
- feed_gain: bfloat16 [2, 2048], P('section'), may hold values from 0.5 to 1.5
- decay_rate: float32 [2, 48], P('section', 'wt'), may hold values from 0.05859375 to 20
- step_bias: float32 [2, 48], P('section', 'wt'), may hold values from -5.5 to -3.5
- skip_gain: float32 [2, 48], P('section', 'wt'), may hold values from 0.5 to 1.5
- query_weight: bfloat16 [2, 2048, 1024], P('section', None, 'wt'), may hold values from -0.125 to 0.125
- mamba_weight: bfloat16 [2, 2048, 2, 3072], P('section', None, None, 'wt'), may hold values from -0.125 to 0.125
- shared_weight: bfloat16 [2, 2048, 1072], P('section'), may hold values from -0.125 to 0.125
- attnout_weight: bfloat16 [2, 1024, 2048], P('section', 'wt'), may hold values from -3 to 3
- mambaout_weight: bfloat16 [2, 3072, 2048], P('section', 'wt'), may hold values from -0.109375 to 0.109375
- gateup_weight: bfloat16 [2, 2048, 2, 4096], P('section', None, None, 'wt'), may hold values from -0.125 to 0.125
- down_weight: bfloat16 [2, 4096, 2048], P('section', 'wt'), may hold values from -0.09375 to 0.09375
- mixin_down: bfloat16 [2, 8, 16, 2048], P('section'), may hold values from -0.125 to 0.125
- query_up: bfloat16 [2, 8, 16, 1024], P('section', None, None, 'wt'), may hold values from -0.59765625 to 0.59765625
- mamba_up: bfloat16 [2, 8, 16, 2, 3072], P('section', None, None, None, 'wt'), may hold values from -0.59765625 to 0.59765625
- shared_up: bfloat16 [2, 8, 16, 1072], P('section'), may hold values from -0.59765625 to 0.59765625
- attnout_down: bfloat16 [2, 8, 16, 1024], P('section', None, None, 'wt'), may hold values from -1.1953125 to 1.1953125
- mambaout_down: bfloat16 [2, 8, 16, 3072], P('section', None, None, 'wt'), may hold values from -0.109375 to 0.109375
- mixout_up: bfloat16 [2, 8, 16, 2048], P('section'), may hold values from -0.59765625 to 0.59765625
- feedin_down: bfloat16 [2, 8, 16, 2048], P('section'), may hold values from -0.125 to 0.125
- feedin_up: bfloat16 [2, 8, 16, 2, 4096], P('section', None, None, None, 'wt'), may hold values from -0.59765625 to 0.59765625
- feedout_down: bfloat16 [2, 8, 16, 4096], P('section', None, None, 'wt'), may hold values from -0.09375 to 0.09375
- feedout_up: bfloat16 [2, 8, 16, 2048], P('section'), may hold values from -0.59765625 to 0.59765625
Outputs:
- section_out: bfloat16 [2, 2, 1024, 2048], P('section', None, 'ctx')
- section_grad: bfloat16 [2, 2, 1024, 2048], P('section', None, 'ctx')
- grad_mixin_down: float32 [2, 8, 16, 2048], P('section')
- grad_query_up: float32 [2, 8, 16, 1024], P('section', None, None, 'wt')
- grad_mamba_up: float32 [2, 8, 16, 2, 3072], P('section', None, None, None, 'wt')
- grad_shared_up: float32 [2, 8, 16, 1072], P('section')
- grad_attnout_down: float32 [2, 8, 16, 1024], P('section', None, None, 'wt')
- grad_mambaout_down: float32 [2, 8, 16, 3072], P('section', None, None, 'wt')
- grad_mixout_up: float32 [2, 8, 16, 2048], P('section')
- grad_feedin_down: float32 [2, 8, 16, 2048], P('section')
- grad_feedin_up: float32 [2, 8, 16, 2, 4096], P('section', None, None, None, 'wt')
- grad_feedout_down: float32 [2, 8, 16, 4096], P('section', None, None, 'wt')
- grad_feedout_up: float32 [2, 8, 16, 2048], P('section')
The draws below stay inside these ranges and needn't reach their ends.
Inputs may be any that keep to these rules, and one draw needn't show every extreme that they name: Micro-batch m holds one sequence at positions 0 to seq_lengths[m] - 1 of its 1024 positions; the rest is padding. In every draw some micro-batch fills its whole slot.
All inputs are finite; a program needn't handle non-finite values.
Results may differ from the reference program's by a relative error of at most 0.035.
Values may be sent and summed in bfloat16 or wider, within the bound.
No kernel may reach another device: no remote copies, remote signals or barrier semaphores. Data moves between devices by JAX's collectives and lax.ppermute only.
A program may use at most 320 MiB of HBM per device.

```python
import math
import jax
import jax.numpy as jnp
from jax import lax

D = 2048
FF = 4096
QHEADS = 8
KVHEADS = 2
HEAD = 128
MHEADS = 48
MHEAD = 64
NSTATE = 256
RANK = 16
NADAPT = 8
MICRO = 2
SCAN_BLOCK = 64
KEY_BLOCK = 256
SLOT = 1024
SHARED = 1072


def draw_seq_lengths(key, part):
    first_key = jax.random.fold_in(key, 11)
    second_key = jax.random.fold_in(key, 12)
    drawn = jax.random.randint(first_key, (MICRO,), SLOT // 4, SLOT + 1)
    filled = jax.random.randint(second_key, (), 0, MICRO)
    return jnp.where(jnp.arange(MICRO) == filled, SLOT, drawn).astype(jnp.int32)


def shard_levels(stream_key, shape, cuts, smallest, top_value):
    def one(position, blocks):
        steps = jax.random.uniform(jax.random.fold_in(jax.random.fold_in(stream_key, 6), position), (blocks,), jnp.float32, smallest / len(cuts), top_value / len(cuts))
        return jnp.repeat(jnp.exp(steps), shape[position] // blocks).reshape((-1,) + (1,) * (len(shape) - position - 1))

    factor_of = one(*cuts[0])
    for cut in cuts[1:]:
        factor_of = factor_of * one(*cut)
    return factor_of


def centred(own_key, dims, scale, most, split=(), held_as=jnp.bfloat16):
    result = jax.random.normal(own_key, dims, jnp.float32) * scale
    if len(split) > 0:
        result = shard_levels(own_key, dims, split, -0.22, 0.18) * result
    return jnp.clip(result, min=-most, max=most).astype(held_as)


def setup_inputs(seed: int = 0) -> dict:
    key_of = jax.random.split(jax.random.key(seed), 28)
    return {
        "layer_input": centred(key_of[0], (MICRO, SLOT, D), 1.0, 6.0, ((1, 4),)),
        "cotangent": centred(key_of[1], (MICRO, SLOT, D), 1.0, 6.0, ((1, 4),)),
        "seq_lengths": draw_seq_lengths(jax.random.fold_in(key_of[27], 71), 0),
        "adapter_ids": jax.random.randint(key_of[3], (MICRO,), 0, NADAPT).astype(jnp.int32),
        "mixer_gain": jnp.clip(1.0 + 0.1 * jax.random.normal(key_of[4], (2, D), jnp.float32), 0.5, 1.5).astype(jnp.bfloat16),
        "feed_gain": jnp.clip(1.0 + 0.1 * jax.random.normal(key_of[5], (2, D), jnp.float32), 0.5, 1.5).astype(jnp.bfloat16),
        "decay_rate": jnp.clip(jnp.exp(math.log(20.0) - 5.8328595 * jax.random.uniform(key_of[6], (2, MHEADS), jnp.float32) ** shard_levels(key_of[6], (2, MHEADS), ((0, 2), (1, 4)), -0.2, 0.2)), 0.05859375, 20.0),
        "step_bias": jnp.clip(-5.5 + 2.0 * jax.random.uniform(key_of[7], (2, MHEADS), jnp.float32) ** shard_levels(key_of[7], (2, MHEADS), ((0, 2), (1, 4)), -0.2, 0.2), -5.5, -3.5),
        "skip_gain": jnp.clip(0.5 + 1.0 * jax.random.uniform(key_of[8], (2, MHEADS), jnp.float32) ** shard_levels(key_of[8], (2, MHEADS), ((0, 2), (1, 4)), -0.2, 0.2), 0.5, 1.5),
        "query_weight": centred(key_of[9], (2, D, QHEADS * HEAD), D ** -0.5, 0.125, ((0, 2), (2, 4))),
        "mamba_weight": centred(key_of[10], (2, D, 2, MHEADS * MHEAD), D ** -0.5, 0.125, ((0, 2), (3, 4))),
        "shared_weight": centred(key_of[11], (2, D, SHARED), D ** -0.5, 0.125, ((0, 2),)),
        "attnout_weight": centred(key_of[12], (2, QHEADS * HEAD, D), 0.5, 3.0, ((0, 2), (1, 4))),
        "mambaout_weight": centred(key_of[13], (2, MHEADS * MHEAD, D), (MHEADS * MHEAD) ** -0.5, 0.109375, ((0, 2), (1, 4))),
        "gateup_weight": centred(key_of[14], (2, D, 2, FF), D ** -0.5, 0.125, ((0, 2), (3, 4))),
        "down_weight": centred(key_of[15], (2, FF, D), FF ** -0.5, 0.09375, ((0, 2), (1, 4))),
        "mixin_down": centred(key_of[16], (2, NADAPT, RANK, D), D ** -0.5, 0.125, ((0, 2),)),
        "query_up": centred(key_of[17], (2, NADAPT, RANK, QHEADS * HEAD), 0.1, 0.59765625, ((0, 2), (3, 4))),
        "mamba_up": centred(key_of[18], (2, NADAPT, RANK, 2, MHEADS * MHEAD), 0.1, 0.59765625, ((0, 2), (4, 4))),
        "shared_up": centred(key_of[19], (2, NADAPT, RANK, SHARED), 0.1, 0.59765625, ((0, 2),)),
        "attnout_down": centred(key_of[20], (2, NADAPT, RANK, QHEADS * HEAD), 0.2, 1.1953125, ((0, 2), (3, 4))),
        "mambaout_down": centred(key_of[21], (2, NADAPT, RANK, MHEADS * MHEAD), (MHEADS * MHEAD) ** -0.5, 0.109375, ((0, 2), (3, 4))),
        "mixout_up": centred(key_of[22], (2, NADAPT, RANK, D), 0.1, 0.59765625, ((0, 2),)),
        "feedin_down": centred(key_of[23], (2, NADAPT, RANK, D), D ** -0.5, 0.125, ((0, 2),)),
        "feedin_up": centred(key_of[24], (2, NADAPT, RANK, 2, FF), 0.1, 0.59765625, ((0, 2), (4, 4))),
        "feedout_down": centred(key_of[25], (2, NADAPT, RANK, FF), FF ** -0.5, 0.09375, ((0, 2), (3, 4))),
        "feedout_up": centred(key_of[26], (2, NADAPT, RANK, D), 0.1, 0.59765625, ((0, 2),)),
    }


epsilon = 1e-05
rope_base = 10000.0
masked_score = -1e+30

@jax.custom_vjp
def low(v):
    return lax.optimization_barrier(v.astype(jnp.bfloat16)).astype(jnp.float32)

@jax.custom_vjp
def low_back(v):
    return v

def low_keep(v):
    return (low(v), None)

def low_pass(kept, grad):
    return (grad,)

def back_keep(v):
    return (v, None)

def back_low(kept, grad):
    return (low(grad),)
low.defvjp(low_keep, low_pass)
low_back.defvjp(back_keep, back_low)

def matmul(first_operand, second_operand):
    return jnp.dot(first_operand, second_operand, precision=lax.Precision.HIGHEST, preferred_element_type=jnp.float32)

def rms_scale(vector):
    return lax.rsqrt(lax.optimization_barrier(jnp.mean(vector * vector, axis=-1, keepdims=True)) + epsilon)

def rotate(head_values, positions, direction):
    half_width = head_values.shape[-1] // 2
    frequencies = rope_base ** (-jnp.arange(half_width, dtype=jnp.float32) / half_width)
    angles = positions.astype(jnp.float32)[:, None] * frequencies[None, :]
    cosine = jnp.cos(angles)[:, None, :]
    sine_part = direction * jnp.sin(angles)[:, None, :]
    first_half = head_values[..., :half_width]
    second_half = head_values[..., half_width:]
    return jnp.concatenate([first_half * cosine - second_half * sine_part, second_half * cosine + first_half * sine_part], axis=-1)

def scan_states(ssm_inputs, input_map, output_map, step_sizes, logdecay, state_start):
    block_count = ssm_inputs.shape[0] // SCAN_BLOCK
    pieces = (ssm_inputs.reshape(block_count, SCAN_BLOCK, ssm_inputs.shape[1], ssm_inputs.shape[2]), input_map.reshape(block_count, SCAN_BLOCK, -1), output_map.reshape(block_count, SCAN_BLOCK, -1), step_sizes.reshape(block_count, SCAN_BLOCK, -1), logdecay.reshape(block_count, SCAN_BLOCK, -1))
    causal = jnp.arange(SCAN_BLOCK)[:, None] >= jnp.arange(SCAN_BLOCK)[None, :]

    def block_step(state_now, block_parts):
        block_inputs, block_in_map, block_out_map, block_steps, block_decay = block_parts
        cumulative = jnp.cumsum(block_decay, axis=0)
        gram_matrix = matmul(block_out_map, block_in_map.T)
        differences = cumulative[:, None, :] - cumulative[None, :, :]
        decay_mask = jnp.where(causal[:, :, None], jnp.exp(jnp.minimum(differences, 0.0)), 0.0)
        weights = gram_matrix[:, :, None] * decay_mask * block_steps[None, :, :]
        within = jnp.einsum('ijh,jhp->ihp', weights, block_inputs, precision=lax.Precision.HIGHEST)
        carried = jnp.exp(cumulative)[:, :, None] * jnp.einsum('in,hnp->ihp', block_out_map, state_now, precision=lax.Precision.HIGHEST)
        tail_weight = jnp.exp(cumulative[-1][None, :] - cumulative) * block_steps
        new_state = jnp.exp(cumulative[-1])[:, None, None] * state_now + jnp.einsum('jh,jn,jhp->hnp', tail_weight, block_in_map, block_inputs, precision=lax.Precision.HIGHEST)
        return (new_state, within + carried)
    final_state, outputs = lax.scan(jax.checkpoint(block_step), state_start, pieces)
    return (outputs.reshape(ssm_inputs.shape), final_state)

def attention(queries, key_rows, value_rows, length):
    span_len = queries.shape[0]
    group_size = QHEADS // KVHEADS
    keys_all = jnp.repeat(key_rows, group_size, axis=1)
    values_all = jnp.repeat(value_rows, group_size, axis=1)
    key_pos = jnp.arange(span_len, dtype=jnp.int32)
    score_scale = HEAD ** (-0.5)

    def query_block(block_index):
        block_start = (block_index * KEY_BLOCK).astype(jnp.int32)
        block_queries = lax.dynamic_slice_in_dim(queries, block_start, KEY_BLOCK, 0)
        query_pos = block_start + jnp.arange(KEY_BLOCK, dtype=jnp.int32)
        scores = low_back(score_scale * jnp.einsum('qhd,khd->hqk', block_queries, keys_all, precision=lax.Precision.HIGHEST))
        allowed = (key_pos[None, :] <= query_pos[:, None]) & (key_pos[None, :] < length)
        probabilities = jax.nn.softmax(jnp.where(allowed[None], scores, masked_score), axis=-1)
        return jnp.einsum('hqk,khd->qhd', low(probabilities), values_all, precision=lax.Precision.HIGHEST)
    blocks_out = lax.map(jax.checkpoint(query_block), jnp.arange(span_len // KEY_BLOCK, dtype=jnp.int32))
    return blocks_out.reshape(span_len, -1)

def layer(layer_entry, fixed_params, adapters, layer_index, adapter, length):
    mixer_gain, feed_gain, decay_rate, step_bias, skip_gain, query_weight, mamba_weight, shared_weight, attnout_weight, mambaout_weight, gateup_weight, down_weight = [item[layer_index] for item in fixed_params]
    mixin_down, query_up, mamba_up, shared_up, attnout_down, mambaout_down, mixout_up, feedin_down, feedin_up, feedout_down, feedout_up = [item[layer_index][adapter] for item in adapters]
    span_len = layer_entry.shape[0]
    positions = jnp.arange(span_len, dtype=jnp.int32)
    live_mask = (positions < length).astype(jnp.float32)
    normed = low(layer_entry * rms_scale(layer_entry) * mixer_gain)
    small_in = matmul(normed, mixin_down.T)
    query_proj = low_back(matmul(normed, query_weight) + matmul(small_in, query_up))
    mamba_proj = low_back(matmul(normed, mamba_weight.reshape(D, -1)) + matmul(small_in, mamba_up.reshape(RANK, -1)))
    shared = low_back(matmul(normed, shared_weight) + matmul(small_in, shared_up))
    pair_width = KVHEADS * HEAD
    queries = low(rotate(query_proj.reshape(span_len, QHEADS, HEAD), positions, 1.0))
    key_rows = low(rotate(shared[:, :pair_width].reshape(span_len, KVHEADS, HEAD), positions, 1.0))
    value_rows = low(shared[:, pair_width:2 * pair_width].reshape(span_len, KVHEADS, HEAD))
    attended = low(low_back(attention(queries, key_rows, value_rows, length)))
    offset = 2 * pair_width
    input_map = shared[:, offset:offset + NSTATE]
    output_map = shared[:, offset + NSTATE:offset + 2 * NSTATE]
    step_raw = shared[:, offset + 2 * NSTATE:]
    step_sizes = jax.nn.softplus(step_raw + step_bias) * live_mask[:, None]
    logdecay = -decay_rate * step_sizes
    mamba_width = MHEADS * MHEAD
    gate_raw = mamba_proj[:, :mamba_width]
    ssm_inputs = mamba_proj[:, mamba_width:].reshape(span_len, MHEADS, MHEAD)
    start_state = jnp.zeros((MHEADS, NSTATE, MHEAD), jnp.float32)
    scanned, final_state = scan_states(ssm_inputs, input_map, output_map, step_sizes, logdecay, start_state)
    gated_out = low((scanned + skip_gain[None, :, None] * ssm_inputs).reshape(span_len, -1) * jax.nn.silu(gate_raw))
    joined = jnp.concatenate([attended, gated_out], axis=1)
    out_weight = jnp.concatenate([attnout_weight, mambaout_weight], axis=0)
    out_down = jnp.concatenate([attnout_down, mambaout_down], axis=1)
    small_mid = matmul(joined, out_down.T)
    mixed_out = low_back(matmul(joined, out_weight) + matmul(small_mid, mixout_up))
    hidden = layer_entry + live_mask[:, None] * mixed_out
    feed_normed = low(hidden * rms_scale(hidden) * feed_gain)
    small_feed = matmul(feed_normed, feedin_down.T)
    gateup = low_back(matmul(feed_normed, gateup_weight.reshape(D, -1)) + matmul(small_feed, feedin_up.reshape(RANK, -1)))
    inner = low(jax.nn.silu(gateup[:, :FF]) * gateup[:, FF:])
    small_out = matmul(inner, feedout_down.T)
    feed_out = low_back(matmul(inner, down_weight) + matmul(small_out, feedout_up))
    return hidden + feed_out

def reference(layer_input, cotangent, seq_lengths, adapter_ids, mixer_gain, feed_gain, decay_rate, step_bias, skip_gain, query_weight, mamba_weight, shared_weight, attnout_weight, mambaout_weight, gateup_weight, down_weight, mixin_down, query_up, mamba_up, shared_up, attnout_down, mambaout_down, mixout_up, feedin_down, feedin_up, feedout_down, feedout_up):
    fixed_params = tuple((item.astype(jnp.float32) for item in (mixer_gain, feed_gain, decay_rate, step_bias, skip_gain, query_weight, mamba_weight, shared_weight, attnout_weight, mambaout_weight, gateup_weight, down_weight)))
    adapters = tuple((item.astype(jnp.float32) for item in (mixin_down, query_up, mamba_up, shared_up, attnout_down, mambaout_down, mixout_up, feedin_down, feedin_up, feedout_down, feedout_up)))
    inputs = layer_input.astype(jnp.float32)
    middle_zeros = jnp.zeros_like(inputs)

    def forward(inputs, middle, adapters):
        first_outs = []
        second_outs = []
        for micro_index in range(MICRO):
            adapter = adapter_ids[micro_index]
            length = seq_lengths[micro_index]
            first_layer = layer(inputs[micro_index], fixed_params, adapters, 0, adapter, length)
            passed = low_back(low(first_layer) + middle[micro_index])
            second_layer = layer(passed, fixed_params, adapters, 1, adapter, length)
            first_outs.append(first_layer)
            second_outs.append(second_layer)
        return (jnp.stack(first_outs), jnp.stack(second_outs))
    (first_all, second_all), pullback = jax.vjp(forward, inputs, middle_zeros, adapters)
    grad_inputs, grad_middle, grad_adapters = pullback((jnp.zeros_like(first_all), cotangent.astype(jnp.float32)))
    section_out = jnp.stack([first_all, second_all]).astype(jnp.bfloat16)
    section_grad = jnp.stack([grad_inputs, grad_middle]).astype(jnp.bfloat16)
    return (section_out, section_grad, grad_adapters[0], grad_adapters[1], grad_adapters[2], grad_adapters[3], grad_adapters[4], grad_adapters[5], grad_adapters[6], grad_adapters[7], grad_adapters[8], grad_adapters[9], grad_adapters[10])
```

```python
import functools

import jax
import jax.numpy as jnp
from jax import lax
from jax.experimental import pallas as pl
from jax.experimental.pallas import tpu as pltpu
from jax.sharding import PartitionSpec as P

QHEADS = 8
KVHEADS = 2
HEAD = 128
MHEAD = 64
NSTATE = 256
KEY_BLOCK = 256
PAIR = 2 * MHEAD

epsilon = 1e-05
rope_base = 10000.0
masked_score = -1e30
BF = jnp.bfloat16
F32 = jnp.float32
HIGH = lax.Precision.HIGHEST


def mm(a, b):
    return jnp.dot(a.astype(BF), b.astype(BF), preferred_element_type=F32)


def mm_t(a, b):
    return lax.dot_general(
        a.astype(BF), b.astype(BF), (((1,), (1,)), ((), ())), preferred_element_type=F32
    )


def t_mm(a, b):
    return lax.dot_general(
        a.astype(BF), b.astype(BF), (((0,), (0,)), ((), ())), preferred_element_type=F32
    )


def rms_scale(vector):
    return lax.rsqrt(jnp.mean(vector * vector, axis=-1, keepdims=True) + epsilon)


def norm_back(vector, grad_normed, gain_vec):
    scale_now = rms_scale(vector)
    weighted = grad_normed * gain_vec
    return weighted * scale_now - vector * scale_now**3 * jnp.mean(
        weighted * vector, axis=-1, keepdims=True
    )


def vmem_call(kernel, out_shape, **kwargs):
    return pl.pallas_call(
        kernel,
        out_shape=out_shape,
        compiler_params=pltpu.CompilerParams(vmem_limit_bytes=56 * 1024 * 1024),
        **kwargs,
    )


def pair_lanes(rows, left, right):
    lane = lax.broadcasted_iota(jnp.int32, (rows, PAIR), 1)
    return jnp.where(lane < MHEAD, left, right)


def scan_forward_kernel(x_ref, b_ref, c_ref, dt_ref, cum_ref, cumt_ref, y_ref, state_ref, tail_scr):
    rows = x_ref.shape[0]
    heads = dt_ref.shape[1]
    gram = mm_t(c_ref[...], b_ref[...])
    row = lax.broadcasted_iota(jnp.int32, (rows, rows), 0)
    col = lax.broadcasted_iota(jnp.int32, (rows, rows), 1)
    gram = jnp.where(row >= col, gram, 0.0)
    cum = cum_ref[...]
    dt = dt_ref[...]
    cumt = cumt_ref[...]
    tail = jnp.exp(cum[rows - 1 : rows, :] - cum)
    for pair in range(heads // 2):
        one, two = 2 * pair, 2 * pair + 1
        lanes = slice(PAIR * pair, PAIR * (pair + 1))
        scaled = x_ref[:, lanes] * pair_lanes(rows, dt[:, one : one + 1], dt[:, two : two + 1])
        scaled_low = scaled.astype(BF)
        tail_scr[:, lanes] = (
            scaled * pair_lanes(rows, tail[:, one : one + 1], tail[:, two : two + 1])
        ).astype(BF)
        parts = []
        for head in (one, two):
            decay = jnp.exp(jnp.minimum(cum[:, head : head + 1] - cumt[head : head + 1, :], 0.0))
            parts.append(mm((gram * decay), scaled_low))
        y_ref[:, lanes] = pair_lanes(rows, parts[0], parts[1])
    state_ref[...] = t_mm(b_ref[...], tail_scr[...]).astype(state_ref.dtype)


def scan_forward(x, b_low, c_low, dt, cum, cumt):
    rows, width = x.shape
    return vmem_call(
        scan_forward_kernel,
        (
            jax.ShapeDtypeStruct((rows, width), F32),
            jax.ShapeDtypeStruct((b_low.shape[1], width), BF),
        ),
        scratch_shapes=[pltpu.VMEM((rows, width), BF)],
    )(x, b_low, c_low, dt, cum, cumt)


def scan_backward_kernel(
    x_ref, dy_ref, b_ref, c_ref, dt_ref, cum_ref, cumt_ref, z_ref, db_ref, dc_ref
):
    rows = x_ref.shape[0]
    heads = dt_ref.shape[1]
    gram_t = mm_t(b_ref[...], c_ref[...])
    row = lax.broadcasted_iota(jnp.int32, (rows, rows), 0)
    col = lax.broadcasted_iota(jnp.int32, (rows, rows), 1)
    causal = col >= row
    gram_t = jnp.where(causal, gram_t, 0.0)
    cum = cum_ref[...]
    dt = dt_ref[...]
    cumt = cumt_ref[...]
    grad_gram_t = jnp.zeros((rows, rows), F32)
    lane = lax.broadcasted_iota(jnp.int32, (rows, PAIR), 1)
    for pair in range(heads // 2):
        one, two = 2 * pair, 2 * pair + 1
        lanes = slice(PAIR * pair, PAIR * (pair + 1))
        scaled_low = (
            x_ref[:, lanes] * pair_lanes(rows, dt[:, one : one + 1], dt[:, two : two + 1])
        ).astype(BF)
        dy = dy_ref[:, lanes]
        parts = []
        for head in (one, two):
            decay = jnp.exp(jnp.minimum(cumt[head : head + 1, :] - cum[:, head : head + 1], 0.0))
            parts.append(mm(gram_t * decay, dy))
            mine = (lane < MHEAD) if head == one else (lane >= MHEAD)
            outer = mm_t(jnp.where(mine, scaled_low, jnp.zeros_like(scaled_low)), dy)
            grad_gram_t = grad_gram_t + decay * outer
        z_ref[:, lanes] = pair_lanes(rows, parts[0], parts[1])
    grad_low = jnp.where(causal, grad_gram_t, 0.0).astype(BF)
    db_ref[...] = mm(grad_low, c_ref[...])
    dc_ref[...] = t_mm(grad_low, b_ref[...])


def scan_backward(x, dy_low, b_low, c_low, dt, cum, cumt):
    rows, width = x.shape
    states = b_low.shape[1]
    return vmem_call(
        scan_backward_kernel,
        (
            jax.ShapeDtypeStruct((rows, width), F32),
            jax.ShapeDtypeStruct((rows, states), F32),
            jax.ShapeDtypeStruct((rows, states), F32),
        ),
    )(x, dy_low, b_low, c_low, dt, cum, cumt)


def block_mask(scores_shape, span, block, ctx_index, length):
    row = lax.broadcasted_iota(jnp.int32, scores_shape, 0)
    query_pos = ctx_index * span + lax.rem(row, span)
    key_pos = block * KEY_BLOCK + lax.broadcasted_iota(jnp.int32, scores_shape, 1)
    return (key_pos <= query_pos) & (key_pos < length)


def attend_forward_kernel(place_ref, q_ref, kv_ref, out_ref, lse_ref, top_scr, sum_scr):
    span = out_ref.shape[0]
    heads = q_ref.shape[0] // span
    length, ctx_index, blocks = place_ref[0], place_ref[1], place_ref[2]
    queries = q_ref[...]
    rows = queries.shape[0]
    top_scr[...] = jnp.full(top_scr.shape, masked_score, F32)
    sum_scr[...] = jnp.zeros(sum_scr.shape, F32)
    lse_ref[...] = jnp.zeros(lse_ref.shape, F32)

    def step(block, nothing):
        start = pl.multiple_of(block * KEY_BLOCK, KEY_BLOCK)
        keys = kv_ref[pl.ds(start, KEY_BLOCK), :HEAD]
        values = kv_ref[pl.ds(start, KEY_BLOCK), HEAD:]
        scores = HEAD ** (-0.5) * mm_t(queries, keys)
        allowed = block_mask(scores.shape, span, block, ctx_index, length)
        scores = jnp.where(allowed, scores, masked_score)
        top = top_scr[...]
        fresh_top = jnp.maximum(top, jnp.max(scores, axis=1, keepdims=True))
        shares = jnp.where(allowed, jnp.exp(scores - fresh_top), 0.0)
        fade = jnp.exp(top - fresh_top)
        lse_ref[...] = lse_ref[...] * fade + jnp.sum(shares, axis=1, keepdims=True)
        sum_scr[...] = sum_scr[...] * fade + mm(shares, values)
        top_scr[...] = fresh_top
        return nothing

    lax.fori_loop(0, blocks, step, 0)
    total = lse_ref[...]
    result = sum_scr[...] / total
    for head in range(heads):
        out_ref[:, head * HEAD : (head + 1) * HEAD] = result[head * span : (head + 1) * span, :]
    lse_ref[...] = top_scr[...] + jnp.log(total)


def attend_forward(place, query_rows, key_all, span):
    rows = query_rows.shape[0]
    return pl.pallas_call(
        attend_forward_kernel,
        out_shape=(
            jax.ShapeDtypeStruct((span, rows // span * HEAD), F32),
            jax.ShapeDtypeStruct((rows, 1), F32),
        ),
        in_specs=[
            pl.BlockSpec(memory_space=pltpu.SMEM),
            pl.BlockSpec(memory_space=pltpu.VMEM),
            pl.BlockSpec(memory_space=pltpu.VMEM),
        ],
        scratch_shapes=[pltpu.VMEM((rows, 1), F32), pltpu.VMEM((rows, HEAD), F32)],
        compiler_params=pltpu.CompilerParams(vmem_limit_bytes=56 * 1024 * 1024),
    )(place, query_rows, key_all)


def attend_backward_kernel(
    place_ref, q_ref, kv_ref, lse_ref, out_ref, grad_ref, dq_ref, dkv_ref, dq_scr
):
    span = out_ref.shape[0]
    heads = q_ref.shape[0] // span
    length, ctx_index, blocks = place_ref[0], place_ref[1], place_ref[2]
    queries = q_ref[...]
    grad_rows = jnp.concatenate(
        [grad_ref[:, head * HEAD : (head + 1) * HEAD] for head in range(heads)], axis=0
    )
    out_rows = jnp.concatenate(
        [out_ref[:, head * HEAD : (head + 1) * HEAD] for head in range(heads)], axis=0
    )
    delta = jnp.sum(grad_rows.astype(F32) * out_rows, axis=1, keepdims=True)
    lse = lse_ref[...]
    dq_scr[...] = jnp.zeros(dq_scr.shape, F32)
    dkv_ref[...] = jnp.zeros(dkv_ref.shape, dkv_ref.dtype)

    def step(block, nothing):
        start = pl.multiple_of(block * KEY_BLOCK, KEY_BLOCK)
        keys = kv_ref[pl.ds(start, KEY_BLOCK), :HEAD]
        values = kv_ref[pl.ds(start, KEY_BLOCK), HEAD:]
        scores = HEAD ** (-0.5) * mm_t(queries, keys)
        allowed = block_mask(scores.shape, span, block, ctx_index, length)
        shares = jnp.where(allowed, jnp.exp(jnp.where(allowed, scores, masked_score) - lse), 0.0)
        grad_share = mm_t(grad_rows, values)
        grad_score = (shares * (grad_share - delta)).astype(BF)
        dq_scr[...] += mm(grad_score, keys)
        dkv_ref[pl.ds(start, KEY_BLOCK), :HEAD] = (
            HEAD ** (-0.5) * t_mm(grad_score, queries)
        ).astype(dkv_ref.dtype)
        dkv_ref[pl.ds(start, KEY_BLOCK), HEAD:] = t_mm(shares, grad_rows).astype(dkv_ref.dtype)
        return nothing

    lax.fori_loop(0, blocks, step, 0)
    for head in range(heads):
        dq_ref[:, head * HEAD : (head + 1) * HEAD] = (
            HEAD ** (-0.5) * dq_scr[head * span : (head + 1) * span, :]
        )


def attend_backward(place, query_rows, key_all, lse, attended, grad_low):
    span = attended.shape[0]
    rows = query_rows.shape[0]
    vm = pl.BlockSpec(memory_space=pltpu.VMEM)
    return pl.pallas_call(
        attend_backward_kernel,
        out_shape=(
            jax.ShapeDtypeStruct(attended.shape, F32),
            jax.ShapeDtypeStruct(key_all.shape, BF),
        ),
        in_specs=[pl.BlockSpec(memory_space=pltpu.SMEM), vm, vm, vm, vm, vm],
        scratch_shapes=[pltpu.VMEM((rows, HEAD), F32)],
        compiler_params=pltpu.CompilerParams(vmem_limit_bytes=56 * 1024 * 1024),
    )(place, query_rows, key_all, lse, attended, grad_low)


def swap(value):
    return lax.ppermute(value, "section", [(0, 1), (1, 0)])


def shifted(value, steps):
    count = lax.axis_size("ctx")
    first, last = max(0, -steps), min(count, count - steps)
    return lax.ppermute(value, "ctx", [(source, source + steps) for source in range(first, last)])


def rope_tables(positions):
    half_width = HEAD // 2
    frequencies = rope_base ** (-jnp.arange(half_width, dtype=F32) / half_width)
    angles = positions.astype(F32)[:, None] * frequencies[None, :]
    return jnp.cos(angles), jnp.sin(angles)


def rotate(values, tables, direction):
    half_width = HEAD // 2
    cosine, sine = tables[0], direction * tables[1]
    heads = []
    for head in range(values.shape[1] // HEAD):
        first = values[:, head * HEAD : head * HEAD + half_width]
        second = values[:, head * HEAD + half_width : (head + 1) * HEAD]
        heads.append(first * cosine - second * sine)
        heads.append(second * cosine + first * sine)
    return jnp.concatenate(heads, axis=1)


def carried_states(local_state, total_decay, reverse):
    count = lax.axis_size("ctx")
    here = lax.axis_index("ctx")
    totals = lax.all_gather(total_decay, "ctx", axis=0)
    summed = jnp.zeros(local_state.shape, F32)
    between = jnp.zeros(total_decay.shape, F32)
    for steps in range(1, count):
        moved = shifted(local_state, -steps if reverse else steps).astype(F32)
        factor = jnp.repeat(jnp.exp(between), MHEAD)[None, :]
        summed = summed + factor * moved
        source = here + steps if reverse else here - steps
        passed = lax.dynamic_index_in_dim(
            totals, jnp.clip(source, 0, count - 1), 0, keepdims=False
        )
        between = between + passed
    return summed


def wide(per_head):
    return jnp.repeat(per_head, MHEAD, axis=1)


def head_sum(values):
    return jnp.sum(values.reshape(values.shape[0], -1, MHEAD), axis=2)


def low_sum(value):
    return lax.psum(value.astype(BF), "wt").astype(F32)


class Weights:
    pass


def layer_forward(entry_low, w, place):
    saved = {"entry": entry_low}
    entry = entry_low.astype(F32)
    normed = (entry * rms_scale(entry) * w.mixer_gain).astype(BF)
    small_in = mm_t(normed, w.mixin_down)
    small_in_low = small_in.astype(BF)
    query_proj = mm(normed, w.query) + mm(small_in_low, w.query_up)
    mamba_proj = mm(normed, w.mamba) + mm(small_in_low, w.mamba_up)
    shared = mm(normed, w.shared) + mm(small_in_low, w.shared_up)
    span = entry.shape[0]
    local_heads = query_proj.shape[1] // HEAD
    key_head = place.wt * local_heads // (QHEADS // KVHEADS)
    rotated = rotate(query_proj, place.tables, 1.0).astype(BF)
    query_rows = jnp.concatenate(
        [rotated[:, head * HEAD : (head + 1) * HEAD] for head in range(local_heads)], axis=0
    )
    key_part = lax.dynamic_slice_in_dim(shared, key_head * HEAD, HEAD, 1)
    value_part = lax.dynamic_slice_in_dim(shared, (KVHEADS + key_head) * HEAD, HEAD, 1)
    key_value = jnp.concatenate([rotate(key_part, place.tables, 1.0), value_part], axis=1)
    key_all = lax.all_gather(key_value.astype(BF), "ctx", axis=0, tiled=True)

    half = mamba_proj.shape[1] // 2
    heads = half // MHEAD
    gate_raw, inputs = mamba_proj[:, :half], mamba_proj[:, half:]
    offset = 2 * KVHEADS * HEAD
    input_map = shared[:, offset : offset + NSTATE].astype(BF)
    output_map = shared[:, offset + NSTATE : offset + 2 * NSTATE].astype(BF)
    step_raw = lax.dynamic_slice_in_dim(
        shared, offset + 2 * NSTATE + place.wt * heads, heads, 1
    )
    step_in = step_raw + w.step_bias
    step_sizes = jax.nn.softplus(step_in) * place.live[:, None]
    cum = jnp.cumsum(-w.decay_rate * step_sizes, axis=0)
    total = cum[-1]
    local_y, local_state = scan_forward(
        inputs, input_map, output_map, step_sizes, cum, cum.T
    )
    attended, lse = attend_forward(place.scalars, query_rows, key_all, span)
    state_in = carried_states(local_state, total, False).astype(BF)
    scanned = local_y + wide(jnp.exp(cum)) * mm(output_map, state_in)
    joined = scanned + jnp.repeat(w.skip_gain, MHEAD)[None, :] * inputs
    gated_low = (joined * jax.nn.silu(gate_raw)).astype(BF)
    attended_low = attended.astype(BF)
    small_mid = mm_t(attended_low, w.attnout_down) + mm_t(gated_low, w.mambaout_down)
    part = (
        mm(attended_low, w.attnout) + mm(gated_low, w.mambaout) + mm(small_mid, w.mixout_up)
    )
    hidden = entry + place.live[:, None] * low_sum(part)

    feed_normed = (hidden * rms_scale(hidden) * w.feed_gain).astype(BF)
    small_feed = mm_t(feed_normed, w.feedin_down)
    gateup = mm(feed_normed, w.gateup) + mm(small_feed, w.feedin_up)
    width = gateup.shape[1] // 2
    gate_value, up_value = gateup[:, :width], gateup[:, width:]
    inner = (jax.nn.silu(gate_value) * up_value).astype(BF)
    small_out = mm_t(inner, w.feedout_down)
    feed_part = mm(inner, w.down) + mm(small_out, w.feedout_up)
    result = hidden + low_sum(feed_part)
    saved.update(
        normed=normed,
        small_in=small_in_low,
        query_rows=query_rows,
        key_all=key_all,
        key_head=key_head,
        gate_raw=gate_raw,
        inputs=inputs,
        input_map=input_map,
        output_map=output_map,
        step_in=step_in,
        step_sizes=step_sizes,
        cum=cum,
        local_state=local_state,
        state_in=state_in,
        scanned=scanned,
        attended=attended,
        lse=lse,
        gated_low=gated_low,
        attended_low=attended_low,
        small_mid=small_mid,
        hidden=hidden,
        feed_normed=feed_normed,
        small_feed=small_feed,
        gate_value=gate_value,
        up_value=up_value,
        inner=inner,
        small_out=small_out,
    )
    return result, saved


def layer_backward(grad_out, w, place, s):
    grads = {}
    span = grad_out.shape[0]
    grad_feed = grad_out.astype(BF)
    grad_small_out = mm_t(grad_feed, w.feedout_up)
    grads["feedout_up"] = t_mm(s["small_out"], grad_feed)
    grads["feedout_down"] = t_mm(grad_small_out, s["inner"])
    grad_inner = mm_t(grad_feed, w.down) + mm(grad_small_out, w.feedout_down)
    gate_value, up_value = s["gate_value"], s["up_value"]
    sigmoid_gate = jax.nn.sigmoid(gate_value)
    grad_gate = grad_inner * up_value * sigmoid_gate * (1.0 + gate_value * (1.0 - sigmoid_gate))
    grad_up = grad_inner * gate_value * sigmoid_gate
    grad_gateup = jnp.concatenate([grad_gate, grad_up], axis=1).astype(BF)
    grad_small_feed = mm_t(grad_gateup, w.feedin_up)
    grads["feedin_up"] = t_mm(s["small_feed"], grad_gateup)
    grads["feedin_down"] = t_mm(grad_small_feed, s["feed_normed"])
    feed_norm_part = mm_t(grad_gateup, w.gateup) + mm(grad_small_feed, w.feedin_down)
    grad_hidden = grad_out + norm_back(s["hidden"], low_sum(feed_norm_part), w.feed_gain)

    grad_mixed = (grad_hidden * place.live[:, None]).astype(BF)
    grad_small_mid = mm_t(grad_mixed, w.mixout_up)
    grads["mixout_up"] = t_mm(s["small_mid"], grad_mixed)
    grads["attnout_down"] = t_mm(grad_small_mid, s["attended_low"])
    grads["mambaout_down"] = t_mm(grad_small_mid, s["gated_low"])
    grad_gated = mm_t(grad_mixed, w.mambaout) + mm(grad_small_mid, w.mambaout_down)
    gate_raw, inputs, scanned = s["gate_raw"], s["inputs"], s["scanned"]
    skip = jnp.repeat(w.skip_gain, MHEAD)[None, :]
    sigmoid_raw = jax.nn.sigmoid(gate_raw)
    silu_raw = gate_raw * sigmoid_raw
    dy_low = (grad_gated * silu_raw).astype(BF)
    dy = dy_low.astype(F32)
    grad_gates = (
        grad_gated * (scanned + skip * inputs) * sigmoid_raw * (1.0 + gate_raw * (1.0 - sigmoid_raw))
    )
    cum, step_sizes = s["cum"], s["step_sizes"]
    grown = wide(jnp.exp(cum))
    grown_dy = (grown * dy).astype(BF)
    local_grad = t_mm(s["output_map"], grown_dy)
    grad_state = carried_states(local_grad.astype(BF), cum[-1], True).astype(BF)

    grad_attended = (
        mm_t(grad_mixed, w.attnout) + mm(grad_small_mid, w.attnout_down)
    ).astype(BF)
    grad_query, grad_keyval = attend_backward(
        place.scalars, s["query_rows"], s["key_all"], s["lse"], s["attended"], grad_attended
    )
    own = lax.psum_scatter(grad_keyval, "ctx", scatter_dimension=0, tiled=True).astype(F32)

    z_local, db_local, dc_local = scan_backward(
        inputs, dy_low, s["input_map"], s["output_map"], step_sizes, cum, cum.T
    )
    dt_wide = wide(step_sizes)
    tail = wide(jnp.exp(cum[-1:] - cum))
    scaled_low = (inputs * dt_wide).astype(BF)
    scaled = scaled_low.astype(F32)
    z_tail = tail * mm(s["input_map"], grad_state)
    z_all = z_local + z_tail
    grad_inputs = dt_wide * z_all + skip * dy
    grad_map_in = db_local + mm_t((tail * scaled), grad_state)
    grad_map_out = dc_local + mm_t(grown_dy, s["state_in"])
    kept = jnp.sum(
        grad_state.astype(F32) * s["state_in"].astype(F32), axis=0
    )[None, :] * jnp.repeat(jnp.exp(cum[-1]), MHEAD)[None, :]
    edge = head_sum(jnp.sum(scaled * z_tail, axis=0, keepdims=True) + kept)
    through = head_sum(dy * scanned - scaled * z_all)
    cum_grad = edge + jnp.flip(jnp.cumsum(jnp.flip(through, 0), axis=0), 0)
    grad_steps = head_sum(inputs * z_all) - w.decay_rate * cum_grad
    grad_step = grad_steps * jax.nn.sigmoid(s["step_in"]) * place.live[:, None]

    heads = cum.shape[1]
    grad_query_low = rotate(grad_query, place.tables, -1.0).astype(BF)
    grad_keys = rotate(own[:, :HEAD], place.tables, -1.0)
    key_head = s["key_head"]
    offset = 2 * KVHEADS * HEAD
    keyval = jnp.zeros((span, offset), F32)
    keyval = lax.dynamic_update_slice_in_dim(keyval, grad_keys, key_head * HEAD, 1)
    keyval = lax.dynamic_update_slice_in_dim(
        keyval, own[:, HEAD:], (KVHEADS + key_head) * HEAD, 1
    )
    all_heads = w.shared.shape[1] - offset - 2 * NSTATE
    step_part = lax.dynamic_update_slice_in_dim(
        jnp.zeros((span, all_heads), F32), grad_step, place.wt * heads, 1
    )
    grad_shared = jnp.concatenate(
        [keyval, grad_map_in, grad_map_out, step_part], axis=1
    ).astype(BF)
    grad_mamba = jnp.concatenate([grad_gates, grad_inputs], axis=1).astype(BF)
    grad_small_in = (
        mm_t(grad_query_low, w.query_up)
        + mm_t(grad_mamba, w.mamba_up)
        + mm_t(grad_shared, w.shared_up)
    )
    grads["query_up"] = t_mm(s["small_in"], grad_query_low)
    grads["mamba_up"] = t_mm(s["small_in"], grad_mamba)
    grads["shared_up"] = t_mm(s["small_in"], grad_shared)
    grads["mixin_down"] = t_mm(grad_small_in, s["normed"])
    norm_part = (
        mm_t(grad_query_low, w.query)
        + mm_t(grad_mamba, w.mamba)
        + mm_t(grad_shared, w.shared)
        + mm(grad_small_in, w.mixin_down)
    )
    grad_entry = grad_hidden + norm_back(
        s["entry"].astype(F32), low_sum(norm_part), w.mixer_gain
    )
    return grad_entry, grads


FIXED = (
    "mixer_gain",
    "feed_gain",
    "decay_rate",
    "step_bias",
    "skip_gain",
    "query",
    "mamba",
    "shared",
    "attnout",
    "mambaout",
    "gateup",
    "down",
)
ADAPTERS = (
    "mixin_down",
    "query_up",
    "mamba_up",
    "shared_up",
    "attnout_down",
    "mambaout_down",
    "mixout_up",
    "feedin_down",
    "feedin_up",
    "feedout_down",
    "feedout_up",
)
REPLICATED = ("mixin_down", "shared_up", "mixout_up", "feedin_down", "feedout_up")


def shards(layer_input, cotangent, seq_lengths, adapter_ids, *params):
    section = lax.axis_index("section")
    ctx_index = lax.axis_index("ctx")
    micro_count, span = layer_input.shape[0], layer_input.shape[1]
    assert micro_count == 2 and lax.axis_size("section") == 2

    place = Weights()
    place.wt = lax.axis_index("wt")
    length = seq_lengths[section]
    positions = ctx_index * span + jnp.arange(span, dtype=jnp.int32)
    place.live = (positions < length).astype(F32)
    place.tables = rope_tables(positions)
    blocks = jnp.minimum(
        ((ctx_index + 1) * span + KEY_BLOCK - 1) // KEY_BLOCK, (length + KEY_BLOCK - 1) // KEY_BLOCK
    )
    place.scalars = jnp.stack([length, ctx_index, blocks]).astype(jnp.int32)

    own, other = {}, {}
    shapes = {}
    for name, item in zip(FIXED, params):
        value = item[0]
        if name in ("mamba", "gateup"):
            value = value.reshape(value.shape[0], -1)
        own[name] = value
        other[name] = swap(value)
    mine, theirs = adapter_ids[section], adapter_ids[1 - section]
    for name, item in zip(ADAPTERS, params[len(FIXED) :]):
        shapes[name] = item.shape[1:]
        flat = item[0].reshape(item.shape[1], item.shape[2], -1)
        own[name] = lax.dynamic_index_in_dim(flat, mine, 0, keepdims=False)
        other[name] = swap(lax.dynamic_index_in_dim(flat, theirs, 0, keepdims=False))

    layers = []
    for index in range(2):
        w = Weights()
        for name in own:
            setattr(w, name, jnp.where(section == index, own[name], other[name]))
        layers.append(w)

    entry = lax.dynamic_index_in_dim(layer_input, section, 0, keepdims=False)
    saved, outs = [], []
    for w in layers:
        result, kept = layer_forward(entry, w, place)
        entry = result.astype(BF)
        outs.append(entry)
        saved.append(kept)

    grad = lax.dynamic_index_in_dim(cotangent, section, 0, keepdims=False).astype(F32)
    grad_lows, grad_sets = [None, None], [None, None]
    for index in (1, 0):
        grad, found = layer_backward(grad, layers[index], place, saved[index])
        grad_low = grad.astype(BF)
        grad_lows[index] = grad_low
        grad = grad_low.astype(F32)
        summed = {}
        replicated = lax.psum(tuple(found[name] for name in REPLICATED), ("ctx", "wt"))
        summed.update(zip(REPLICATED, replicated))
        for name in ADAPTERS:
            if name not in REPLICATED:
                summed[name] = lax.psum(found[name].astype(BF), "ctx")
        grad_sets[index] = summed

    def by_layer(values):
        keep = jnp.where(section == 0, values[0], values[1])
        moved = swap(jnp.where(section == 0, values[1], values[0]))
        return keep, moved

    def stacked(values):
        keep, moved = by_layer(values)
        return jnp.stack(
            [jnp.where(section == 0, keep, moved), jnp.where(section == 0, moved, keep)]
        )[None]

    results = [stacked(outs), stacked(grad_lows)]
    for name in ADAPTERS:
        keep, moved = by_layer((grad_sets[0][name], grad_sets[1][name]))
        shape = shapes[name]
        total = jnp.zeros((shape[0],) + keep.shape, F32)
        total = total.at[mine].add(keep.astype(F32)).at[theirs].add(moved.astype(F32))
        results.append(total.reshape(shape)[None])
    return tuple(results)


def solution(mesh):
    in_specs = (
        P(None, "ctx", None),
        P(None, "ctx", None),
        P(),
        P(),
        P("section", None),
        P("section", None),
        P("section", "wt"),
        P("section", "wt"),
        P("section", "wt"),
        P("section", None, "wt"),
        P("section", None, None, "wt"),
        P("section", None, None),
        P("section", "wt", None),
        P("section", "wt", None),
        P("section", None, None, "wt"),
        P("section", "wt", None),
        P("section", None, None, None),
        P("section", None, None, "wt"),
        P("section", None, None, None, "wt"),
        P("section", None, None, None),
        P("section", None, None, "wt"),
        P("section", None, None, "wt"),
        P("section", None, None, None),
        P("section", None, None, None),
        P("section", None, None, None, "wt"),
        P("section", None, None, "wt"),
        P("section", None, None, None),
    )
    out_specs = (
        P("section", None, "ctx", None),
        P("section", None, "ctx", None),
    ) + in_specs[16:]
    return jax.shard_map(shards, mesh=mesh, in_specs=in_specs, out_specs=out_specs, check_vma=False)
```

```python
import functools

import jax
import jax.numpy as jnp
from jax import lax
from jax.experimental import pallas as pl
from jax.experimental.pallas import tpu as pltpu
from jax.sharding import PartitionSpec as P

QHEADS = 8
KVHEADS = 2
HEAD = 128
MHEAD = 64
NSTATE = 256
KEY_BLOCK = 256
PAIR = 2 * MHEAD

epsilon = 1e-05
rope_base = 10000.0
masked_score = -1e30
BF = jnp.bfloat16
F32 = jnp.float32
HIGH = lax.Precision.HIGHEST


def mm(a, b):
    return jnp.dot(a.astype(BF), b.astype(BF), preferred_element_type=F32)


def mm_t(a, b):
    return lax.dot_general(
        a.astype(BF), b.astype(BF), (((1,), (1,)), ((), ())), preferred_element_type=F32
    )


def t_mm(a, b):
    return lax.dot_general(
        a.astype(BF), b.astype(BF), (((0,), (0,)), ((), ())), preferred_element_type=F32
    )


def rms_scale(vector):
    return lax.rsqrt(jnp.mean(vector * vector, axis=-1, keepdims=True) + epsilon)


def norm_back(vector, grad_normed, gain_vec):
    scale_now = rms_scale(vector)
    weighted = grad_normed * gain_vec
    return weighted * scale_now - vector * scale_now**3 * jnp.mean(
        weighted * vector, axis=-1, keepdims=True
    )


def vmem_call(kernel, out_shape, **kwargs):
    return pl.pallas_call(
        kernel,
        out_shape=out_shape,
        compiler_params=pltpu.CompilerParams(vmem_limit_bytes=56 * 1024 * 1024),
        **kwargs,
    )


def pair_lanes(rows, left, right):
    lane = lax.broadcasted_iota(jnp.int32, (rows, PAIR), 1)
    return jnp.where(lane < MHEAD, left, right)


def scan_forward_kernel(x_ref, b_ref, c_ref, dt_ref, cum_ref, cumt_ref, y_ref, state_ref, tail_scr):
    rows = x_ref.shape[0]
    heads = dt_ref.shape[1]
    gram = mm_t(c_ref[...], b_ref[...])
    row = lax.broadcasted_iota(jnp.int32, (rows, rows), 0)
    col = lax.broadcasted_iota(jnp.int32, (rows, rows), 1)
    gram = jnp.where(row >= col, gram, 0.0)
    cum = cum_ref[...]
    dt = dt_ref[...]
    cumt = cumt_ref[...]
    tail = jnp.exp(cum[rows - 1 : rows, :] - cum)
    for pair in range(heads // 2):
        one, two = 2 * pair, 2 * pair + 1
        lanes = slice(PAIR * pair, PAIR * (pair + 1))
        scaled = x_ref[:, lanes] * pair_lanes(rows, dt[:, one : one + 1], dt[:, two : two + 1])
        scaled_low = scaled.astype(BF)
        tail_scr[:, lanes] = (
            scaled * pair_lanes(rows, tail[:, one : one + 1], tail[:, two : two + 1])
        ).astype(BF)
        parts = []
        for head in (one, two):
            decay = jnp.exp(jnp.minimum(cum[:, head : head + 1] - cumt[head : head + 1, :], 0.0))
            parts.append(mm((gram * decay), scaled_low))
        y_ref[:, lanes] = pair_lanes(rows, parts[0], parts[1])
    state_ref[...] = t_mm(b_ref[...], tail_scr[...]).astype(state_ref.dtype)


def scan_forward(x, b_low, c_low, dt, cum, cumt):
    rows, width = x.shape
    return vmem_call(
        scan_forward_kernel,
        (
            jax.ShapeDtypeStruct((rows, width), F32),
            jax.ShapeDtypeStruct((b_low.shape[1], width), BF),
        ),
        scratch_shapes=[pltpu.VMEM((rows, width), BF)],
    )(x, b_low, c_low, dt, cum, cumt)


def scan_backward_kernel(
    x_ref, dy_ref, b_ref, c_ref, dt_ref, cum_ref, cumt_ref, z_ref, db_ref, dc_ref
):
    rows = x_ref.shape[0]
    heads = dt_ref.shape[1]
    gram_t = mm_t(b_ref[...], c_ref[...])
    row = lax.broadcasted_iota(jnp.int32, (rows, rows), 0)
    col = lax.broadcasted_iota(jnp.int32, (rows, rows), 1)
    causal = col >= row
    gram_t = jnp.where(causal, gram_t, 0.0)
    cum = cum_ref[...]
    dt = dt_ref[...]
    cumt = cumt_ref[...]
    grad_gram_t = jnp.zeros((rows, rows), F32)
    lane = lax.broadcasted_iota(jnp.int32, (rows, PAIR), 1)
    for pair in range(heads // 2):
        one, two = 2 * pair, 2 * pair + 1
        lanes = slice(PAIR * pair, PAIR * (pair + 1))
        scaled_low = (
            x_ref[:, lanes] * pair_lanes(rows, dt[:, one : one + 1], dt[:, two : two + 1])
        ).astype(BF)
        dy = dy_ref[:, lanes]
        parts = []
        for head in (one, two):
            decay = jnp.exp(jnp.minimum(cumt[head : head + 1, :] - cum[:, head : head + 1], 0.0))
            parts.append(mm(gram_t * decay, dy))
            mine = (lane < MHEAD) if head == one else (lane >= MHEAD)
            outer = mm_t(jnp.where(mine, scaled_low, jnp.zeros_like(scaled_low)), dy)
            grad_gram_t = grad_gram_t + decay * outer
        z_ref[:, lanes] = pair_lanes(rows, parts[0], parts[1])
    grad_low = jnp.where(causal, grad_gram_t, 0.0).astype(BF)
    db_ref[...] = mm(grad_low, c_ref[...])
    dc_ref[...] = t_mm(grad_low, b_ref[...])


def scan_backward(x, dy_low, b_low, c_low, dt, cum, cumt):
    rows, width = x.shape
    states = b_low.shape[1]
    return vmem_call(
        scan_backward_kernel,
        (
            jax.ShapeDtypeStruct((rows, width), F32),
            jax.ShapeDtypeStruct((rows, states), F32),
            jax.ShapeDtypeStruct((rows, states), F32),
        ),
    )(x, dy_low, b_low, c_low, dt, cum, cumt)


def block_mask(scores_shape, span, block, ctx_index, length):
    row = lax.broadcasted_iota(jnp.int32, scores_shape, 0)
    query_pos = ctx_index * span + lax.rem(row, span)
    key_pos = block * KEY_BLOCK + lax.broadcasted_iota(jnp.int32, scores_shape, 1)
    return (key_pos <= query_pos) & (key_pos < length)


def attend_forward_kernel(place_ref, q_ref, kv_ref, out_ref, lse_ref, top_scr, sum_scr):
    span = out_ref.shape[0]
    heads = q_ref.shape[0] // span
    length, ctx_index, blocks = place_ref[0], place_ref[1], place_ref[2]
    queries = q_ref[...]
    rows = queries.shape[0]
    top_scr[...] = jnp.full(top_scr.shape, masked_score, F32)
    sum_scr[...] = jnp.zeros(sum_scr.shape, F32)
    lse_ref[...] = jnp.zeros(lse_ref.shape, F32)

    def step(block, nothing):
        start = pl.multiple_of(block * KEY_BLOCK, KEY_BLOCK)
        keys = kv_ref[pl.ds(start, KEY_BLOCK), :HEAD]
        values = kv_ref[pl.ds(start, KEY_BLOCK), HEAD:]
        scores = HEAD ** (-0.5) * mm_t(queries, keys)
        allowed = block_mask(scores.shape, span, block, ctx_index, length)
        scores = jnp.where(allowed, scores, masked_score)
        top = top_scr[...]
        fresh_top = jnp.maximum(top, jnp.max(scores, axis=1, keepdims=True))
        shares = jnp.where(allowed, jnp.exp(scores - fresh_top), 0.0)
        fade = jnp.exp(top - fresh_top)
        lse_ref[...] = lse_ref[...] * fade + jnp.sum(shares, axis=1, keepdims=True)
        sum_scr[...] = sum_scr[...] * fade + mm(shares, values)
        top_scr[...] = fresh_top
        return nothing

    lax.fori_loop(0, blocks, step, 0)
    total = lse_ref[...]
    result = sum_scr[...] / total
    for head in range(heads):
        out_ref[:, head * HEAD : (head + 1) * HEAD] = result[head * span : (head + 1) * span, :]
    lse_ref[...] = top_scr[...] + jnp.log(total)


def attend_forward(place, query_rows, key_all, span):
    rows = query_rows.shape[0]
    return pl.pallas_call(
        attend_forward_kernel,
        out_shape=(
            jax.ShapeDtypeStruct((span, rows // span * HEAD), F32),
            jax.ShapeDtypeStruct((rows, 1), F32),
        ),
        in_specs=[
            pl.BlockSpec(memory_space=pltpu.SMEM),
            pl.BlockSpec(memory_space=pltpu.VMEM),
            pl.BlockSpec(memory_space=pltpu.VMEM),
        ],
        scratch_shapes=[pltpu.VMEM((rows, 1), F32), pltpu.VMEM((rows, HEAD), F32)],
        compiler_params=pltpu.CompilerParams(vmem_limit_bytes=56 * 1024 * 1024),
    )(place, query_rows, key_all)


def attend_backward_kernel(
    place_ref, q_ref, kv_ref, lse_ref, out_ref, grad_ref, dq_ref, dkv_ref, dq_scr
):
    span = out_ref.shape[0]
    heads = q_ref.shape[0] // span
    length, ctx_index, blocks = place_ref[0], place_ref[1], place_ref[2]
    queries = q_ref[...]
    grad_rows = jnp.concatenate(
        [grad_ref[:, head * HEAD : (head + 1) * HEAD] for head in range(heads)], axis=0
    )
    out_rows = jnp.concatenate(
        [out_ref[:, head * HEAD : (head + 1) * HEAD] for head in range(heads)], axis=0
    )
    delta = jnp.sum(grad_rows.astype(F32) * out_rows, axis=1, keepdims=True)
    lse = lse_ref[...]
    dq_scr[...] = jnp.zeros(dq_scr.shape, F32)
    dkv_ref[...] = jnp.zeros(dkv_ref.shape, dkv_ref.dtype)

    def step(block, nothing):
        start = pl.multiple_of(block * KEY_BLOCK, KEY_BLOCK)
        keys = kv_ref[pl.ds(start, KEY_BLOCK), :HEAD]
        values = kv_ref[pl.ds(start, KEY_BLOCK), HEAD:]
        scores = HEAD ** (-0.5) * mm_t(queries, keys)
        allowed = block_mask(scores.shape, span, block, ctx_index, length)
        shares = jnp.where(allowed, jnp.exp(jnp.where(allowed, scores, masked_score) - lse), 0.0)
        grad_share = mm_t(grad_rows, values)
        grad_score = (shares * (grad_share - delta)).astype(BF)
        dq_scr[...] += mm(grad_score, keys)
        dkv_ref[pl.ds(start, KEY_BLOCK), :HEAD] = (
            HEAD ** (-0.5) * t_mm(grad_score, queries)
        ).astype(dkv_ref.dtype)
        dkv_ref[pl.ds(start, KEY_BLOCK), HEAD:] = t_mm(shares, grad_rows).astype(dkv_ref.dtype)
        return nothing

    lax.fori_loop(0, blocks, step, 0)
    for head in range(heads):
        dq_ref[:, head * HEAD : (head + 1) * HEAD] = (
            HEAD ** (-0.5) * dq_scr[head * span : (head + 1) * span, :]
        )


def attend_backward(place, query_rows, key_all, lse, attended, grad_low):
    span = attended.shape[0]
    rows = query_rows.shape[0]
    vm = pl.BlockSpec(memory_space=pltpu.VMEM)
    return pl.pallas_call(
        attend_backward_kernel,
        out_shape=(
            jax.ShapeDtypeStruct(attended.shape, F32),
            jax.ShapeDtypeStruct(key_all.shape, BF),
        ),
        in_specs=[pl.BlockSpec(memory_space=pltpu.SMEM), vm, vm, vm, vm, vm],
        scratch_shapes=[pltpu.VMEM((rows, HEAD), F32)],
        compiler_params=pltpu.CompilerParams(vmem_limit_bytes=56 * 1024 * 1024),
    )(place, query_rows, key_all, lse, attended, grad_low)


def swap(value):
    return lax.ppermute(value, "section", [(0, 1), (1, 0)])


def after(value, *others):
    return lax.optimization_barrier((value,) + others)[0]


def shifted(value, steps):
    count = lax.axis_size("ctx")
    first, last = max(0, -steps), min(count, count - steps)
    return lax.ppermute(value, "ctx", [(source, source + steps) for source in range(first, last)])


def exchange_sum(value, axis):
    count = lax.axis_size(axis)
    bit = 1
    while bit < count:
        moved = lax.ppermute(value, axis, [(place, place ^ bit) for place in range(count)])
        value = (value.astype(F32) + moved.astype(F32)).astype(value.dtype)
        bit *= 2
    return value


def rope_tables(positions):
    half_width = HEAD // 2
    frequencies = rope_base ** (-jnp.arange(half_width, dtype=F32) / half_width)
    angles = positions.astype(F32)[:, None] * frequencies[None, :]
    return jnp.cos(angles), jnp.sin(angles)


def rotate(values, tables, direction):
    half_width = HEAD // 2
    cosine, sine = tables[0], direction * tables[1]
    heads = []
    for head in range(values.shape[1] // HEAD):
        first = values[:, head * HEAD : head * HEAD + half_width]
        second = values[:, head * HEAD + half_width : (head + 1) * HEAD]
        heads.append(first * cosine - second * sine)
        heads.append(second * cosine + first * sine)
    return jnp.concatenate(heads, axis=1)


def gathered_rows(own, ctx_index):
    span = own.shape[0]
    count = lax.axis_size("ctx")
    rows = jnp.zeros((count * span, own.shape[1]), own.dtype)
    for steps in range(count - 1, 0, -1):
        place = jnp.maximum(ctx_index - steps, 0) * span
        rows = lax.dynamic_update_slice_in_dim(rows, shifted(own, steps), place, 0)
    return lax.dynamic_update_slice_in_dim(rows, own, ctx_index * span, 0)


def returned_rows(rows, span, ctx_index):
    count = lax.axis_size("ctx")
    total = lax.dynamic_slice_in_dim(rows, ctx_index * span, span, 0).astype(F32)
    for steps in range(1, count):
        place = jnp.maximum(ctx_index - steps, 0) * span
        part = lax.dynamic_slice_in_dim(rows, place, span, 0)
        total = total + shifted(part, -steps).astype(F32)
    return total


def carried_states(payload, states, reverse):
    count = lax.axis_size("ctx")
    summed = jnp.zeros((states, payload.shape[1]), F32)
    between = jnp.ones((1, payload.shape[1]), F32)
    for steps in range(1, count):
        moved = shifted(payload, -steps if reverse else steps).astype(F32)
        summed = summed + between * moved[:states]
        between = between * (moved[states : states + 1] + moved[states + 1 : states + 2])
    return summed


def state_payload(state, total):
    decay = jnp.repeat(jnp.exp(total), MHEAD)[None, :]
    high = decay.astype(BF)
    low = (decay - high.astype(F32)).astype(BF)
    pad = jnp.zeros((14, decay.shape[1]), BF)
    return jnp.concatenate([state.astype(BF), high, low, pad], axis=0)


def wide(per_head):
    return jnp.repeat(per_head, MHEAD, axis=1)


def head_sum(values):
    return jnp.sum(values.reshape(values.shape[0], -1, MHEAD), axis=2)


def low_sum(value):
    return lax.psum(value.astype(BF), "wt").astype(F32)


class Weights:
    pass


def layer_forward(entry_low, w, place, last):
    saved = {"entry": entry_low}
    entry = entry_low.astype(F32)
    normed = (entry * rms_scale(entry) * w.mixer_gain).astype(BF)
    small_in = mm_t(normed, w.mixin_down).astype(BF)
    shared = mm(normed, w.shared) + mm(small_in, w.shared_up)
    query_proj = mm(normed, w.query) + mm(small_in, w.query_up)
    mamba_proj = mm(normed, w.mamba) + mm(small_in, w.mamba_up)
    span = entry.shape[0]
    local_heads = query_proj.shape[1] // HEAD
    key_head = place.wt * local_heads // (QHEADS // KVHEADS)
    key_part = lax.dynamic_slice_in_dim(shared, key_head * HEAD, HEAD, 1)
    value_part = lax.dynamic_slice_in_dim(shared, (KVHEADS + key_head) * HEAD, HEAD, 1)
    key_value = jnp.concatenate([rotate(key_part, place.tables, 1.0), value_part], axis=1)
    key_all = gathered_rows(key_value.astype(BF), place.ctx)
    rotated = rotate(query_proj, place.tables, 1.0).astype(BF)
    query_rows = jnp.concatenate(
        [rotated[:, head * HEAD : (head + 1) * HEAD] for head in range(local_heads)], axis=0
    )

    half = mamba_proj.shape[1] // 2
    heads = half // MHEAD
    gate_raw, inputs = mamba_proj[:, :half], mamba_proj[:, half:]
    offset = 2 * KVHEADS * HEAD
    input_map = shared[:, offset : offset + NSTATE].astype(BF)
    output_map = shared[:, offset + NSTATE : offset + 2 * NSTATE].astype(BF)
    step_raw = lax.dynamic_slice_in_dim(
        shared, offset + 2 * NSTATE + place.wt * heads, heads, 1
    )
    step_in = step_raw + w.step_bias
    step_sizes = jax.nn.softplus(step_in) * place.live[:, None]
    cum = jnp.dot(place.lower, -w.decay_rate * step_sizes, precision=HIGH)
    local_y, local_state = scan_forward(
        inputs, input_map, output_map, step_sizes, cum, cum.T
    )
    state_sum = carried_states(state_payload(local_state, cum[-1]), NSTATE, False)
    attended, lse = attend_forward(place.scalars, query_rows, key_all, span)
    state_in = state_sum.astype(BF)
    scanned = local_y + wide(jnp.exp(cum)) * mm(output_map, state_in)
    joined = scanned + jnp.repeat(w.skip_gain, MHEAD)[None, :] * inputs
    gated_low = (joined * jax.nn.silu(gate_raw)).astype(BF)
    attended_low = attended.astype(BF)
    small_mid = mm_t(attended_low, w.attnout_down) + mm_t(gated_low, w.mambaout_down)
    part = (
        mm(attended_low, w.attnout) + mm(gated_low, w.mambaout) + mm(small_mid, w.mixout_up)
    )
    hidden = entry + place.live[:, None] * low_sum(part)

    feed_normed = (hidden * rms_scale(hidden) * w.feed_gain).astype(BF)
    small_feed = mm_t(feed_normed, w.feedin_down).astype(BF)
    gateup = mm(feed_normed, w.gateup) + mm(small_feed, w.feedin_up)
    width = gateup.shape[1] // 2
    gate_value, up_value = gateup[:, :width], gateup[:, width:]
    inner = (jax.nn.silu(gate_value) * up_value).astype(BF)
    small_out = mm_t(inner, w.feedout_down)
    feed_part = (mm(inner, w.down) + mm(small_out, w.feedout_up)).astype(BF)
    saved.update(
        normed=normed,
        small_in=small_in,
        query_rows=query_rows,
        key_all=key_all,
        key_head=key_head,
        gate_raw=gate_raw,
        inputs=inputs,
        input_map=input_map,
        output_map=output_map,
        step_in=step_in,
        step_sizes=step_sizes,
        cum=cum,
        state_in=state_in,
        scanned=scanned,
        attended=attended,
        lse=lse,
        gated_low=gated_low,
        attended_low=attended_low,
        small_mid=exchange_sum(small_mid, "wt"),
        hidden=hidden,
        feed_normed=feed_normed,
        small_feed=small_feed,
        gate_value=gate_value,
        up_value=up_value,
        inner=inner,
        small_out=exchange_sum(small_out, "wt"),
    )
    if last:
        return feed_part, saved
    return hidden + low_sum(feed_part), saved


def feed_backward(grad_out, w, place, s):
    grads = {}
    grad_feed = grad_out.astype(BF)
    grad_small_out = mm_t(grad_feed, w.feedout_up)
    grads["feedout_up"] = t_mm(s["small_out"], grad_feed)
    grads["feedout_down"] = t_mm(grad_small_out, s["inner"])
    grad_inner = mm_t(grad_feed, w.down) + mm(grad_small_out, w.feedout_down)
    gate_value, up_value = s["gate_value"], s["up_value"]
    sigmoid_gate = jax.nn.sigmoid(gate_value)
    grad_gate = grad_inner * up_value * sigmoid_gate * (1.0 + gate_value * (1.0 - sigmoid_gate))
    grad_up = grad_inner * gate_value * sigmoid_gate
    grad_gateup = jnp.concatenate([grad_gate, grad_up], axis=1).astype(BF)
    grad_small_feed = mm_t(grad_gateup, w.feedin_up)
    grads["feedin_up"] = t_mm(s["small_feed"], grad_gateup)
    feed_norm_part = mm_t(grad_gateup, w.gateup) + mm(grad_small_feed, w.feedin_down)
    summed = low_sum(feed_norm_part)
    grads["feedin_down"] = t_mm(exchange_sum(grad_small_feed, "wt"), s["feed_normed"])
    return grad_out + norm_back(s["hidden"], summed, w.feed_gain), grads


def mixer_backward(grad_hidden, w, place, s):
    grads = {}
    span = grad_hidden.shape[0]
    grad_mixed = (grad_hidden * place.live[:, None]).astype(BF)
    grad_small_mid = mm_t(grad_mixed, w.mixout_up)
    grads["mixout_up"] = t_mm(s["small_mid"], grad_mixed)
    grads["attnout_down"] = t_mm(grad_small_mid, s["attended_low"])
    grads["mambaout_down"] = t_mm(grad_small_mid, s["gated_low"])
    grad_gated = mm_t(grad_mixed, w.mambaout) + mm(grad_small_mid, w.mambaout_down)
    gate_raw, inputs, scanned = s["gate_raw"], s["inputs"], s["scanned"]
    skip = jnp.repeat(w.skip_gain, MHEAD)[None, :]
    sigmoid_raw = jax.nn.sigmoid(gate_raw)
    silu_raw = gate_raw * sigmoid_raw
    dy_low = (grad_gated * silu_raw).astype(BF)
    dy = dy_low.astype(F32)
    grad_gates = (
        grad_gated * (scanned + skip * inputs) * sigmoid_raw * (1.0 + gate_raw * (1.0 - sigmoid_raw))
    )
    cum, step_sizes = s["cum"], s["step_sizes"]
    grown = wide(jnp.exp(cum))
    grown_dy = (grown * dy).astype(BF)
    local_grad = t_mm(s["output_map"], grown_dy)
    grad_state = carried_states(state_payload(local_grad, cum[-1]), NSTATE, True).astype(BF)

    grad_attended = (
        mm_t(grad_mixed, w.attnout) + mm(grad_small_mid, w.attnout_down)
    ).astype(BF)
    grad_query, grad_keyval = attend_backward(
        place.scalars, s["query_rows"], s["key_all"], s["lse"], s["attended"], grad_attended
    )
    own = returned_rows(grad_keyval, span, place.ctx)

    z_local, db_local, dc_local = scan_backward(
        inputs, dy_low, s["input_map"], s["output_map"], step_sizes, cum, cum.T
    )
    dt_wide = wide(step_sizes)
    tail = wide(jnp.exp(cum[-1:] - cum))
    scaled_low = (inputs * dt_wide).astype(BF)
    scaled = scaled_low.astype(F32)
    z_tail = tail * mm(s["input_map"], grad_state)
    z_all = z_local + z_tail
    grad_inputs = dt_wide * z_all + skip * dy
    grad_map_in = db_local + mm_t((tail * scaled), grad_state)
    grad_map_out = dc_local + mm_t(grown_dy, s["state_in"])
    kept = jnp.sum(
        grad_state.astype(F32) * s["state_in"].astype(F32), axis=0
    )[None, :] * jnp.repeat(jnp.exp(cum[-1]), MHEAD)[None, :]
    edge = head_sum(jnp.sum(scaled * z_tail, axis=0, keepdims=True) + kept)
    through = head_sum(dy * scanned - scaled * z_all)
    cum_grad = edge + jnp.dot(place.lower.T, through, precision=HIGH)
    grad_steps = head_sum(inputs * z_all) - w.decay_rate * cum_grad
    grad_step = grad_steps * jax.nn.sigmoid(s["step_in"]) * place.live[:, None]

    heads = cum.shape[1]
    grad_query_low = rotate(grad_query, place.tables, -1.0).astype(BF)
    grad_keys = rotate(own[:, :HEAD], place.tables, -1.0)
    key_head = s["key_head"]
    offset = 2 * KVHEADS * HEAD
    keyval = jnp.zeros((span, offset), F32)
    keyval = lax.dynamic_update_slice_in_dim(keyval, grad_keys, key_head * HEAD, 1)
    keyval = lax.dynamic_update_slice_in_dim(
        keyval, own[:, HEAD:], (KVHEADS + key_head) * HEAD, 1
    )
    all_heads = w.shared.shape[1] - offset - 2 * NSTATE
    step_part = lax.dynamic_update_slice_in_dim(
        jnp.zeros((span, all_heads), F32), grad_step, place.wt * heads, 1
    )
    grad_shared = jnp.concatenate(
        [keyval, grad_map_in, grad_map_out, step_part], axis=1
    ).astype(BF)
    grad_mamba = jnp.concatenate([grad_gates, grad_inputs], axis=1).astype(BF)
    grad_small_in = (
        mm_t(grad_query_low, w.query_up)
        + mm_t(grad_mamba, w.mamba_up)
        + mm_t(grad_shared, w.shared_up)
    )
    norm_part = (
        mm_t(grad_query_low, w.query)
        + mm_t(grad_mamba, w.mamba)
        + mm_t(grad_shared, w.shared)
        + mm(grad_small_in, w.mixin_down)
    )
    summed = low_sum(norm_part)
    grads["query_up"] = t_mm(s["small_in"], grad_query_low)
    grads["mamba_up"] = t_mm(s["small_in"], grad_mamba)
    grads["shared_up"] = t_mm(s["small_in"], grad_shared)
    grads["mixin_down"] = t_mm(grad_small_in, s["normed"])
    grad_entry = grad_hidden + norm_back(s["entry"].astype(F32), summed, w.mixer_gain)
    return grad_entry, grads


FIXED = (
    "mixer_gain",
    "feed_gain",
    "decay_rate",
    "step_bias",
    "skip_gain",
    "query",
    "mamba",
    "shared",
    "attnout",
    "mambaout",
    "gateup",
    "down",
)
ADAPTERS = (
    "mixin_down",
    "query_up",
    "mamba_up",
    "shared_up",
    "attnout_down",
    "mambaout_down",
    "mixout_up",
    "feedin_down",
    "feedin_up",
    "feedout_down",
    "feedout_up",
)
PARTIAL = ("mixin_down", "shared_up")
GROUPS = (
    ("shared", "query", "mamba"),
    ("attnout", "mambaout"),
    ("gateup", "down"),
)


def shards(layer_input, cotangent, seq_lengths, adapter_ids, *params):
    section = lax.axis_index("section")
    ctx_index = lax.axis_index("ctx")
    micro_count, span = layer_input.shape[0], layer_input.shape[1]
    assert micro_count == 2 and lax.axis_size("section") == 2

    place = Weights()
    place.wt = lax.axis_index("wt")
    place.ctx = ctx_index
    length = seq_lengths[section]
    positions = ctx_index * span + jnp.arange(span, dtype=jnp.int32)
    place.live = (positions < length).astype(F32)
    place.tables = rope_tables(positions)
    row = lax.broadcasted_iota(jnp.int32, (span, span), 0)
    col = lax.broadcasted_iota(jnp.int32, (span, span), 1)
    place.lower = (row >= col).astype(F32)
    blocks = jnp.minimum(
        ((ctx_index + 1) * span + KEY_BLOCK - 1) // KEY_BLOCK, (length + KEY_BLOCK - 1) // KEY_BLOCK
    )
    place.scalars = jnp.stack([length, ctx_index, blocks]).astype(jnp.int32)

    own, other, shapes = {}, {}, {}
    for name, item in zip(FIXED, params):
        own[name] = item[0]
    mine, theirs = adapter_ids[section], adapter_ids[1 - section]
    for name, item in zip(ADAPTERS, params[len(FIXED) :]):
        shapes[name] = item.shape[1:]
        own[name] = lax.dynamic_index_in_dim(item[0], mine, 0, keepdims=False)
        other[name] = swap(lax.dynamic_index_in_dim(item[0], theirs, 0, keepdims=False))
    done = []
    for group in GROUPS:
        for name in group:
            other[name] = swap(after(own[name], *done))
        done = [other[name] for name in group]
    for name in own:
        if name not in other:
            other[name] = swap(own[name])

    layers = []
    for index in range(2):
        w = Weights()
        for name in own:
            value = jnp.where(section == index, own[name], other[name])
            if value.ndim == 3:
                value = value.reshape(value.shape[0], -1)
            if name in FIXED[5:]:
                value = lax.optimization_barrier(value)
            setattr(w, name, value)
        layers.append(w)

    entry = lax.dynamic_index_in_dim(layer_input, section, 0, keepdims=False)
    result, saved_first = layer_forward(entry, layers[0], place, False)
    first_out = result.astype(BF)
    last_part, saved_second = layer_forward(first_out, layers[1], place, True)

    def by_layer(values):
        keep = jnp.where(section == 0, values[0], values[1])
        return keep, swap(jnp.where(section == 0, values[1], values[0]))

    def reduced(found):
        names = list(found)
        packed = jnp.concatenate(
            [found[name].astype(BF).reshape(found[name].shape[0], -1) for name in names], axis=1
        )
        return names, [found[name].shape[1] for name in names], packed

    def summed_grads(found):
        partial = {name: found[name] for name in found if name in PARTIAL}
        whole = {name: found[name] for name in found if name not in PARTIAL}
        names, widths, packed = reduced(whole)
        if partial:
            more, extra, part = reduced(partial)
            names, widths = names + more, widths + extra
            packed = jnp.concatenate([packed, exchange_sum(part, "wt")], axis=1)
        return names, widths, exchange_sum(packed, "ctx")

    grad = lax.dynamic_index_in_dim(cotangent, section, 0, keepdims=False).astype(F32)
    kept_sets = []
    grad_hidden, feed_grads = feed_backward(grad, layers[1], place, saved_second)
    last_part = after(last_part, grad_hidden)
    second_out = (saved_second["hidden"] + low_sum(last_part)).astype(BF)
    grad, mixer_grads = mixer_backward(grad_hidden, layers[1], place, saved_second)
    second_grad = grad.astype(BF)
    second_sets = [summed_grads(feed_grads), summed_grads(mixer_grads)]

    grad_hidden, feed_grads = feed_backward(second_grad.astype(F32), layers[0], place, saved_first)
    first_sets = [summed_grads(feed_grads)]
    grad, mixer_grads = mixer_backward(grad_hidden, layers[0], place, saved_first)
    first_grad = grad.astype(BF)
    first_sets.append(summed_grads(mixer_grads))

    def stacked(values):
        keep, moved = by_layer(values)
        return jnp.stack(
            [jnp.where(section == 0, keep, moved), jnp.where(section == 0, moved, keep)]
        )[None]

    found = {}
    adapters = jnp.arange(params[len(FIXED)].shape[1], dtype=jnp.int32)[:, None, None]
    for first_set, second_set in zip(first_sets, second_sets):
        keep, moved = by_layer((first_set[2], second_set[2]))
        start = 0
        for name, width in zip(first_set[0], first_set[1]):
            lanes = slice(start, start + width)
            start += width
            total = jnp.where(adapters == mine, keep[None, :, lanes].astype(F32), 0.0)
            total = total + jnp.where(adapters == theirs, moved[None, :, lanes].astype(F32), 0.0)
            found[name] = total.reshape(shapes[name])[None]
    return (
        stacked((first_out, second_out)),
        stacked((first_grad, second_grad)),
    ) + tuple(found[name] for name in ADAPTERS)


def solution(mesh):
    in_specs = (
        P(None, "ctx", None),
        P(None, "ctx", None),
        P(),
        P(),
        P("section", None),
        P("section", None),
        P("section", "wt"),
        P("section", "wt"),
        P("section", "wt"),
        P("section", None, "wt"),
        P("section", None, None, "wt"),
        P("section", None, None),
        P("section", "wt", None),
        P("section", "wt", None),
        P("section", None, None, "wt"),
        P("section", "wt", None),
        P("section", None, None, None),
        P("section", None, None, "wt"),
        P("section", None, None, None, "wt"),
        P("section", None, None, None),
        P("section", None, None, "wt"),
        P("section", None, None, "wt"),
        P("section", None, None, None),
        P("section", None, None, None),
        P("section", None, None, None, "wt"),
        P("section", None, None, "wt"),
        P("section", None, None, None),
    )
    out_specs = (
        P("section", None, "ctx", None),
        P("section", None, "ctx", None),
    ) + in_specs[16:]
    return jax.shard_map(shards, mesh=mesh, in_specs=in_specs, out_specs=out_specs, check_vma=False)
```

```python
import functools

import jax
import jax.numpy as jnp
from jax import lax
from jax.experimental import pallas as pl
from jax.experimental.pallas import tpu as pltpu
from jax.sharding import PartitionSpec as P

QHEADS = 8
KVHEADS = 2
HEAD = 128
MHEAD = 64
NSTATE = 256
KEY_BLOCK = 256
PAIR = 2 * MHEAD

epsilon = 1e-05
rope_base = 10000.0
masked_score = -1e30
BF = jnp.bfloat16
F32 = jnp.float32
HIGH = lax.Precision.HIGHEST


def mm(a, b):
    return jnp.dot(a.astype(BF), b.astype(BF), preferred_element_type=F32)


def mm_t(a, b):
    return lax.dot_general(
        a.astype(BF), b.astype(BF), (((1,), (1,)), ((), ())), preferred_element_type=F32
    )


def t_mm(a, b):
    return lax.dot_general(
        a.astype(BF), b.astype(BF), (((0,), (0,)), ((), ())), preferred_element_type=F32
    )


def rms_scale(vector):
    return lax.rsqrt(jnp.mean(vector * vector, axis=-1, keepdims=True) + epsilon)


def norm_back(vector, grad_normed, gain_vec):
    scale_now = rms_scale(vector)
    weighted = grad_normed * gain_vec
    return weighted * scale_now - vector * scale_now**3 * jnp.mean(
        weighted * vector, axis=-1, keepdims=True
    )


def vmem_call(kernel, out_shape, **kwargs):
    return pl.pallas_call(
        kernel,
        out_shape=out_shape,
        compiler_params=pltpu.CompilerParams(vmem_limit_bytes=56 * 1024 * 1024),
        **kwargs,
    )


def pair_lanes(rows, left, right):
    lane = lax.broadcasted_iota(jnp.int32, (rows, PAIR), 1)
    return jnp.where(lane < MHEAD, left, right)


def scan_forward_kernel(x_ref, b_ref, c_ref, dt_ref, cum_ref, cumt_ref, y_ref, state_ref, tail_scr):
    rows = x_ref.shape[0]
    heads = dt_ref.shape[1]
    gram = mm_t(c_ref[...], b_ref[...])
    row = lax.broadcasted_iota(jnp.int32, (rows, rows), 0)
    col = lax.broadcasted_iota(jnp.int32, (rows, rows), 1)
    gram = jnp.where(row >= col, gram, 0.0)
    cum = cum_ref[...]
    dt = dt_ref[...]
    cumt = cumt_ref[...]
    tail = jnp.exp(cum[rows - 1 : rows, :] - cum)
    for pair in range(heads // 2):
        one, two = 2 * pair, 2 * pair + 1
        lanes = slice(PAIR * pair, PAIR * (pair + 1))
        scaled = x_ref[:, lanes] * pair_lanes(rows, dt[:, one : one + 1], dt[:, two : two + 1])
        scaled_low = scaled.astype(BF)
        tail_scr[:, lanes] = (
            scaled * pair_lanes(rows, tail[:, one : one + 1], tail[:, two : two + 1])
        ).astype(BF)
        parts = []
        for head in (one, two):
            decay = jnp.exp(jnp.minimum(cum[:, head : head + 1] - cumt[head : head + 1, :], 0.0))
            parts.append(mm((gram * decay), scaled_low))
        y_ref[:, lanes] = pair_lanes(rows, parts[0], parts[1])
    state_ref[...] = t_mm(b_ref[...], tail_scr[...]).astype(state_ref.dtype)


def scan_forward(x, b_low, c_low, dt, cum, cumt):
    rows, width = x.shape
    return vmem_call(
        scan_forward_kernel,
        (
            jax.ShapeDtypeStruct((rows, width), F32),
            jax.ShapeDtypeStruct((b_low.shape[1], width), BF),
        ),
        scratch_shapes=[pltpu.VMEM((rows, width), BF)],
    )(x, b_low, c_low, dt, cum, cumt)


def scan_backward_kernel(
    x_ref, dy_ref, b_ref, c_ref, dt_ref, cum_ref, cumt_ref, z_ref, db_ref, dc_ref
):
    rows = x_ref.shape[0]
    heads = dt_ref.shape[1]
    gram_t = mm_t(b_ref[...], c_ref[...])
    row = lax.broadcasted_iota(jnp.int32, (rows, rows), 0)
    col = lax.broadcasted_iota(jnp.int32, (rows, rows), 1)
    causal = col >= row
    gram_t = jnp.where(causal, gram_t, 0.0)
    cum = cum_ref[...]
    dt = dt_ref[...]
    cumt = cumt_ref[...]
    grad_gram_t = jnp.zeros((rows, rows), F32)
    lane = lax.broadcasted_iota(jnp.int32, (rows, PAIR), 1)
    for pair in range(heads // 2):
        one, two = 2 * pair, 2 * pair + 1
        lanes = slice(PAIR * pair, PAIR * (pair + 1))
        scaled_low = (
            x_ref[:, lanes] * pair_lanes(rows, dt[:, one : one + 1], dt[:, two : two + 1])
        ).astype(BF)
        dy = dy_ref[:, lanes]
        parts = []
        for head in (one, two):
            decay = jnp.exp(jnp.minimum(cumt[head : head + 1, :] - cum[:, head : head + 1], 0.0))
            parts.append(mm(gram_t * decay, dy))
            mine = (lane < MHEAD) if head == one else (lane >= MHEAD)
            outer = mm_t(jnp.where(mine, scaled_low, jnp.zeros_like(scaled_low)), dy)
            grad_gram_t = grad_gram_t + decay * outer
        z_ref[:, lanes] = pair_lanes(rows, parts[0], parts[1])
    grad_low = jnp.where(causal, grad_gram_t, 0.0).astype(BF)
    db_ref[...] = mm(grad_low, c_ref[...])
    dc_ref[...] = t_mm(grad_low, b_ref[...])


def scan_backward(x, dy_low, b_low, c_low, dt, cum, cumt):
    rows, width = x.shape
    states = b_low.shape[1]
    return vmem_call(
        scan_backward_kernel,
        (
            jax.ShapeDtypeStruct((rows, width), F32),
            jax.ShapeDtypeStruct((rows, states), F32),
            jax.ShapeDtypeStruct((rows, states), F32),
        ),
    )(x, dy_low, b_low, c_low, dt, cum, cumt)


def scan_close_kernel(
    x_ref,
    dy_ref,
    z_ref,
    y_ref,
    b_ref,
    grad_state_ref,
    state_ref,
    db_ref,
    dc_ref,
    dt_ref,
    cum_ref,
    step_ref,
    live_ref,
    rate_ref,
    skip_ref,
    dx_ref,
    db_out_ref,
    dc_out_ref,
    dstep_ref,
    through_scr,
    step_scr,
    edge_scr,
    tail_scr,
    grown_scr,
):
    rows, width = x_ref.shape
    heads = dt_ref.shape[1]
    cum = cum_ref[...]
    dt = dt_ref[...]
    last = cum[rows - 1 : rows, :]
    tail = jnp.exp(last - cum)
    grown = jnp.exp(cum)
    whole = jnp.exp(last)
    for pair in range(heads // 2):
        one, two = 2 * pair, 2 * pair + 1
        lanes = slice(PAIR * pair, PAIR * (pair + 1))
        dt_pair = pair_lanes(rows, dt[:, one : one + 1], dt[:, two : two + 1])
        tail_pair = pair_lanes(rows, tail[:, one : one + 1], tail[:, two : two + 1])
        grown_pair = pair_lanes(rows, grown[:, one : one + 1], grown[:, two : two + 1])
        whole_pair = pair_lanes(1, whole[:, one : one + 1], whole[:, two : two + 1])
        x = x_ref[:, lanes]
        dy = dy_ref[:, lanes].astype(F32)
        grad_state = grad_state_ref[:, lanes]
        z_tail = tail_pair * mm(b_ref[...], grad_state)
        z_all = z_ref[:, lanes] + z_tail
        dx_ref[:, lanes] = (dt_pair * z_all + skip_ref[:, lanes] * dy).astype(dx_ref.dtype)
        scaled = (x * dt_pair).astype(BF).astype(F32)
        tail_scr[:, lanes] = (tail_pair * scaled).astype(BF)
        grown_scr[:, lanes] = (grown_pair * dy).astype(BF)
        through_scr[:, lanes] = dy * y_ref[:, lanes] - scaled * z_all
        step_scr[:, lanes] = x * z_all
        kept = jnp.sum(
            grad_state.astype(F32) * state_ref[:, lanes].astype(F32), axis=0, keepdims=True
        )
        edge = jnp.sum(scaled * z_tail, axis=0, keepdims=True) + kept * whole_pair
        edge_scr[:, lanes] = jnp.broadcast_to(edge, (edge_scr.shape[0], PAIR))
    db_out_ref[...] = (db_ref[...] + mm_t(tail_scr[...], grad_state_ref[...])).astype(BF)
    dc_out_ref[...] = (dc_ref[...] + mm_t(grown_scr[...], state_ref[...])).astype(BF)
    lane = lax.broadcasted_iota(jnp.int32, (width, heads), 0)
    head = lax.broadcasted_iota(jnp.int32, (width, heads), 1)
    member = ((lane >= head * MHEAD) & (lane < (head + 1) * MHEAD)).astype(F32)
    row = lax.broadcasted_iota(jnp.int32, (rows, rows), 0)
    col = lax.broadcasted_iota(jnp.int32, (rows, rows), 1)
    later = (col >= row).astype(F32)

    def exact(a, b):
        return jnp.dot(a, b, precision=HIGH, preferred_element_type=F32)

    cum_grad = exact(later, exact(through_scr[...], member))
    cum_grad = cum_grad + exact(edge_scr[...], member)[0:1, :]
    grad_steps = exact(step_scr[...], member) - rate_ref[...] * cum_grad
    dstep_ref[...] = grad_steps * live_ref[...] / (1.0 + jnp.exp(-step_ref[...]))


def scan_close(x, dy_low, z, y, b_low, grad_state, state, db, dc, dt, cum, step, live, rate, skip):
    rows, width = x.shape
    states, heads = b_low.shape[1], dt.shape[1]
    return vmem_call(
        scan_close_kernel,
        (
            jax.ShapeDtypeStruct((rows, width), BF),
            jax.ShapeDtypeStruct((rows, states), BF),
            jax.ShapeDtypeStruct((rows, states), BF),
            jax.ShapeDtypeStruct((rows, heads), F32),
        ),
        scratch_shapes=[
            pltpu.VMEM((rows, width), F32),
            pltpu.VMEM((rows, width), F32),
            pltpu.VMEM((8, width), F32),
            pltpu.VMEM((rows, width), BF),
            pltpu.VMEM((rows, width), BF),
        ],
    )(x, dy_low, z, y, b_low, grad_state, state, db, dc, dt, cum, step, live, rate, skip)


def block_mask(scores_shape, span, block, ctx_index, length):
    row = lax.broadcasted_iota(jnp.int32, scores_shape, 0)
    query_pos = ctx_index * span + lax.rem(row, span)
    key_pos = block * KEY_BLOCK + lax.broadcasted_iota(jnp.int32, scores_shape, 1)
    return (key_pos <= query_pos) & (key_pos < length)


def attend_forward_kernel(place_ref, q_ref, kv_ref, out_ref, lse_ref, top_scr, sum_scr):
    span = out_ref.shape[0]
    heads = q_ref.shape[0] // span
    length, ctx_index, blocks = place_ref[0], place_ref[1], place_ref[2]
    queries = q_ref[...]
    rows = queries.shape[0]
    top_scr[...] = jnp.full(top_scr.shape, masked_score, F32)
    sum_scr[...] = jnp.zeros(sum_scr.shape, F32)
    lse_ref[...] = jnp.zeros(lse_ref.shape, F32)

    def step(block, nothing):
        start = pl.multiple_of(block * KEY_BLOCK, KEY_BLOCK)
        keys = kv_ref[pl.ds(start, KEY_BLOCK), :HEAD]
        values = kv_ref[pl.ds(start, KEY_BLOCK), HEAD:]
        scores = HEAD ** (-0.5) * mm_t(queries, keys)
        allowed = block_mask(scores.shape, span, block, ctx_index, length)
        scores = jnp.where(allowed, scores, masked_score)
        top = top_scr[...]
        fresh_top = jnp.maximum(top, jnp.max(scores, axis=1, keepdims=True))
        shares = jnp.where(allowed, jnp.exp(scores - fresh_top), 0.0)
        fade = jnp.exp(top - fresh_top)
        lse_ref[...] = lse_ref[...] * fade + jnp.sum(shares, axis=1, keepdims=True)
        sum_scr[...] = sum_scr[...] * fade + mm(shares, values)
        top_scr[...] = fresh_top
        return nothing

    lax.fori_loop(0, blocks, step, 0)
    total = lse_ref[...]
    result = sum_scr[...] / total
    for head in range(heads):
        out_ref[:, head * HEAD : (head + 1) * HEAD] = result[head * span : (head + 1) * span, :]
    lse_ref[...] = top_scr[...] + jnp.log(total)


def attend_forward(place, query_rows, key_all, span):
    rows = query_rows.shape[0]
    return pl.pallas_call(
        attend_forward_kernel,
        out_shape=(
            jax.ShapeDtypeStruct((span, rows // span * HEAD), F32),
            jax.ShapeDtypeStruct((rows, 1), F32),
        ),
        in_specs=[
            pl.BlockSpec(memory_space=pltpu.SMEM),
            pl.BlockSpec(memory_space=pltpu.VMEM),
            pl.BlockSpec(memory_space=pltpu.VMEM),
        ],
        scratch_shapes=[pltpu.VMEM((rows, 1), F32), pltpu.VMEM((rows, HEAD), F32)],
        compiler_params=pltpu.CompilerParams(vmem_limit_bytes=56 * 1024 * 1024),
    )(place, query_rows, key_all)


def attend_backward_kernel(
    place_ref, q_ref, kv_ref, lse_ref, out_ref, grad_ref, dq_ref, dkv_ref, dq_scr
):
    span = out_ref.shape[0]
    heads = q_ref.shape[0] // span
    length, ctx_index, blocks = place_ref[0], place_ref[1], place_ref[2]
    queries = q_ref[...]
    grad_rows = jnp.concatenate(
        [grad_ref[:, head * HEAD : (head + 1) * HEAD] for head in range(heads)], axis=0
    )
    out_rows = jnp.concatenate(
        [out_ref[:, head * HEAD : (head + 1) * HEAD] for head in range(heads)], axis=0
    )
    delta = jnp.sum(grad_rows.astype(F32) * out_rows, axis=1, keepdims=True)
    lse = lse_ref[...]
    dq_scr[...] = jnp.zeros(dq_scr.shape, F32)
    dkv_ref[...] = jnp.zeros(dkv_ref.shape, dkv_ref.dtype)

    def step(block, nothing):
        start = pl.multiple_of(block * KEY_BLOCK, KEY_BLOCK)
        keys = kv_ref[pl.ds(start, KEY_BLOCK), :HEAD]
        values = kv_ref[pl.ds(start, KEY_BLOCK), HEAD:]
        scores = HEAD ** (-0.5) * mm_t(queries, keys)
        allowed = block_mask(scores.shape, span, block, ctx_index, length)
        shares = jnp.where(allowed, jnp.exp(jnp.where(allowed, scores, masked_score) - lse), 0.0)
        grad_share = mm_t(grad_rows, values)
        grad_score = (shares * (grad_share - delta)).astype(BF)
        dq_scr[...] += mm(grad_score, keys)
        dkv_ref[pl.ds(start, KEY_BLOCK), :HEAD] = (
            HEAD ** (-0.5) * t_mm(grad_score, queries)
        ).astype(dkv_ref.dtype)
        dkv_ref[pl.ds(start, KEY_BLOCK), HEAD:] = t_mm(shares, grad_rows).astype(dkv_ref.dtype)
        return nothing

    lax.fori_loop(0, blocks, step, 0)
    for head in range(heads):
        dq_ref[:, head * HEAD : (head + 1) * HEAD] = (
            HEAD ** (-0.5) * dq_scr[head * span : (head + 1) * span, :]
        )


def attend_backward(place, query_rows, key_all, lse, attended, grad_low):
    span = attended.shape[0]
    rows = query_rows.shape[0]
    vm = pl.BlockSpec(memory_space=pltpu.VMEM)
    return pl.pallas_call(
        attend_backward_kernel,
        out_shape=(
            jax.ShapeDtypeStruct(attended.shape, F32),
            jax.ShapeDtypeStruct(key_all.shape, BF),
        ),
        in_specs=[pl.BlockSpec(memory_space=pltpu.SMEM), vm, vm, vm, vm, vm],
        scratch_shapes=[pltpu.VMEM((rows, HEAD), F32)],
        compiler_params=pltpu.CompilerParams(vmem_limit_bytes=56 * 1024 * 1024),
    )(place, query_rows, key_all, lse, attended, grad_low)


def swap(value):
    return lax.ppermute(value, "section", [(0, 1), (1, 0)])


def after(value, *others):
    return lax.optimization_barrier((value,) + others)[0]


def shifted(value, steps):
    count = lax.axis_size("ctx")
    first, last = max(0, -steps), min(count, count - steps)
    return lax.ppermute(value, "ctx", [(source, source + steps) for source in range(first, last)])


def exchange_sum(value, axis):
    count = lax.axis_size(axis)
    bit = 1
    while bit < count:
        moved = lax.ppermute(value, axis, [(place, place ^ bit) for place in range(count)])
        value = (value.astype(F32) + moved.astype(F32)).astype(value.dtype)
        bit *= 2
    return value


def rope_tables(positions):
    half_width = HEAD // 2
    frequencies = rope_base ** (-jnp.arange(half_width, dtype=F32) / half_width)
    angles = positions.astype(F32)[:, None] * frequencies[None, :]
    return jnp.cos(angles), jnp.sin(angles)


def rotate(values, tables, direction):
    half_width = HEAD // 2
    cosine, sine = tables[0], direction * tables[1]
    heads = []
    for head in range(values.shape[1] // HEAD):
        first = values[:, head * HEAD : head * HEAD + half_width]
        second = values[:, head * HEAD + half_width : (head + 1) * HEAD]
        heads.append(first * cosine - second * sine)
        heads.append(second * cosine + first * sine)
    return jnp.concatenate(heads, axis=1)


def gathered_rows(own, ctx_index):
    span = own.shape[0]
    count = lax.axis_size("ctx")
    rows = jnp.zeros((count * span, own.shape[1]), own.dtype)
    for steps in range(count - 1, 0, -1):
        place = jnp.maximum(ctx_index - steps, 0) * span
        rows = lax.dynamic_update_slice_in_dim(rows, shifted(own, steps), place, 0)
    return lax.dynamic_update_slice_in_dim(rows, own, ctx_index * span, 0)


def returned_rows(rows, span, ctx_index):
    count = lax.axis_size("ctx")
    total = lax.dynamic_slice_in_dim(rows, ctx_index * span, span, 0).astype(F32)
    for steps in range(1, count):
        place = jnp.maximum(ctx_index - steps, 0) * span
        part = lax.dynamic_slice_in_dim(rows, place, span, 0)
        total = total + shifted(part, -steps).astype(F32)
    return total


def carried_states(payload, states, reverse):
    count = lax.axis_size("ctx")
    summed = jnp.zeros((states, payload.shape[1]), F32)
    between = jnp.ones((1, payload.shape[1]), F32)
    for steps in range(1, count):
        moved = shifted(payload, -steps if reverse else steps).astype(F32)
        summed = summed + between * moved[:states]
        between = between * (moved[states : states + 1] + moved[states + 1 : states + 2])
    return summed


def state_payload(state, total):
    decay = jnp.repeat(jnp.exp(total), MHEAD)[None, :]
    high = decay.astype(BF)
    low = (decay - high.astype(F32)).astype(BF)
    pad = jnp.zeros((14, decay.shape[1]), BF)
    return jnp.concatenate([state.astype(BF), high, low, pad], axis=0)


def wide(per_head):
    return jnp.repeat(per_head, MHEAD, axis=1)


def head_sum(values):
    return jnp.sum(values.reshape(values.shape[0], -1, MHEAD), axis=2)


def low_sum(value):
    return lax.psum(value.astype(BF), "wt").astype(F32)


class Weights:
    def keep(self, **values):
        self.__dict__.update(values)


def mixer_forward(entry_low, w, place):
    saved = Weights()
    saved.entry = entry_low
    entry = entry_low.astype(F32)
    normed = (entry * rms_scale(entry) * w.mixer_gain).astype(BF)
    small_in = mm_t(normed, w.mixin_down).astype(BF)
    shared = mm(normed, w.shared) + mm(small_in, w.shared_up)
    query_proj = mm(normed, w.query) + mm(small_in, w.query_up)
    mamba_proj = mm(normed, w.mamba) + mm(small_in, w.mamba_up)
    span = entry.shape[0]
    local_heads = query_proj.shape[1] // HEAD
    key_head = place.wt * local_heads // (QHEADS // KVHEADS)
    key_part = lax.dynamic_slice_in_dim(shared, key_head * HEAD, HEAD, 1)
    value_part = lax.dynamic_slice_in_dim(shared, (KVHEADS + key_head) * HEAD, HEAD, 1)
    key_value = jnp.concatenate([rotate(key_part, place.tables, 1.0), value_part], axis=1)
    key_all = gathered_rows(key_value.astype(BF), place.ctx)
    rotated = rotate(query_proj, place.tables, 1.0).astype(BF)
    query_rows = jnp.concatenate(
        [rotated[:, head * HEAD : (head + 1) * HEAD] for head in range(local_heads)], axis=0
    )

    half = mamba_proj.shape[1] // 2
    heads = half // MHEAD
    gate_raw, inputs = mamba_proj[:, :half], mamba_proj[:, half:]
    offset = 2 * KVHEADS * HEAD
    input_map = shared[:, offset : offset + NSTATE].astype(BF)
    output_map = shared[:, offset + NSTATE : offset + 2 * NSTATE].astype(BF)
    step_raw = lax.dynamic_slice_in_dim(
        shared, offset + 2 * NSTATE + place.wt * heads, heads, 1
    )
    step_in = step_raw + w.step_bias
    step_sizes = jax.nn.softplus(step_in) * place.live[:, None]
    cum = jnp.dot(place.lower, -w.decay_rate * step_sizes, precision=HIGH)
    local_y, local_state = scan_forward(
        inputs, input_map, output_map, step_sizes, cum, cum.T
    )
    state_sum = carried_states(state_payload(local_state, cum[-1]), NSTATE, False)
    attended, lse = attend_forward(place.scalars, query_rows, key_all, span)
    state_in = state_sum.astype(BF)
    scanned = local_y + wide(jnp.exp(cum)) * mm(output_map, state_in)
    joined = scanned + jnp.repeat(w.skip_gain, MHEAD)[None, :] * inputs
    gated_low = (joined * jax.nn.silu(gate_raw)).astype(BF)
    attended_low = attended.astype(BF)
    small_mid = mm_t(attended_low, w.attnout_down) + mm_t(gated_low, w.mambaout_down)
    part = (
        mm(attended_low, w.attnout) + mm(gated_low, w.mambaout) + mm(small_mid, w.mixout_up)
    )
    saved.keep(
        normed=normed,
        small_in=small_in,
        query_rows=query_rows,
        key_all=key_all,
        key_head=key_head,
        gate_raw=gate_raw,
        inputs=inputs,
        input_map=input_map,
        output_map=output_map,
        step_in=step_in,
        step_sizes=step_sizes,
        cum=cum,
        state_in=state_in,
        scanned=scanned,
        attended=attended,
        lse=lse,
        gated_low=gated_low,
        attended_low=attended_low,
        small_mid=small_mid,
    )
    return part.astype(BF), saved


def feed_forward(entry_low, part, w, place, saved):
    mixed = after(lax.psum(part, "wt"), w.gateup, w.down)
    hidden = entry_low.astype(F32) + place.live[:, None] * mixed.astype(F32)
    feed_normed = (hidden * rms_scale(hidden) * w.feed_gain).astype(BF)
    small_feed = mm_t(feed_normed, w.feedin_down).astype(BF)
    gateup = mm(feed_normed, w.gateup) + mm(small_feed, w.feedin_up)
    width = gateup.shape[1] // 2
    gate_value, up_value = gateup[:, :width], gateup[:, width:]
    inner = (jax.nn.silu(gate_value) * up_value).astype(BF)
    small_out = mm_t(inner, w.feedout_down)
    feed_part = (mm(inner, w.down) + mm(small_out, w.feedout_up)).astype(BF)
    saved.keep(
        hidden=hidden,
        feed_normed=feed_normed,
        small_feed=small_feed,
        gate_value=gate_value,
        up_value=up_value,
        inner=inner,
        small_out=small_out,
    )
    return feed_part


def feed_backward(grad_out, w, place, s, finish):
    grads = Weights()
    grad_feed = grad_out.astype(BF)
    grad_small_out = mm_t(grad_feed, w.feedout_up)
    grad_inner = mm_t(grad_feed, w.down) + mm(grad_small_out, w.feedout_down)
    gate_value, up_value = s.gate_value, s.up_value
    sigmoid_gate = jax.nn.sigmoid(gate_value)
    grad_gate = grad_inner * up_value * sigmoid_gate * (1.0 + gate_value * (1.0 - sigmoid_gate))
    grad_up = grad_inner * gate_value * sigmoid_gate
    grad_gateup = jnp.concatenate([grad_gate, grad_up], axis=1).astype(BF)
    grad_small_feed = mm_t(grad_gateup, w.feedin_up)
    feed_norm_part = mm_t(grad_gateup, w.gateup) + mm(grad_small_feed, w.feedin_down)
    summed = lax.psum(feed_norm_part.astype(BF), "wt")
    small_all = exchange_sum(
        jnp.concatenate(
            [part.astype(BF) for part in (s.small_mid, s.small_out, grad_small_feed)], axis=1
        ),
        "wt",
    )
    rank = grad_small_feed.shape[1]
    s.small_mid = small_all[:, :rank]
    grads.feedout_up = t_mm(small_all[:, rank : 2 * rank], grad_feed)
    grads.feedout_down = t_mm(grad_small_out, s.inner)
    grads.feedin_up = t_mm(s.small_feed, grad_gateup)
    grads.feedin_down = t_mm(small_all[:, 2 * rank :], s.feed_normed)
    found = finish(grads)
    summed = after(summed, found[2]).astype(F32)
    return grad_out + norm_back(s.hidden, summed, w.feed_gain), found


def mixer_backward(grad_hidden, w, place, s, finish, before=()):
    grads = Weights()
    span = grad_hidden.shape[0]
    grad_mixed = (grad_hidden * place.live[:, None]).astype(BF)
    grad_small_mid = mm_t(grad_mixed, w.mixout_up)
    grad_gated = mm_t(grad_mixed, w.mambaout) + mm(grad_small_mid, w.mambaout_down)
    gate_raw, inputs, scanned = s.gate_raw, s.inputs, s.scanned
    skip = jnp.repeat(w.skip_gain, MHEAD)[None, :]
    sigmoid_raw = jax.nn.sigmoid(gate_raw)
    silu_raw = gate_raw * sigmoid_raw
    dy_low = (grad_gated * silu_raw).astype(BF)
    dy = dy_low.astype(F32)
    grad_gates = (
        grad_gated * (scanned + skip * inputs) * sigmoid_raw * (1.0 + gate_raw * (1.0 - sigmoid_raw))
    )
    cum, step_sizes = s.cum, s.step_sizes
    grown = wide(jnp.exp(cum))
    grown_dy = (grown * dy).astype(BF)
    local_grad = t_mm(s.output_map, grown_dy)
    payload = state_payload(local_grad, cum[-1])
    grad_state = carried_states(payload, NSTATE, True).astype(BF)
    dy_now, grad_mid, small_now = lax.optimization_barrier(
        (dy_low, grad_mixed, grad_small_mid, payload)
    )[:3]

    grad_attended = (
        mm_t(grad_mid, w.attnout) + mm(small_now, w.attnout_down)
    ).astype(BF)
    grad_query, grad_keyval = attend_backward(
        place.scalars, s.query_rows, s.key_all, s.lse, s.attended, grad_attended
    )
    own = returned_rows(after(grad_keyval, grad_state), span, place.ctx)

    z_local, db_local, dc_local = scan_backward(
        inputs, dy_now, s.input_map, s.output_map, step_sizes, cum, cum.T
    )
    grad_inputs, grad_map_in, grad_map_out, grad_step = scan_close(
        inputs,
        dy_low,
        z_local,
        scanned,
        s.input_map,
        grad_state,
        s.state_in,
        db_local,
        dc_local,
        step_sizes,
        cum,
        s.step_in,
        place.live[:, None],
        w.decay_rate[None, :],
        skip,
    )

    heads = cum.shape[1]
    grad_query_low = rotate(grad_query, place.tables, -1.0).astype(BF)
    grad_keys = rotate(own[:, :HEAD], place.tables, -1.0)
    key_head = s.key_head
    offset = 2 * KVHEADS * HEAD
    keyval = jnp.zeros((span, offset), F32)
    keyval = lax.dynamic_update_slice_in_dim(keyval, grad_keys, key_head * HEAD, 1)
    keyval = lax.dynamic_update_slice_in_dim(
        keyval, own[:, HEAD:], (KVHEADS + key_head) * HEAD, 1
    )
    all_heads = w.shared.shape[1] - offset - 2 * NSTATE
    step_part = lax.dynamic_update_slice_in_dim(
        jnp.zeros((span, all_heads), F32), grad_step, place.wt * heads, 1
    )
    grad_shared = jnp.concatenate(
        [keyval.astype(BF), grad_map_in, grad_map_out, step_part.astype(BF)], axis=1
    )
    grad_mamba = jnp.concatenate([grad_gates.astype(BF), grad_inputs], axis=1)
    grad_small_in = (
        mm_t(grad_query_low, w.query_up)
        + mm_t(grad_mamba, w.mamba_up)
        + mm_t(grad_shared, w.shared_up)
    )
    norm_part = (
        mm_t(grad_query_low, w.query)
        + mm_t(grad_mamba, w.mamba)
        + mm_t(grad_shared, w.shared)
        + mm(grad_small_in, w.mixin_down)
    )
    norm_part = after(norm_part.astype(BF), *before)
    summed = lax.psum(norm_part, "wt")
    grads.mixout_up = t_mm(s.small_mid, grad_mixed)
    grads.attnout_down = t_mm(grad_small_mid, s.attended_low)
    grads.mambaout_down = t_mm(grad_small_mid, s.gated_low)
    grads.query_up = t_mm(s.small_in, grad_query_low)
    grads.mamba_up = t_mm(s.small_in, grad_mamba)
    grads.shared_up = t_mm(s.small_in, grad_shared)
    grads.mixin_down = t_mm(grad_small_in, s.normed)
    found = finish(grads, *((summed,) if before else ()))
    grad_entry = grad_hidden + norm_back(
        s.entry.astype(F32), summed.astype(F32), w.mixer_gain
    )
    return grad_entry, found


FIXED = (
    "mixer_gain",
    "feed_gain",
    "decay_rate",
    "step_bias",
    "skip_gain",
    "query",
    "mamba",
    "shared",
    "attnout",
    "mambaout",
    "gateup",
    "down",
)
ADAPTERS = (
    "mixin_down",
    "query_up",
    "mamba_up",
    "shared_up",
    "attnout_down",
    "mambaout_down",
    "mixout_up",
    "feedin_down",
    "feedin_up",
    "feedout_down",
    "feedout_up",
)
PARTIAL = ("mixin_down", "shared_up")
PACKS = (
    ("mixin_down", "mamba_up", "query_up", "shared_up"),
    ("mixout_up", "mambaout_down", "attnout_down"),
    ("feedin_down", "feedin_up", "feedout_up", "feedout_down"),
)
GROUPS = (
    ("shared", "query", "mamba"),
    ("attnout", "mambaout"),
    ("gateup", "down"),
)


def shards(layer_input, cotangent, seq_lengths, adapter_ids, *params):
    section = lax.axis_index("section")
    ctx_index = lax.axis_index("ctx")
    micro_count, span = layer_input.shape[0], layer_input.shape[1]
    assert micro_count == 2 and lax.axis_size("section") == 2

    place = Weights()
    place.wt = lax.axis_index("wt")
    place.ctx = ctx_index
    length = seq_lengths[section]
    positions = ctx_index * span + jnp.arange(span, dtype=jnp.int32)
    place.live = (positions < length).astype(F32)
    place.tables = rope_tables(positions)
    row = lax.broadcasted_iota(jnp.int32, (span, span), 0)
    col = lax.broadcasted_iota(jnp.int32, (span, span), 1)
    place.lower = (row >= col).astype(F32)
    blocks = jnp.minimum(
        ((ctx_index + 1) * span + KEY_BLOCK - 1) // KEY_BLOCK, (length + KEY_BLOCK - 1) // KEY_BLOCK
    )
    place.scalars = jnp.stack([length, ctx_index, blocks]).astype(jnp.int32)

    own, items, shapes = {}, {}, {}
    for name, item in zip(FIXED, params):
        own[name] = item[0]
    mine, theirs = adapter_ids[section], adapter_ids[1 - section]
    for name, item in zip(ADAPTERS, params[len(FIXED) :]):
        shapes[name] = item.shape[1:]
        items[name] = item[0]
    layers = (Weights(), Weights())

    def packed_items(names, which):
        return jnp.concatenate(
            [
                lax.dynamic_index_in_dim(items[name], which, 0, keepdims=False).reshape(
                    items[name].shape[1], -1
                )
                for name in names
            ],
            axis=1,
        )

    def place_pack(names, widths, kept, moved):
        for index, w in enumerate(layers):
            value = jnp.where(section == index, kept, moved)
            start = 0
            for name, width in zip(names, widths):
                setattr(w, name, value[..., start : start + width])
                start += width

    def exchange_pack(number, *gates):
        names = PACKS[number]
        widths = [items[name][0, 0].size for name in names]
        moved = swap(after(packed_items(names, theirs), *gates))
        place_pack(names, widths, packed_items(names, mine), moved)

    vectors = FIXED[:5]
    joined = jnp.concatenate([own[name].astype(F32) for name in vectors])
    place_pack(vectors, [own[name].size for name in vectors], joined, swap(joined))
    exchange_pack(0)
    done = []
    for group in GROUPS:
        moved = {name: swap(after(own[name], *done)) for name in group}
        done = done or list(moved.values())
        for name in group:
            for index, w in enumerate(layers):
                value = jnp.where(section == index, own[name], moved[name])
                if value.ndim == 3:
                    value = value.reshape(value.shape[0], -1)
                setattr(w, name, lax.optimization_barrier(value))
    exchange_pack(1, *done)

    first, second = layers
    entry = lax.dynamic_index_in_dim(layer_input, section, 0, keepdims=False)
    part, saved_first = mixer_forward(entry, first, place)
    exchange_pack(2, part)
    feed_part = feed_forward(entry, part, first, place, saved_first)
    following = [getattr(second, name) for name in GROUPS[0] + GROUPS[1]]
    fed = after(lax.psum(feed_part, "wt"), *following)
    first_out = (saved_first.hidden + fed.astype(F32)).astype(BF)
    part, saved_second = mixer_forward(first_out, second, place)
    last_part = feed_forward(first_out, part, second, place, saved_second)

    def forth(value):
        return lax.ppermute(value, "section", [(0, 1)])

    def back(value):
        return lax.ppermute(value, "section", [(1, 0)])

    def reduced(found):
        names = list(found)
        packed = jnp.concatenate(
            [found[name].astype(BF).reshape(found[name].shape[0], -1) for name in names], axis=1
        )
        return names, [found[name].shape[1] for name in names], packed

    def summed_grads(grads, *gates):
        found = vars(grads)
        partial = {name: found[name] for name in found if name in PARTIAL}
        whole = {name: found[name] for name in found if name not in PARTIAL}
        names, widths, packed = reduced(whole)
        packed = after(packed, *gates)
        if partial:
            more, extra, part = reduced(partial)
            part = after(part, *gates)
            names, widths = names + more, widths + extra
            packed = jnp.concatenate([packed, exchange_sum(part, "wt")], axis=1)
        return names, widths, exchange_sum(packed, "ctx")

    grad = lax.dynamic_index_in_dim(cotangent, section, 0, keepdims=False).astype(F32)
    grad_hidden, found = feed_backward(grad, second, place, saved_second, summed_grads)
    second_sets = [found]
    last_part = after(last_part, grad_hidden)
    second_out = (saved_second.hidden + low_sum(last_part)).astype(BF)
    grad, found = mixer_backward(
        grad_hidden, second, place, saved_second, summed_grads, (second_out,)
    )
    second_grad = grad.astype(BF)
    second_sets.append(found)
    grad_hidden, found = feed_backward(
        second_grad.astype(F32), first, place, saved_first, summed_grads
    )
    first_sets = [found]
    grad, found = mixer_backward(grad_hidden, first, place, saved_first, summed_grads)
    first_grad = grad.astype(BF)
    first_sets.append(found)

    def stacked(early, late):
        return jnp.where(
            section == 0, jnp.stack([early, back(early)]), jnp.stack([forth(late), late])
        )[None]

    found = {}
    adapters = jnp.arange(params[len(FIXED)].shape[1], dtype=jnp.int32)[:, None, None]
    for first_set, second_set in zip(first_sets, second_sets):
        keep = jnp.where(section == 0, first_set[2], second_set[2])
        moved = jnp.where(section == 0, back(first_set[2]), forth(second_set[2]))
        start = 0
        for name, width in zip(first_set[0], first_set[1]):
            lanes = slice(start, start + width)
            start += width
            total = jnp.where(adapters == mine, keep[None, :, lanes].astype(F32), 0.0)
            total = total + jnp.where(adapters == theirs, moved[None, :, lanes].astype(F32), 0.0)
            found[name] = total.reshape(shapes[name])[None]
    return (
        stacked(first_out, second_out),
        stacked(first_grad, second_grad),
    ) + tuple(found[name] for name in ADAPTERS)


def solution(mesh):
    in_specs = (
        P(None, "ctx", None),
        P(None, "ctx", None),
        P(),
        P(),
        P("section", None),
        P("section", None),
        P("section", "wt"),
        P("section", "wt"),
        P("section", "wt"),
        P("section", None, "wt"),
        P("section", None, None, "wt"),
        P("section", None, None),
        P("section", "wt", None),
        P("section", "wt", None),
        P("section", None, None, "wt"),
        P("section", "wt", None),
        P("section", None, None, None),
        P("section", None, None, "wt"),
        P("section", None, None, None, "wt"),
        P("section", None, None, None),
        P("section", None, None, "wt"),
        P("section", None, None, "wt"),
        P("section", None, None, None),
        P("section", None, None, None),
        P("section", None, None, None, "wt"),
        P("section", None, None, "wt"),
        P("section", None, None, None),
    )
    out_specs = (
        P("section", None, "ctx", None),
        P("section", None, "ctx", None),
    ) + in_specs[16:]
    return jax.shard_map(shards, mesh=mesh, in_specs=in_specs, out_specs=out_specs, check_vma=False)
```

```python
import functools

import jax
import jax.numpy as jnp
from jax import lax
from jax.experimental import pallas as pl
from jax.experimental.pallas import tpu as pltpu
from jax.sharding import PartitionSpec as P

QHEADS = 8
KVHEADS = 2
HEAD = 128
MHEAD = 64
NSTATE = 256
KEY_BLOCK = 256
PAIR = 2 * MHEAD

epsilon = 1e-05
rope_base = 10000.0
masked_score = -1e30
BF = jnp.bfloat16
F32 = jnp.float32
HIGH = lax.Precision.HIGHEST


def mm(a, b):
    return jnp.dot(a.astype(BF), b.astype(BF), preferred_element_type=F32)


def mm_t(a, b):
    return lax.dot_general(
        a.astype(BF), b.astype(BF), (((1,), (1,)), ((), ())), preferred_element_type=F32
    )


def t_mm(a, b):
    return lax.dot_general(
        a.astype(BF), b.astype(BF), (((0,), (0,)), ((), ())), preferred_element_type=F32
    )


def rms_scale(vector):
    return lax.rsqrt(jnp.mean(vector * vector, axis=-1, keepdims=True) + epsilon)


def norm_back(vector, grad_normed, gain_vec):
    scale_now = rms_scale(vector)
    weighted = grad_normed * gain_vec
    return weighted * scale_now - vector * scale_now**3 * jnp.mean(
        weighted * vector, axis=-1, keepdims=True
    )


def vmem_call(kernel, out_shape, **kwargs):
    return pl.pallas_call(
        kernel,
        out_shape=out_shape,
        compiler_params=pltpu.CompilerParams(vmem_limit_bytes=56 * 1024 * 1024),
        **kwargs,
    )


def pair_lanes(rows, left, right):
    lane = lax.broadcasted_iota(jnp.int32, (rows, PAIR), 1)
    return jnp.where(lane < MHEAD, left, right)


def moved_sum(moved_refs, states, lanes):
    total, between = 0.0, 1.0
    for moved_ref in moved_refs:
        total = total + between * moved_ref[:states, lanes].astype(F32)
        ends = moved_ref[states : states + 16, lanes].astype(F32)
        between = between * (ends[0:1, :] + ends[1:2, :])
    return total


def scan_finish_kernel(y_ref, proj_ref, c_ref, cum_ref, skip_ref, *refs):
    moved_refs, (out_ref, gated_ref, state_ref) = refs[:-3], refs[-3:]
    rows, width = y_ref.shape
    states = c_ref.shape[1]
    heads = cum_ref.shape[1]
    grown = jnp.exp(cum_ref[...])
    for pair in range(heads // 2):
        one, two = 2 * pair, 2 * pair + 1
        lanes = slice(PAIR * pair, PAIR * (pair + 1))
        state = moved_sum(moved_refs, states, lanes).astype(BF)
        state_ref[:, lanes] = state
        grown_pair = pair_lanes(rows, grown[:, one : one + 1], grown[:, two : two + 1])
        scanned = y_ref[:, lanes] + grown_pair * mm(c_ref[...], state)
        out_ref[:, lanes] = scanned
        gate = proj_ref[:, lanes]
        joined = scanned + skip_ref[:, lanes] * proj_ref[:, width + PAIR * pair : width + PAIR * (pair + 1)]
        gated_ref[:, lanes] = (joined * (gate / (1.0 + jnp.exp(-gate)))).astype(BF)


def scan_finish(y, proj, c_low, cum, skip, moved):
    rows, width = y.shape
    return vmem_call(
        scan_finish_kernel,
        (
            jax.ShapeDtypeStruct((rows, width), F32),
            jax.ShapeDtypeStruct((rows, width), BF),
            jax.ShapeDtypeStruct((c_low.shape[1], width), BF),
        ),
    )(y, proj, c_low, cum, skip, *moved)


def scan_forward_kernel(x_ref, b_ref, c_ref, dt_ref, cum_ref, cumt_ref, y_ref, state_ref, tail_scr):
    rows = x_ref.shape[0]
    heads = dt_ref.shape[1]
    width = heads * MHEAD
    gram = mm_t(c_ref[...], b_ref[...])
    row = lax.broadcasted_iota(jnp.int32, (rows, rows), 0)
    col = lax.broadcasted_iota(jnp.int32, (rows, rows), 1)
    gram = jnp.where(row >= col, gram, 0.0)
    cum = cum_ref[...]
    dt = dt_ref[...]
    cumt = cumt_ref[...]
    tail = jnp.exp(cum[rows - 1 : rows, :] - cum)
    for pair in range(heads // 2):
        one, two = 2 * pair, 2 * pair + 1
        lanes = slice(PAIR * pair, PAIR * (pair + 1))
        scaled = x_ref[:, width + PAIR * pair : width + PAIR * (pair + 1)] * pair_lanes(rows, dt[:, one : one + 1], dt[:, two : two + 1])
        scaled_low = scaled.astype(BF)
        tail_scr[:, lanes] = (
            scaled * pair_lanes(rows, tail[:, one : one + 1], tail[:, two : two + 1])
        ).astype(BF)
        parts = []
        for head in (one, two):
            decay = jnp.exp(jnp.minimum(cum[:, head : head + 1] - cumt[head : head + 1, :], 0.0))
            parts.append(mm((gram * decay), scaled_low))
        y_ref[:, lanes] = pair_lanes(rows, parts[0], parts[1])
    state_ref[...] = t_mm(b_ref[...], tail_scr[...]).astype(state_ref.dtype)


def scan_forward(x, b_low, c_low, dt, cum, cumt):
    rows, width = x.shape[0], dt.shape[1] * MHEAD
    return vmem_call(
        scan_forward_kernel,
        (
            jax.ShapeDtypeStruct((rows, width), F32),
            jax.ShapeDtypeStruct((b_low.shape[1], width), BF),
        ),
        scratch_shapes=[pltpu.VMEM((rows, width), BF)],
    )(x, b_low, c_low, dt, cum, cumt)


def scan_backward_kernel(
    x_ref, dy_ref, b_ref, c_ref, dt_ref, cum_ref, cumt_ref, z_ref, db_ref, dc_ref
):
    rows = x_ref.shape[0]
    heads = dt_ref.shape[1]
    gram_t = mm_t(b_ref[...], c_ref[...])
    row = lax.broadcasted_iota(jnp.int32, (rows, rows), 0)
    col = lax.broadcasted_iota(jnp.int32, (rows, rows), 1)
    causal = col >= row
    gram_t = jnp.where(causal, gram_t, 0.0)
    cum = cum_ref[...]
    dt = dt_ref[...]
    cumt = cumt_ref[...]
    grad_gram_t = jnp.zeros((rows, rows), F32)
    lane = lax.broadcasted_iota(jnp.int32, (rows, PAIR), 1)
    for pair in range(heads // 2):
        one, two = 2 * pair, 2 * pair + 1
        lanes = slice(PAIR * pair, PAIR * (pair + 1))
        scaled_low = (
            x_ref[:, lanes] * pair_lanes(rows, dt[:, one : one + 1], dt[:, two : two + 1])
        ).astype(BF)
        dy = dy_ref[:, lanes]
        parts = []
        for head in (one, two):
            decay = jnp.exp(jnp.minimum(cumt[head : head + 1, :] - cum[:, head : head + 1], 0.0))
            parts.append(mm(gram_t * decay, dy))
            mine = (lane < MHEAD) if head == one else (lane >= MHEAD)
            outer = mm_t(jnp.where(mine, scaled_low, jnp.zeros_like(scaled_low)), dy)
            grad_gram_t = grad_gram_t + decay * outer
        z_ref[:, lanes] = pair_lanes(rows, parts[0], parts[1])
    grad_low = jnp.where(causal, grad_gram_t, 0.0).astype(BF)
    db_ref[...] = mm(grad_low, c_ref[...])
    dc_ref[...] = t_mm(grad_low, b_ref[...])


def scan_backward(x, dy_low, b_low, c_low, dt, cum, cumt):
    rows, width = x.shape
    states = b_low.shape[1]
    return vmem_call(
        scan_backward_kernel,
        (
            jax.ShapeDtypeStruct((rows, width), F32),
            jax.ShapeDtypeStruct((rows, states), F32),
            jax.ShapeDtypeStruct((rows, states), F32),
        ),
    )(x, dy_low, b_low, c_low, dt, cum, cumt)


def scan_close_kernel(
    x_ref,
    dy_ref,
    z_ref,
    y_ref,
    b_ref,
    state_ref,
    db_ref,
    dc_ref,
    dt_ref,
    cum_ref,
    step_ref,
    live_ref,
    rate_ref,
    skip_ref,
    *refs,
):
    moved_refs = refs[:-10]
    dx_ref, db_out_ref, dc_out_ref, dstep_ref = refs[-10:-6]
    through_scr, step_scr, edge_scr, tail_scr, grown_scr, grad_state_scr = refs[-6:]
    rows, width = x_ref.shape
    heads = dt_ref.shape[1]
    cum = cum_ref[...]
    dt = dt_ref[...]
    last = cum[rows - 1 : rows, :]
    tail = jnp.exp(last - cum)
    grown = jnp.exp(cum)
    whole = jnp.exp(last)
    for pair in range(heads // 2):
        one, two = 2 * pair, 2 * pair + 1
        lanes = slice(PAIR * pair, PAIR * (pair + 1))
        dt_pair = pair_lanes(rows, dt[:, one : one + 1], dt[:, two : two + 1])
        tail_pair = pair_lanes(rows, tail[:, one : one + 1], tail[:, two : two + 1])
        grown_pair = pair_lanes(rows, grown[:, one : one + 1], grown[:, two : two + 1])
        whole_pair = pair_lanes(1, whole[:, one : one + 1], whole[:, two : two + 1])
        x = x_ref[:, lanes]
        dy = dy_ref[:, lanes].astype(F32)
        grad_state = moved_sum(moved_refs, b_ref.shape[1], lanes).astype(BF)
        grad_state_scr[:, lanes] = grad_state
        z_tail = tail_pair * mm(b_ref[...], grad_state)
        z_all = z_ref[:, lanes] + z_tail
        dx_ref[:, lanes] = (dt_pair * z_all + skip_ref[:, lanes] * dy).astype(dx_ref.dtype)
        scaled = (x * dt_pair).astype(BF).astype(F32)
        tail_scr[:, lanes] = (tail_pair * scaled).astype(BF)
        grown_scr[:, lanes] = (grown_pair * dy).astype(BF)
        through_scr[:, lanes] = dy * y_ref[:, lanes] - scaled * z_all
        step_scr[:, lanes] = x * z_all
        kept = jnp.sum(
            grad_state.astype(F32) * state_ref[:, lanes].astype(F32), axis=0, keepdims=True
        )
        edge = jnp.sum(scaled * z_tail, axis=0, keepdims=True) + kept * whole_pair
        edge_scr[:, lanes] = jnp.broadcast_to(edge, (edge_scr.shape[0], PAIR))
    db_out_ref[...] = (db_ref[...] + mm_t(tail_scr[...], grad_state_scr[...])).astype(BF)
    dc_out_ref[...] = (dc_ref[...] + mm_t(grown_scr[...], state_ref[...])).astype(BF)
    lane = lax.broadcasted_iota(jnp.int32, (width, heads), 0)
    head = lax.broadcasted_iota(jnp.int32, (width, heads), 1)
    member = ((lane >= head * MHEAD) & (lane < (head + 1) * MHEAD)).astype(F32)
    row = lax.broadcasted_iota(jnp.int32, (rows, rows), 0)
    col = lax.broadcasted_iota(jnp.int32, (rows, rows), 1)
    later = (col >= row).astype(F32)

    def exact(a, b):
        return jnp.dot(a, b, precision=HIGH, preferred_element_type=F32)

    cum_grad = exact(later, exact(through_scr[...], member))
    cum_grad = cum_grad + exact(edge_scr[...], member)[0:1, :]
    grad_steps = exact(step_scr[...], member) - rate_ref[...] * cum_grad
    dstep_ref[...] = grad_steps * live_ref[...] / (1.0 + jnp.exp(-step_ref[...]))


def scan_close(x, dy_low, z, y, b_low, state, db, dc, dt, cum, step, live, rate, skip, moved):
    rows, width = x.shape
    states, heads = b_low.shape[1], dt.shape[1]
    return vmem_call(
        scan_close_kernel,
        (
            jax.ShapeDtypeStruct((rows, width), BF),
            jax.ShapeDtypeStruct((rows, states), BF),
            jax.ShapeDtypeStruct((rows, states), BF),
            jax.ShapeDtypeStruct((rows, heads), F32),
        ),
        scratch_shapes=[
            pltpu.VMEM((rows, width), F32),
            pltpu.VMEM((rows, width), F32),
            pltpu.VMEM((8, width), F32),
            pltpu.VMEM((rows, width), BF),
            pltpu.VMEM((rows, width), BF),
            pltpu.VMEM((states, width), BF),
        ],
    )(x, dy_low, z, y, b_low, state, db, dc, dt, cum, step, live, rate, skip, *moved)


def block_mask(scores_shape, span, block, ctx_index, length):
    row = lax.broadcasted_iota(jnp.int32, scores_shape, 0)
    query_pos = ctx_index * span + lax.rem(row, span)
    key_pos = block * KEY_BLOCK + lax.broadcasted_iota(jnp.int32, scores_shape, 1)
    return (key_pos <= query_pos) & (key_pos < length)


def attend_forward_kernel(place_ref, q_ref, kv_ref, out_ref, lse_ref, top_scr, sum_scr):
    span = out_ref.shape[0]
    heads = q_ref.shape[0] // span
    length, ctx_index, blocks = place_ref[0], place_ref[1], place_ref[2]
    queries = q_ref[...]
    rows = queries.shape[0]
    top_scr[...] = jnp.full(top_scr.shape, masked_score, F32)
    sum_scr[...] = jnp.zeros(sum_scr.shape, F32)
    lse_ref[...] = jnp.zeros(lse_ref.shape, F32)

    def step(block, nothing):
        start = pl.multiple_of(block * KEY_BLOCK, KEY_BLOCK)
        keys = kv_ref[pl.ds(start, KEY_BLOCK), :HEAD]
        values = kv_ref[pl.ds(start, KEY_BLOCK), HEAD:]
        scores = HEAD ** (-0.5) * mm_t(queries, keys)
        allowed = block_mask(scores.shape, span, block, ctx_index, length)
        scores = jnp.where(allowed, scores, masked_score)
        top = top_scr[...]
        fresh_top = jnp.maximum(top, jnp.max(scores, axis=1, keepdims=True))
        shares = jnp.where(allowed, jnp.exp(scores - fresh_top), 0.0)
        fade = jnp.exp(top - fresh_top)
        lse_ref[...] = lse_ref[...] * fade + jnp.sum(shares, axis=1, keepdims=True)
        sum_scr[...] = sum_scr[...] * fade + mm(shares, values)
        top_scr[...] = fresh_top
        return nothing

    lax.fori_loop(0, blocks, step, 0)
    total = lse_ref[...]
    result = sum_scr[...] / total
    for head in range(heads):
        out_ref[:, head * HEAD : (head + 1) * HEAD] = result[head * span : (head + 1) * span, :]
    lse_ref[...] = top_scr[...] + jnp.log(total)


def attend_forward(place, query_rows, key_all, span):
    rows = query_rows.shape[0]
    return pl.pallas_call(
        attend_forward_kernel,
        out_shape=(
            jax.ShapeDtypeStruct((span, rows // span * HEAD), F32),
            jax.ShapeDtypeStruct((rows, 1), F32),
        ),
        in_specs=[
            pl.BlockSpec(memory_space=pltpu.SMEM),
            pl.BlockSpec(memory_space=pltpu.VMEM),
            pl.BlockSpec(memory_space=pltpu.VMEM),
        ],
        scratch_shapes=[pltpu.VMEM((rows, 1), F32), pltpu.VMEM((rows, HEAD), F32)],
        compiler_params=pltpu.CompilerParams(vmem_limit_bytes=56 * 1024 * 1024),
    )(place, query_rows, key_all)


def attend_backward_kernel(
    place_ref, q_ref, kv_ref, lse_ref, out_ref, grad_ref, dq_ref, dkv_ref, dq_scr
):
    span = out_ref.shape[0]
    heads = q_ref.shape[0] // span
    length, ctx_index, blocks = place_ref[0], place_ref[1], place_ref[2]
    queries = q_ref[...]
    grad_rows = jnp.concatenate(
        [grad_ref[:, head * HEAD : (head + 1) * HEAD] for head in range(heads)], axis=0
    )
    out_rows = jnp.concatenate(
        [out_ref[:, head * HEAD : (head + 1) * HEAD] for head in range(heads)], axis=0
    )
    delta = jnp.sum(grad_rows.astype(F32) * out_rows, axis=1, keepdims=True)
    lse = lse_ref[...]
    dq_scr[...] = jnp.zeros(dq_scr.shape, F32)
    dkv_ref[...] = jnp.zeros(dkv_ref.shape, dkv_ref.dtype)

    def step(block, nothing):
        start = pl.multiple_of(block * KEY_BLOCK, KEY_BLOCK)
        keys = kv_ref[pl.ds(start, KEY_BLOCK), :HEAD]
        values = kv_ref[pl.ds(start, KEY_BLOCK), HEAD:]
        scores = HEAD ** (-0.5) * mm_t(queries, keys)
        allowed = block_mask(scores.shape, span, block, ctx_index, length)
        shares = jnp.where(allowed, jnp.exp(jnp.where(allowed, scores, masked_score) - lse), 0.0)
        grad_share = mm_t(grad_rows, values)
        grad_score = (shares * (grad_share - delta)).astype(BF)
        dq_scr[...] += mm(grad_score, keys)
        dkv_ref[pl.ds(start, KEY_BLOCK), :HEAD] = (
            HEAD ** (-0.5) * t_mm(grad_score, queries)
        ).astype(dkv_ref.dtype)
        dkv_ref[pl.ds(start, KEY_BLOCK), HEAD:] = t_mm(shares, grad_rows).astype(dkv_ref.dtype)
        return nothing

    lax.fori_loop(0, blocks, step, 0)
    for head in range(heads):
        dq_ref[:, head * HEAD : (head + 1) * HEAD] = (
            HEAD ** (-0.5) * dq_scr[head * span : (head + 1) * span, :]
        )


def attend_backward(place, query_rows, key_all, lse, attended, grad_low):
    span = attended.shape[0]
    rows = query_rows.shape[0]
    vm = pl.BlockSpec(memory_space=pltpu.VMEM)
    return pl.pallas_call(
        attend_backward_kernel,
        out_shape=(
            jax.ShapeDtypeStruct(attended.shape, F32),
            jax.ShapeDtypeStruct(key_all.shape, BF),
        ),
        in_specs=[pl.BlockSpec(memory_space=pltpu.SMEM), vm, vm, vm, vm, vm],
        scratch_shapes=[pltpu.VMEM((rows, HEAD), F32)],
        compiler_params=pltpu.CompilerParams(vmem_limit_bytes=56 * 1024 * 1024),
    )(place, query_rows, key_all, lse, attended, grad_low)


def swap(value):
    return lax.ppermute(value, "section", [(0, 1), (1, 0)])


def after(value, *others):
    return lax.optimization_barrier((value,) + others)[0]


def shifted(value, steps):
    count = lax.axis_size("ctx")
    first, last = max(0, -steps), min(count, count - steps)
    return lax.ppermute(value, "ctx", [(source, source + steps) for source in range(first, last)])


def exchange_sum(value, axis):
    count = lax.axis_size(axis)
    bit = 1
    while bit < count:
        moved = lax.ppermute(value, axis, [(place, place ^ bit) for place in range(count)])
        value = (value.astype(F32) + moved.astype(F32)).astype(value.dtype)
        bit *= 2
    return value


def rope_tables(positions):
    half_width = HEAD // 2
    frequencies = rope_base ** (-jnp.arange(half_width, dtype=F32) / half_width)
    angles = positions.astype(F32)[:, None] * frequencies[None, :]
    return jnp.cos(angles), jnp.sin(angles)


def rotate(values, tables, direction):
    half_width = HEAD // 2
    cosine, sine = tables[0], direction * tables[1]
    heads = []
    for head in range(values.shape[1] // HEAD):
        first = values[:, head * HEAD : head * HEAD + half_width]
        second = values[:, head * HEAD + half_width : (head + 1) * HEAD]
        heads.append(first * cosine - second * sine)
        heads.append(second * cosine + first * sine)
    return jnp.concatenate(heads, axis=1)


def gathered_rows(own, ctx_index):
    span = own.shape[0]
    count = lax.axis_size("ctx")
    rows = jnp.zeros((count * span, own.shape[1]), own.dtype)
    for steps in range(count - 1, 0, -1):
        place = jnp.maximum(ctx_index - steps, 0) * span
        rows = lax.dynamic_update_slice_in_dim(rows, shifted(own, steps), place, 0)
    return lax.dynamic_update_slice_in_dim(rows, own, ctx_index * span, 0)


def returned_rows(rows, span, ctx_index):
    count = lax.axis_size("ctx")
    total = lax.dynamic_slice_in_dim(rows, ctx_index * span, span, 0).astype(F32)
    for steps in range(1, count):
        place = jnp.maximum(ctx_index - steps, 0) * span
        part = lax.dynamic_slice_in_dim(rows, place, span, 0)
        total = total + shifted(part, -steps).astype(F32)
    return total


def moved_states(payload, reverse):
    count = lax.axis_size("ctx")
    return [shifted(payload, -steps if reverse else steps) for steps in range(1, count)]


def state_payload(state, total):
    decay = jnp.repeat(jnp.exp(total), MHEAD)[None, :]
    high = decay.astype(BF)
    low = (decay - high.astype(F32)).astype(BF)
    pad = jnp.zeros((14, decay.shape[1]), BF)
    return jnp.concatenate([state.astype(BF), high, low, pad], axis=0)


def wide(per_head):
    return jnp.repeat(per_head, MHEAD, axis=1)


def head_sum(values):
    return jnp.sum(values.reshape(values.shape[0], -1, MHEAD), axis=2)


def low_sum(value):
    return lax.psum(value.astype(BF), "wt").astype(F32)


class Weights:
    def keep(self, **values):
        self.__dict__.update(values)


def mixer_forward(entry_low, w, place):
    saved = Weights()
    saved.entry = entry_low
    entry = entry_low.astype(F32)
    normed = (entry * rms_scale(entry) * w.mixer_gain).astype(BF)
    small_in = mm_t(normed, w.mixin_down).astype(BF)
    shared = mm(normed, w.shared) + mm(small_in, w.shared_up)
    mamba_proj = mm(normed, w.mamba) + mm(small_in, w.mamba_up)
    span = entry.shape[0]
    local_heads = w.query.shape[1] // HEAD
    key_head = place.wt * local_heads // (QHEADS // KVHEADS)
    key_part = lax.dynamic_slice_in_dim(shared, key_head * HEAD, HEAD, 1)
    value_part = lax.dynamic_slice_in_dim(shared, (KVHEADS + key_head) * HEAD, HEAD, 1)
    key_value = jnp.concatenate([rotate(key_part, place.tables, 1.0), value_part], axis=1)
    key_all = gathered_rows(key_value.astype(BF), place.ctx)

    half = mamba_proj.shape[1] // 2
    heads = half // MHEAD
    gate_raw, inputs = mamba_proj[:, :half], mamba_proj[:, half:]
    offset = 2 * KVHEADS * HEAD
    input_map = shared[:, offset : offset + NSTATE].astype(BF)
    output_map = shared[:, offset + NSTATE : offset + 2 * NSTATE].astype(BF)
    step_raw = lax.dynamic_slice_in_dim(
        shared, offset + 2 * NSTATE + place.wt * heads, heads, 1
    )
    step_in = step_raw + w.step_bias
    step_sizes = jax.nn.softplus(step_in) * place.live[:, None]
    cum = jnp.dot(place.lower, -w.decay_rate * step_sizes, precision=HIGH)
    local_y, local_state = scan_forward(
        mamba_proj, input_map, output_map, step_sizes, cum, cum.T
    )
    payload = after(state_payload(local_state, cum[-1]), key_all)
    moved = moved_states(payload, False)
    normed_now, small_now = lax.optimization_barrier((normed, small_in, payload))[:2]
    query_proj = mm(normed_now, w.query) + mm(small_now, w.query_up)
    rotated = rotate(query_proj, place.tables, 1.0).astype(BF)
    query_rows = jnp.concatenate(
        [rotated[:, head * HEAD : (head + 1) * HEAD] for head in range(local_heads)], axis=0
    )
    attended, lse = attend_forward(place.scalars, query_rows, key_all, span)
    skip = jnp.repeat(w.skip_gain, MHEAD)[None, :]
    scanned, gated_low, state_in = scan_finish(
        local_y, mamba_proj, output_map, cum, skip, moved
    )
    attended_low = attended.astype(BF)
    small_mid = mm_t(attended_low, w.attnout_down) + mm_t(gated_low, w.mambaout_down)
    part = (
        mm(attended_low, w.attnout) + mm(gated_low, w.mambaout) + mm(small_mid, w.mixout_up)
    )
    saved.keep(
        normed=normed,
        small_in=small_in,
        query_rows=query_rows,
        key_all=key_all,
        key_head=key_head,
        gate_raw=gate_raw,
        inputs=inputs,
        proj=mamba_proj,
        input_map=input_map,
        output_map=output_map,
        step_in=step_in,
        step_sizes=step_sizes,
        cum=cum,
        state_in=state_in,
        scanned=scanned,
        attended=attended,
        lse=lse,
        gated_low=gated_low,
        attended_low=attended_low,
        small_mid=small_mid,
    )
    return part.astype(BF), saved


def feed_forward(entry_low, part, w, place, saved):
    mixed = after(lax.psum(part, "wt"), w.gateup, w.down)
    hidden = entry_low.astype(F32) + place.live[:, None] * mixed.astype(F32)
    feed_normed = (hidden * rms_scale(hidden) * w.feed_gain).astype(BF)
    small_feed = mm_t(feed_normed, w.feedin_down).astype(BF)
    gateup = mm(feed_normed, w.gateup) + mm(small_feed, w.feedin_up)
    width = gateup.shape[1] // 2
    gate_value, up_value = gateup[:, :width], gateup[:, width:]
    inner = (jax.nn.silu(gate_value) * up_value).astype(BF)
    small_out = mm_t(inner, w.feedout_down)
    feed_part = (mm(inner, w.down) + mm(small_out, w.feedout_up)).astype(BF)
    saved.keep(
        hidden=hidden,
        feed_normed=feed_normed,
        small_feed=small_feed,
        gate_value=gate_value,
        up_value=up_value,
        inner=inner,
        small_out=small_out,
    )
    return feed_part


def feed_backward(grad_out, w, place, s, finish):
    grads = Weights()
    grad_feed = grad_out.astype(BF)
    grad_small_out = mm_t(grad_feed, w.feedout_up)
    grad_inner = mm_t(grad_feed, w.down) + mm(grad_small_out, w.feedout_down)
    gate_value, up_value = s.gate_value, s.up_value
    sigmoid_gate = jax.nn.sigmoid(gate_value)
    grad_gate = grad_inner * up_value * sigmoid_gate * (1.0 + gate_value * (1.0 - sigmoid_gate))
    grad_up = grad_inner * gate_value * sigmoid_gate
    grad_gateup = jnp.concatenate([grad_gate, grad_up], axis=1).astype(BF)
    grad_small_feed = mm_t(grad_gateup, w.feedin_up)
    feed_norm_part = mm_t(grad_gateup, w.gateup) + mm(grad_small_feed, w.feedin_down)
    summed = lax.psum(feed_norm_part.astype(BF), "wt")
    small_all = exchange_sum(
        jnp.concatenate(
            [part.astype(BF) for part in (s.small_mid, s.small_out, grad_small_feed)], axis=1
        ),
        "wt",
    )
    rank = grad_small_feed.shape[1]
    s.small_mid = small_all[:, :rank]
    grads.feedout_up = t_mm(small_all[:, rank : 2 * rank], grad_feed)
    grads.feedout_down = t_mm(grad_small_out, s.inner)
    grads.feedin_up = t_mm(s.small_feed, grad_gateup)
    grads.feedin_down = t_mm(small_all[:, 2 * rank :], s.feed_normed)
    found = finish(grads)
    summed = after(summed, found[2]).astype(F32)
    return grad_out + norm_back(s.hidden, summed, w.feed_gain), found


def mixer_backward(grad_hidden, w, place, s, finish, before, late):
    grads = Weights()
    span = grad_hidden.shape[0]
    grad_mixed = (grad_hidden * place.live[:, None]).astype(BF)
    grad_small_mid = mm_t(grad_mixed, w.mixout_up)
    grad_gated = mm_t(grad_mixed, w.mambaout) + mm(grad_small_mid, w.mambaout_down)
    gate_raw, inputs, scanned = s.gate_raw, s.inputs, s.scanned
    skip = jnp.repeat(w.skip_gain, MHEAD)[None, :]
    sigmoid_raw = jax.nn.sigmoid(gate_raw)
    silu_raw = gate_raw * sigmoid_raw
    dy_low = (grad_gated * silu_raw).astype(BF)
    dy = dy_low.astype(F32)
    grad_gates = (
        grad_gated * (scanned + skip * inputs) * sigmoid_raw * (1.0 + gate_raw * (1.0 - sigmoid_raw))
    )
    cum, step_sizes = s.cum, s.step_sizes
    grown = wide(jnp.exp(cum))
    grown_dy = (grown * dy).astype(BF)
    local_grad = t_mm(s.output_map, grown_dy)
    payload = state_payload(local_grad, cum[-1])
    moved = moved_states(payload, True)
    dy_now, grad_mid, small_now = lax.optimization_barrier(
        (dy_low, grad_mixed, grad_small_mid, payload)
    )[:3]

    grad_attended = (
        mm_t(grad_mid, w.attnout) + mm(small_now, w.attnout_down)
    ).astype(BF)
    grad_query, grad_keyval = attend_backward(
        place.scalars, s.query_rows, s.key_all, s.lse, s.attended, grad_attended
    )
    own = returned_rows(after(grad_keyval, *moved), span, place.ctx)

    z_local, db_local, dc_local = scan_backward(
        inputs, dy_now, s.input_map, s.output_map, step_sizes, cum, cum.T
    )
    grad_inputs, grad_map_in, grad_map_out, grad_step = scan_close(
        inputs,
        dy_low,
        z_local,
        scanned,
        s.input_map,
        s.state_in,
        db_local,
        dc_local,
        step_sizes,
        cum,
        s.step_in,
        place.live[:, None],
        w.decay_rate[None, :],
        skip,
        moved,
    )

    heads = cum.shape[1]
    grad_query_low = rotate(grad_query, place.tables, -1.0).astype(BF)
    grad_keys = rotate(own[:, :HEAD], place.tables, -1.0)
    key_head = s.key_head
    offset = 2 * KVHEADS * HEAD
    keyval = jnp.zeros((span, offset), F32)
    keyval = lax.dynamic_update_slice_in_dim(keyval, grad_keys, key_head * HEAD, 1)
    keyval = lax.dynamic_update_slice_in_dim(
        keyval, own[:, HEAD:], (KVHEADS + key_head) * HEAD, 1
    )
    all_heads = w.shared.shape[1] - offset - 2 * NSTATE
    step_part = lax.dynamic_update_slice_in_dim(
        jnp.zeros((span, all_heads), F32), grad_step, place.wt * heads, 1
    )
    grad_shared = jnp.concatenate(
        [keyval.astype(BF), grad_map_in, grad_map_out, step_part.astype(BF)], axis=1
    )
    grad_mamba = jnp.concatenate([grad_gates.astype(BF), grad_inputs], axis=1)
    grad_small_in = (
        mm_t(grad_query_low, w.query_up)
        + mm_t(grad_mamba, w.mamba_up)
        + mm_t(grad_shared, w.shared_up)
    )
    norm_part = (
        mm_t(grad_query_low, w.query)
        + mm_t(grad_mamba, w.mamba)
        + mm_t(grad_shared, w.shared)
        + mm(grad_small_in, w.mixin_down)
    )
    norm_part = after(norm_part.astype(BF), *before)
    summed = lax.psum(norm_part, "wt")
    grads.mixout_up = t_mm(s.small_mid, grad_mixed)
    grads.attnout_down = t_mm(grad_small_mid, s.attended_low)
    grads.mambaout_down = t_mm(grad_small_mid, s.gated_low)
    grads.query_up = t_mm(s.small_in, grad_query_low)
    grads.mamba_up = t_mm(s.small_in, grad_mamba)
    grads.shared_up = t_mm(s.small_in, grad_shared)
    grads.mixin_down = t_mm(grad_small_in, s.normed)
    found = finish(grads, *((summed,) if late else ()))
    grad_entry = grad_hidden + norm_back(
        s.entry.astype(F32), summed.astype(F32), w.mixer_gain
    )
    return grad_entry, found


FIXED = (
    "mixer_gain",
    "feed_gain",
    "decay_rate",
    "step_bias",
    "skip_gain",
    "query",
    "mamba",
    "shared",
    "attnout",
    "mambaout",
    "gateup",
    "down",
)
ADAPTERS = (
    "mixin_down",
    "query_up",
    "mamba_up",
    "shared_up",
    "attnout_down",
    "mambaout_down",
    "mixout_up",
    "feedin_down",
    "feedin_up",
    "feedout_down",
    "feedout_up",
)
PARTIAL = ("mixin_down", "shared_up")
PACKS = (
    ("mixin_down", "mamba_up", "query_up", "shared_up"),
    ("mixout_up", "mambaout_down", "attnout_down"),
    ("feedin_down", "feedin_up", "feedout_up", "feedout_down"),
)
GROUPS = (
    ("shared", "query", "mamba"),
    ("attnout", "mambaout"),
    ("gateup", "down"),
)


def shards(layer_input, cotangent, seq_lengths, adapter_ids, *params):
    section = lax.axis_index("section")
    ctx_index = lax.axis_index("ctx")
    micro_count, span = layer_input.shape[0], layer_input.shape[1]
    assert micro_count == 2 and lax.axis_size("section") == 2

    place = Weights()
    place.wt = lax.axis_index("wt")
    place.ctx = ctx_index
    length = seq_lengths[section]
    positions = ctx_index * span + jnp.arange(span, dtype=jnp.int32)
    place.live = (positions < length).astype(F32)
    place.tables = rope_tables(positions)
    row = lax.broadcasted_iota(jnp.int32, (span, span), 0)
    col = lax.broadcasted_iota(jnp.int32, (span, span), 1)
    place.lower = (row >= col).astype(F32)
    blocks = jnp.minimum(
        ((ctx_index + 1) * span + KEY_BLOCK - 1) // KEY_BLOCK, (length + KEY_BLOCK - 1) // KEY_BLOCK
    )
    place.scalars = jnp.stack([length, ctx_index, blocks]).astype(jnp.int32)

    own, items, shapes = {}, {}, {}
    for name, item in zip(FIXED, params):
        own[name] = item[0]
    mine, theirs = adapter_ids[section], adapter_ids[1 - section]
    for name, item in zip(ADAPTERS, params[len(FIXED) :]):
        shapes[name] = item.shape[1:]
        items[name] = item[0]
    layers = (Weights(), Weights())

    def place_pack(names, widths, kept, moved):
        for index, w in enumerate(layers):
            value = jnp.where(section == index, kept, moved)
            start = 0
            for name, width in zip(names, widths):
                setattr(w, name, value[..., start : start + width])
                start += width

    def exchange_pack(number, *gates):
        names = PACKS[number]
        widths = [items[name][0, 0].size for name in names]
        packed = jnp.concatenate(
            [items[name].reshape(items[name].shape[:2] + (-1,)) for name in names], axis=2
        )
        packed = lax.optimization_barrier((packed,) + gates)[0]
        moved = swap(lax.dynamic_index_in_dim(packed, theirs, 0, keepdims=False))
        kept = lax.dynamic_index_in_dim(packed, mine, 0, keepdims=False)
        place_pack(names, widths, kept, moved)

    vectors = FIXED[:5]
    joined = jnp.concatenate([own[name].astype(F32) for name in vectors])
    place_pack(vectors, [own[name].size for name in vectors], joined, swap(joined))
    exchange_pack(0)
    done = []
    for group in GROUPS:
        moved = {name: swap(after(own[name], *done)) for name in group}
        done = done or list(moved.values())
        for name in group:
            for index, w in enumerate(layers):
                value = jnp.where(section == index, own[name], moved[name])
                if value.ndim == 3:
                    value = value.reshape(value.shape[0], -1)
                setattr(w, name, lax.optimization_barrier(value))
    exchange_pack(1, *done)

    first, second = layers
    entry = lax.dynamic_index_in_dim(layer_input, section, 0, keepdims=False)
    part, saved_first = mixer_forward(entry, first, place)
    exchange_pack(2, part)
    feed_part = feed_forward(entry, part, first, place, saved_first)
    following = [getattr(second, name) for name in GROUPS[0] + GROUPS[1]]
    fed = after(lax.psum(feed_part, "wt"), *following)
    first_out = (saved_first.hidden + fed.astype(F32)).astype(BF)
    part, saved_second = mixer_forward(first_out, second, place)
    last_part = feed_forward(first_out, part, second, place, saved_second)

    def forth(value):
        return lax.ppermute(value, "section", [(0, 1)])

    def back(value):
        return lax.ppermute(value, "section", [(1, 0)])

    def reduced(found):
        names = list(found)
        packed = jnp.concatenate(
            [found[name].astype(BF).reshape(found[name].shape[0], -1) for name in names], axis=1
        )
        return names, [found[name].shape[1] for name in names], packed

    def summed_grads(grads, *gates):
        found = vars(grads)
        partial = {name: found[name] for name in found if name in PARTIAL}
        whole = {name: found[name] for name in found if name not in PARTIAL}
        names, widths, packed = reduced(whole)
        packed = after(packed, *gates)
        if partial:
            more, extra, part = reduced(partial)
            part = after(part, *gates)
            names, widths = names + more, widths + extra
            packed = jnp.concatenate([packed, exchange_sum(part, "wt")], axis=1)
        return names, widths, exchange_sum(packed, "ctx")

    grad = lax.dynamic_index_in_dim(cotangent, section, 0, keepdims=False).astype(F32)
    grad_hidden, found = feed_backward(grad, second, place, saved_second, summed_grads)
    second_sets = [found]
    last_part = after(last_part, grad_hidden)
    second_out = (saved_second.hidden + low_sum(last_part)).astype(BF)
    grad, found = mixer_backward(
        grad_hidden, second, place, saved_second, summed_grads, (second_out,), True
    )
    second_grad = grad.astype(BF)
    second_sets.append(found)
    grad_hidden, found = feed_backward(
        second_grad.astype(F32), first, place, saved_first, summed_grads
    )
    first_sets = [found]
    grad, found = mixer_backward(
        grad_hidden, first, place, saved_first, summed_grads, (), False
    )
    first_grad = grad.astype(BF)
    first_sets.append(found)

    def stacked(early, late):
        return jnp.where(
            section == 0, jnp.stack([early, back(early)]), jnp.stack([forth(late), late])
        )[None]

    found = {}
    adapters = jnp.arange(params[len(FIXED)].shape[1], dtype=jnp.int32)[:, None, None]
    for first_set, second_set in zip(first_sets, second_sets):
        keep = jnp.where(section == 0, first_set[2], second_set[2])
        moved = jnp.where(section == 0, back(first_set[2]), forth(second_set[2]))
        start = 0
        for name, width in zip(first_set[0], first_set[1]):
            lanes = slice(start, start + width)
            start += width
            total = jnp.where(adapters == mine, keep[None, :, lanes].astype(F32), 0.0)
            total = total + jnp.where(adapters == theirs, moved[None, :, lanes].astype(F32), 0.0)
            found[name] = total.reshape(shapes[name])[None]
    return (
        stacked(first_out, second_out),
        stacked(first_grad, second_grad),
    ) + tuple(found[name] for name in ADAPTERS)


def solution(mesh):
    in_specs = (
        P(None, "ctx", None),
        P(None, "ctx", None),
        P(),
        P(),
        P("section", None),
        P("section", None),
        P("section", "wt"),
        P("section", "wt"),
        P("section", "wt"),
        P("section", None, "wt"),
        P("section", None, None, "wt"),
        P("section", None, None),
        P("section", "wt", None),
        P("section", "wt", None),
        P("section", None, None, "wt"),
        P("section", "wt", None),
        P("section", None, None, None),
        P("section", None, None, "wt"),
        P("section", None, None, None, "wt"),
        P("section", None, None, None),
        P("section", None, None, "wt"),
        P("section", None, None, "wt"),
        P("section", None, None, None),
        P("section", None, None, None),
        P("section", None, None, None, "wt"),
        P("section", None, None, "wt"),
        P("section", None, None, None),
    )
    out_specs = (
        P("section", None, "ctx", None),
        P("section", None, "ctx", None),
    ) + in_specs[16:]
    return jax.shard_map(shards, mesh=mesh, in_specs=in_specs, out_specs=out_specs, check_vma=False)
```

```python
import functools

import jax
import jax.numpy as jnp
from jax import lax
from jax.experimental import pallas as pl
from jax.experimental.pallas import tpu as pltpu
from jax.sharding import PartitionSpec as P

QHEADS = 8
KVHEADS = 2
HEAD = 128
MHEAD = 64
NSTATE = 256
KEY_BLOCK = 256
PAIR = 2 * MHEAD

epsilon = 1e-05
rope_base = 10000.0
masked_score = -1e30
BF = jnp.bfloat16
F32 = jnp.float32
HIGH = lax.Precision.HIGHEST


def mm(a, b):
    return jnp.dot(a.astype(BF), b.astype(BF), preferred_element_type=F32)


def mm_t(a, b):
    return lax.dot_general(
        a.astype(BF), b.astype(BF), (((1,), (1,)), ((), ())), preferred_element_type=F32
    )


def t_mm(a, b):
    return lax.dot_general(
        a.astype(BF), b.astype(BF), (((0,), (0,)), ((), ())), preferred_element_type=F32
    )


def rms_scale(vector):
    return lax.rsqrt(jnp.mean(vector * vector, axis=-1, keepdims=True) + epsilon)


def norm_back(vector, grad_normed, gain_vec):
    scale_now = rms_scale(vector)
    weighted = grad_normed * gain_vec
    return weighted * scale_now - vector * scale_now**3 * jnp.mean(
        weighted * vector, axis=-1, keepdims=True
    )


def vmem_call(kernel, out_shape, **kwargs):
    return pl.pallas_call(
        kernel,
        out_shape=out_shape,
        compiler_params=pltpu.CompilerParams(vmem_limit_bytes=56 * 1024 * 1024),
        **kwargs,
    )


def pair_lanes(rows, left, right):
    lane = lax.broadcasted_iota(jnp.int32, (rows, PAIR), 1)
    return jnp.where(lane < MHEAD, left, right)


def moved_sum(moved_refs, states, lanes):
    total, between = 0.0, 1.0
    for moved_ref in moved_refs:
        total = total + between * moved_ref[:states, lanes].astype(F32)
        ends = moved_ref[states : states + 16, lanes].astype(F32)
        between = between * (ends[0:1, :] + ends[1:2, :])
    return total


def scan_finish_kernel(y_ref, proj_ref, c_ref, cum_ref, skip_ref, *refs):
    moved_refs, (out_ref, gated_ref, state_ref) = refs[:-3], refs[-3:]
    rows, width = y_ref.shape
    states = c_ref.shape[1]
    heads = cum_ref.shape[1]
    grown = jnp.exp(cum_ref[...])
    for pair in range(heads // 2):
        one, two = 2 * pair, 2 * pair + 1
        lanes = slice(PAIR * pair, PAIR * (pair + 1))
        state = moved_sum(moved_refs, states, lanes).astype(BF)
        state_ref[:, lanes] = state
        grown_pair = pair_lanes(rows, grown[:, one : one + 1], grown[:, two : two + 1])
        scanned = y_ref[:, lanes] + grown_pair * mm(c_ref[...], state)
        out_ref[:, lanes] = scanned
        gate = proj_ref[:, lanes]
        joined = scanned + skip_ref[:, lanes] * proj_ref[:, width + PAIR * pair : width + PAIR * (pair + 1)]
        gated_ref[:, lanes] = (joined * (gate / (1.0 + jnp.exp(-gate)))).astype(BF)


def scan_finish(y, proj, c_low, cum, skip, moved):
    rows, width = y.shape
    return vmem_call(
        scan_finish_kernel,
        (
            jax.ShapeDtypeStruct((rows, width), F32),
            jax.ShapeDtypeStruct((rows, width), BF),
            jax.ShapeDtypeStruct((c_low.shape[1], width), BF),
        ),
    )(y, proj, c_low, cum, skip, *moved)


def scan_forward_kernel(x_ref, b_ref, c_ref, dt_ref, cum_ref, cumt_ref, y_ref, state_ref, tail_scr):
    rows = x_ref.shape[0]
    heads = dt_ref.shape[1]
    width = heads * MHEAD
    gram = mm_t(c_ref[...], b_ref[...])
    row = lax.broadcasted_iota(jnp.int32, (rows, rows), 0)
    col = lax.broadcasted_iota(jnp.int32, (rows, rows), 1)
    gram = jnp.where(row >= col, gram, 0.0)
    cum = cum_ref[...]
    dt = dt_ref[...]
    cumt = cumt_ref[...]
    tail = jnp.exp(cum[rows - 1 : rows, :] - cum)
    for pair in range(heads // 2):
        one, two = 2 * pair, 2 * pair + 1
        lanes = slice(PAIR * pair, PAIR * (pair + 1))
        scaled = x_ref[:, width + PAIR * pair : width + PAIR * (pair + 1)] * pair_lanes(rows, dt[:, one : one + 1], dt[:, two : two + 1])
        scaled_low = scaled.astype(BF)
        tail_scr[:, lanes] = (
            scaled * pair_lanes(rows, tail[:, one : one + 1], tail[:, two : two + 1])
        ).astype(BF)
        parts = []
        for head in (one, two):
            decay = jnp.exp(jnp.minimum(cum[:, head : head + 1] - cumt[head : head + 1, :], 0.0))
            parts.append(mm((gram * decay), scaled_low))
        y_ref[:, lanes] = pair_lanes(rows, parts[0], parts[1])
    state_ref[...] = t_mm(b_ref[...], tail_scr[...]).astype(state_ref.dtype)


def scan_forward(x, b_low, c_low, dt, cum, cumt):
    rows, width = x.shape[0], dt.shape[1] * MHEAD
    return vmem_call(
        scan_forward_kernel,
        (
            jax.ShapeDtypeStruct((rows, width), F32),
            jax.ShapeDtypeStruct((b_low.shape[1], width), BF),
        ),
        scratch_shapes=[pltpu.VMEM((rows, width), BF)],
    )(x, b_low, c_low, dt, cum, cumt)


def scan_backward_kernel(
    x_ref, dy_ref, b_ref, c_ref, dt_ref, cum_ref, cumt_ref, z_ref, db_ref, dc_ref
):
    rows = x_ref.shape[0]
    heads = dt_ref.shape[1]
    gram_t = mm_t(b_ref[...], c_ref[...])
    row = lax.broadcasted_iota(jnp.int32, (rows, rows), 0)
    col = lax.broadcasted_iota(jnp.int32, (rows, rows), 1)
    causal = col >= row
    gram_t = jnp.where(causal, gram_t, 0.0)
    cum = cum_ref[...]
    dt = dt_ref[...]
    cumt = cumt_ref[...]
    grad_gram_t = jnp.zeros((rows, rows), F32)
    lane = lax.broadcasted_iota(jnp.int32, (rows, PAIR), 1)
    for pair in range(heads // 2):
        one, two = 2 * pair, 2 * pair + 1
        lanes = slice(PAIR * pair, PAIR * (pair + 1))
        scaled_low = (
            x_ref[:, lanes] * pair_lanes(rows, dt[:, one : one + 1], dt[:, two : two + 1])
        ).astype(BF)
        dy = dy_ref[:, lanes]
        parts = []
        for head in (one, two):
            decay = jnp.exp(jnp.minimum(cumt[head : head + 1, :] - cum[:, head : head + 1], 0.0))
            parts.append(mm(gram_t * decay, dy))
            mine = (lane < MHEAD) if head == one else (lane >= MHEAD)
            outer = mm_t(jnp.where(mine, scaled_low, jnp.zeros_like(scaled_low)), dy)
            grad_gram_t = grad_gram_t + decay * outer
        z_ref[:, lanes] = pair_lanes(rows, parts[0], parts[1])
    grad_low = jnp.where(causal, grad_gram_t, 0.0).astype(BF)
    db_ref[...] = mm(grad_low, c_ref[...])
    dc_ref[...] = t_mm(grad_low, b_ref[...])


def scan_backward(x, dy_low, b_low, c_low, dt, cum, cumt):
    rows, width = x.shape
    states = b_low.shape[1]
    return vmem_call(
        scan_backward_kernel,
        (
            jax.ShapeDtypeStruct((rows, width), F32),
            jax.ShapeDtypeStruct((rows, states), F32),
            jax.ShapeDtypeStruct((rows, states), F32),
        ),
    )(x, dy_low, b_low, c_low, dt, cum, cumt)


def scan_close_kernel(
    x_ref,
    dy_ref,
    z_ref,
    y_ref,
    b_ref,
    state_ref,
    db_ref,
    dc_ref,
    dt_ref,
    cum_ref,
    step_ref,
    live_ref,
    rate_ref,
    skip_ref,
    *refs,
):
    moved_refs = refs[:-10]
    dx_ref, db_out_ref, dc_out_ref, dstep_ref = refs[-10:-6]
    through_scr, step_scr, edge_scr, tail_scr, grown_scr, grad_state_scr = refs[-6:]
    rows, width = x_ref.shape
    heads = dt_ref.shape[1]
    cum = cum_ref[...]
    dt = dt_ref[...]
    last = cum[rows - 1 : rows, :]
    tail = jnp.exp(last - cum)
    grown = jnp.exp(cum)
    whole = jnp.exp(last)
    for pair in range(heads // 2):
        one, two = 2 * pair, 2 * pair + 1
        lanes = slice(PAIR * pair, PAIR * (pair + 1))
        dt_pair = pair_lanes(rows, dt[:, one : one + 1], dt[:, two : two + 1])
        tail_pair = pair_lanes(rows, tail[:, one : one + 1], tail[:, two : two + 1])
        grown_pair = pair_lanes(rows, grown[:, one : one + 1], grown[:, two : two + 1])
        whole_pair = pair_lanes(1, whole[:, one : one + 1], whole[:, two : two + 1])
        x = x_ref[:, lanes]
        dy = dy_ref[:, lanes].astype(F32)
        grad_state = moved_sum(moved_refs, b_ref.shape[1], lanes).astype(BF)
        grad_state_scr[:, lanes] = grad_state
        z_tail = tail_pair * mm(b_ref[...], grad_state)
        z_all = z_ref[:, lanes] + z_tail
        dx_ref[:, lanes] = (dt_pair * z_all + skip_ref[:, lanes] * dy).astype(dx_ref.dtype)
        scaled = (x * dt_pair).astype(BF).astype(F32)
        tail_scr[:, lanes] = (tail_pair * scaled).astype(BF)
        grown_scr[:, lanes] = (grown_pair * dy).astype(BF)
        through_scr[:, lanes] = dy * y_ref[:, lanes] - scaled * z_all
        step_scr[:, lanes] = x * z_all
        kept = jnp.sum(
            grad_state.astype(F32) * state_ref[:, lanes].astype(F32), axis=0, keepdims=True
        )
        edge = jnp.sum(scaled * z_tail, axis=0, keepdims=True) + kept * whole_pair
        edge_scr[:, lanes] = jnp.broadcast_to(edge, (edge_scr.shape[0], PAIR))
    db_out_ref[...] = (db_ref[...] + mm_t(tail_scr[...], grad_state_scr[...])).astype(BF)
    dc_out_ref[...] = (dc_ref[...] + mm_t(grown_scr[...], state_ref[...])).astype(BF)
    lane = lax.broadcasted_iota(jnp.int32, (width, heads), 0)
    head = lax.broadcasted_iota(jnp.int32, (width, heads), 1)
    member = ((lane >= head * MHEAD) & (lane < (head + 1) * MHEAD)).astype(F32)
    row = lax.broadcasted_iota(jnp.int32, (rows, rows), 0)
    col = lax.broadcasted_iota(jnp.int32, (rows, rows), 1)
    later = (col >= row).astype(F32)

    def exact(a, b):
        return jnp.dot(a, b, precision=HIGH, preferred_element_type=F32)

    cum_grad = exact(later, exact(through_scr[...], member))
    cum_grad = cum_grad + exact(edge_scr[...], member)[0:1, :]
    grad_steps = exact(step_scr[...], member) - rate_ref[...] * cum_grad
    dstep_ref[...] = grad_steps * live_ref[...] / (1.0 + jnp.exp(-step_ref[...]))


def scan_close(x, dy_low, z, y, b_low, state, db, dc, dt, cum, step, live, rate, skip, moved):
    rows, width = x.shape
    states, heads = b_low.shape[1], dt.shape[1]
    return vmem_call(
        scan_close_kernel,
        (
            jax.ShapeDtypeStruct((rows, width), BF),
            jax.ShapeDtypeStruct((rows, states), BF),
            jax.ShapeDtypeStruct((rows, states), BF),
            jax.ShapeDtypeStruct((rows, heads), F32),
        ),
        scratch_shapes=[
            pltpu.VMEM((rows, width), F32),
            pltpu.VMEM((rows, width), F32),
            pltpu.VMEM((8, width), F32),
            pltpu.VMEM((rows, width), BF),
            pltpu.VMEM((rows, width), BF),
            pltpu.VMEM((states, width), BF),
        ],
    )(x, dy_low, z, y, b_low, state, db, dc, dt, cum, step, live, rate, skip, *moved)


def block_mask(scores_shape, span, block, ctx_index, length):
    row = lax.broadcasted_iota(jnp.int32, scores_shape, 0)
    query_pos = ctx_index * span + lax.rem(row, span)
    key_pos = block * KEY_BLOCK + lax.broadcasted_iota(jnp.int32, scores_shape, 1)
    return (key_pos <= query_pos) & (key_pos < length)


def attend_forward_kernel(place_ref, q_ref, kv_ref, out_ref, lse_ref, top_scr, sum_scr):
    span = out_ref.shape[0]
    heads = q_ref.shape[0] // span
    length, ctx_index, blocks = place_ref[0], place_ref[1], place_ref[2]
    queries = q_ref[...]
    rows = queries.shape[0]
    top_scr[...] = jnp.full(top_scr.shape, masked_score, F32)
    sum_scr[...] = jnp.zeros(sum_scr.shape, F32)
    lse_ref[...] = jnp.zeros(lse_ref.shape, F32)

    def step(block, nothing):
        start = pl.multiple_of(block * KEY_BLOCK, KEY_BLOCK)
        keys = kv_ref[pl.ds(start, KEY_BLOCK), :HEAD]
        values = kv_ref[pl.ds(start, KEY_BLOCK), HEAD:]
        scores = HEAD ** (-0.5) * mm_t(queries, keys)
        allowed = block_mask(scores.shape, span, block, ctx_index, length)
        scores = jnp.where(allowed, scores, masked_score)
        top = top_scr[...]
        fresh_top = jnp.maximum(top, jnp.max(scores, axis=1, keepdims=True))
        shares = jnp.where(allowed, jnp.exp(scores - fresh_top), 0.0)
        fade = jnp.exp(top - fresh_top)
        lse_ref[...] = lse_ref[...] * fade + jnp.sum(shares, axis=1, keepdims=True)
        sum_scr[...] = sum_scr[...] * fade + mm(shares, values)
        top_scr[...] = fresh_top
        return nothing

    lax.fori_loop(0, blocks, step, 0)
    total = lse_ref[...]
    result = sum_scr[...] / total
    for head in range(heads):
        out_ref[:, head * HEAD : (head + 1) * HEAD] = result[head * span : (head + 1) * span, :]
    lse_ref[...] = top_scr[...] + jnp.log(total)


def attend_forward(place, query_rows, key_all, span):
    rows = query_rows.shape[0]
    return pl.pallas_call(
        attend_forward_kernel,
        out_shape=(
            jax.ShapeDtypeStruct((span, rows // span * HEAD), F32),
            jax.ShapeDtypeStruct((rows, 1), F32),
        ),
        in_specs=[
            pl.BlockSpec(memory_space=pltpu.SMEM),
            pl.BlockSpec(memory_space=pltpu.VMEM),
            pl.BlockSpec(memory_space=pltpu.VMEM),
        ],
        scratch_shapes=[pltpu.VMEM((rows, 1), F32), pltpu.VMEM((rows, HEAD), F32)],
        compiler_params=pltpu.CompilerParams(vmem_limit_bytes=56 * 1024 * 1024),
    )(place, query_rows, key_all)


def attend_backward_kernel(
    place_ref, q_ref, kv_ref, lse_ref, out_ref, grad_ref, dq_ref, dkv_ref, dq_scr
):
    span = out_ref.shape[0]
    heads = q_ref.shape[0] // span
    length, ctx_index, blocks = place_ref[0], place_ref[1], place_ref[2]
    queries = q_ref[...]
    grad_rows = jnp.concatenate(
        [grad_ref[:, head * HEAD : (head + 1) * HEAD] for head in range(heads)], axis=0
    )
    out_rows = jnp.concatenate(
        [out_ref[:, head * HEAD : (head + 1) * HEAD] for head in range(heads)], axis=0
    )
    delta = jnp.sum(grad_rows.astype(F32) * out_rows, axis=1, keepdims=True)
    lse = lse_ref[...]
    dq_scr[...] = jnp.zeros(dq_scr.shape, F32)
    dkv_ref[...] = jnp.zeros(dkv_ref.shape, dkv_ref.dtype)

    def step(block, nothing):
        start = pl.multiple_of(block * KEY_BLOCK, KEY_BLOCK)
        keys = kv_ref[pl.ds(start, KEY_BLOCK), :HEAD]
        values = kv_ref[pl.ds(start, KEY_BLOCK), HEAD:]
        scores = HEAD ** (-0.5) * mm_t(queries, keys)
        allowed = block_mask(scores.shape, span, block, ctx_index, length)
        shares = jnp.where(allowed, jnp.exp(jnp.where(allowed, scores, masked_score) - lse), 0.0)
        grad_share = mm_t(grad_rows, values)
        grad_score = (shares * (grad_share - delta)).astype(BF)
        dq_scr[...] += mm(grad_score, keys)
        dkv_ref[pl.ds(start, KEY_BLOCK), :HEAD] = (
            HEAD ** (-0.5) * t_mm(grad_score, queries)
        ).astype(dkv_ref.dtype)
        dkv_ref[pl.ds(start, KEY_BLOCK), HEAD:] = t_mm(shares, grad_rows).astype(dkv_ref.dtype)
        return nothing

    lax.fori_loop(0, blocks, step, 0)
    for head in range(heads):
        dq_ref[:, head * HEAD : (head + 1) * HEAD] = (
            HEAD ** (-0.5) * dq_scr[head * span : (head + 1) * span, :]
        )


def attend_backward(place, query_rows, key_all, lse, attended, grad_low):
    span = attended.shape[0]
    rows = query_rows.shape[0]
    vm = pl.BlockSpec(memory_space=pltpu.VMEM)
    return pl.pallas_call(
        attend_backward_kernel,
        out_shape=(
            jax.ShapeDtypeStruct(attended.shape, F32),
            jax.ShapeDtypeStruct(key_all.shape, BF),
        ),
        in_specs=[pl.BlockSpec(memory_space=pltpu.SMEM), vm, vm, vm, vm, vm],
        scratch_shapes=[pltpu.VMEM((rows, HEAD), F32)],
        compiler_params=pltpu.CompilerParams(vmem_limit_bytes=56 * 1024 * 1024),
    )(place, query_rows, key_all, lse, attended, grad_low)


def swap(value):
    return lax.ppermute(value, "section", [(0, 1), (1, 0)])


def after(value, *others):
    return lax.optimization_barrier((value,) + others)[0]


def shifted(value, steps):
    count = lax.axis_size("ctx")
    first, last = max(0, -steps), min(count, count - steps)
    return lax.ppermute(value, "ctx", [(source, source + steps) for source in range(first, last)])


def exchange_sum(value, axis):
    count = lax.axis_size(axis)
    if count == 4:
        parts = [value.astype(F32)]
        for step in range(1, count):
            pairs = [(place, place ^ step) for place in range(count)]
            parts.append(lax.ppermute(value, axis, pairs).astype(F32))
        return ((parts[0] + parts[1]) + (parts[2] + parts[3])).astype(value.dtype)
    bit = 1
    while bit < count:
        moved = lax.ppermute(value, axis, [(place, place ^ bit) for place in range(count)])
        value = (value.astype(F32) + moved.astype(F32)).astype(value.dtype)
        bit *= 2
    return value


def rope_tables(positions):
    half_width = HEAD // 2
    frequencies = rope_base ** (-jnp.arange(half_width, dtype=F32) / half_width)
    angles = positions.astype(F32)[:, None] * frequencies[None, :]
    return jnp.cos(angles), jnp.sin(angles)


def rotate(values, tables, direction):
    half_width = HEAD // 2
    cosine, sine = tables[0], direction * tables[1]
    heads = []
    for head in range(values.shape[1] // HEAD):
        first = values[:, head * HEAD : head * HEAD + half_width]
        second = values[:, head * HEAD + half_width : (head + 1) * HEAD]
        heads.append(first * cosine - second * sine)
        heads.append(second * cosine + first * sine)
    return jnp.concatenate(heads, axis=1)


def gathered_rows(own, ctx_index):
    span = own.shape[0]
    count = lax.axis_size("ctx")
    rows = jnp.zeros((count * span, own.shape[1]), own.dtype)
    for steps in range(count - 1, 0, -1):
        place = jnp.maximum(ctx_index - steps, 0) * span
        rows = lax.dynamic_update_slice_in_dim(rows, shifted(own, steps), place, 0)
    return lax.dynamic_update_slice_in_dim(rows, own, ctx_index * span, 0)


def returned_rows(rows, span, ctx_index):
    count = lax.axis_size("ctx")
    total = lax.dynamic_slice_in_dim(rows, ctx_index * span, span, 0).astype(F32)
    for steps in range(1, count):
        place = jnp.maximum(ctx_index - steps, 0) * span
        part = lax.dynamic_slice_in_dim(rows, place, span, 0)
        total = total + shifted(part, -steps).astype(F32)
    return total


def moved_states(payload, reverse):
    count = lax.axis_size("ctx")
    return [shifted(payload, -steps if reverse else steps) for steps in range(1, count)]


def state_payload(state, total):
    decay = jnp.repeat(jnp.exp(total), MHEAD)[None, :]
    high = decay.astype(BF)
    low = (decay - high.astype(F32)).astype(BF)
    pad = jnp.zeros((14, decay.shape[1]), BF)
    return jnp.concatenate([state.astype(BF), high, low, pad], axis=0)


def wide(per_head):
    return jnp.repeat(per_head, MHEAD, axis=1)


def head_sum(values):
    return jnp.sum(values.reshape(values.shape[0], -1, MHEAD), axis=2)


def low_sum(value):
    return lax.psum(value.astype(BF), "wt").astype(F32)


class Weights:
    def keep(self, **values):
        self.__dict__.update(values)


def mixer_forward(entry_low, w, place):
    saved = Weights()
    saved.entry = entry_low
    entry = entry_low.astype(F32)
    normed = (entry * rms_scale(entry) * w.mixer_gain).astype(BF)
    small_in = mm_t(normed, w.mixin_down).astype(BF)
    shared = mm(normed, w.shared) + mm(small_in, w.shared_up)
    mamba_proj = mm(normed, w.mamba) + mm(small_in, w.mamba_up)
    span = entry.shape[0]
    local_heads = w.query.shape[1] // HEAD
    key_head = place.wt * local_heads // (QHEADS // KVHEADS)
    key_part = lax.dynamic_slice_in_dim(shared, key_head * HEAD, HEAD, 1)
    value_part = lax.dynamic_slice_in_dim(shared, (KVHEADS + key_head) * HEAD, HEAD, 1)
    key_value = jnp.concatenate([rotate(key_part, place.tables, 1.0), value_part], axis=1)
    key_all = gathered_rows(key_value.astype(BF), place.ctx)

    half = mamba_proj.shape[1] // 2
    heads = half // MHEAD
    gate_raw, inputs = mamba_proj[:, :half], mamba_proj[:, half:]
    offset = 2 * KVHEADS * HEAD
    input_map = shared[:, offset : offset + NSTATE].astype(BF)
    output_map = shared[:, offset + NSTATE : offset + 2 * NSTATE].astype(BF)
    step_raw = lax.dynamic_slice_in_dim(
        shared, offset + 2 * NSTATE + place.wt * heads, heads, 1
    )
    step_in = step_raw + w.step_bias
    step_sizes = jax.nn.softplus(step_in) * place.live[:, None]
    cum = jnp.dot(place.lower, -w.decay_rate * step_sizes, precision=HIGH)
    local_y, local_state = scan_forward(
        mamba_proj, input_map, output_map, step_sizes, cum, cum.T
    )
    payload = after(state_payload(local_state, cum[-1]), key_all)
    moved = moved_states(payload, False)
    normed_now, small_now = lax.optimization_barrier((normed, small_in, payload))[:2]
    query_proj = mm(normed_now, w.query) + mm(small_now, w.query_up)
    rotated = rotate(query_proj, place.tables, 1.0).astype(BF)
    query_rows = jnp.concatenate(
        [rotated[:, head * HEAD : (head + 1) * HEAD] for head in range(local_heads)], axis=0
    )
    attended, lse = attend_forward(place.scalars, query_rows, key_all, span)
    skip = jnp.repeat(w.skip_gain, MHEAD)[None, :]
    scanned, gated_low, state_in = scan_finish(
        local_y, mamba_proj, output_map, cum, skip, moved
    )
    attended_low = attended.astype(BF)
    small_mid = mm_t(attended_low, w.attnout_down) + mm_t(gated_low, w.mambaout_down)
    part = (
        mm(attended_low, w.attnout) + mm(gated_low, w.mambaout) + mm(small_mid, w.mixout_up)
    )
    saved.keep(
        normed=normed,
        small_in=small_in,
        query_rows=query_rows,
        key_all=key_all,
        key_head=key_head,
        gate_raw=gate_raw,
        inputs=inputs,
        proj=mamba_proj,
        input_map=input_map,
        output_map=output_map,
        step_in=step_in,
        step_sizes=step_sizes,
        cum=cum,
        state_in=state_in,
        scanned=scanned,
        attended=attended,
        lse=lse,
        gated_low=gated_low,
        attended_low=attended_low,
        small_mid=small_mid,
    )
    return part.astype(BF), saved


def feed_forward(entry_low, part, w, place, saved):
    mixed = after(lax.psum(part, "wt"), w.gateup, w.down)
    hidden = entry_low.astype(F32) + place.live[:, None] * mixed.astype(F32)
    feed_normed = (hidden * rms_scale(hidden) * w.feed_gain).astype(BF)
    small_feed = mm_t(feed_normed, w.feedin_down).astype(BF)
    gateup = mm(feed_normed, w.gateup) + mm(small_feed, w.feedin_up)
    width = gateup.shape[1] // 2
    gate_value, up_value = gateup[:, :width], gateup[:, width:]
    inner = (jax.nn.silu(gate_value) * up_value).astype(BF)
    small_out = mm_t(inner, w.feedout_down)
    feed_part = (mm(inner, w.down) + mm(small_out, w.feedout_up)).astype(BF)
    saved.keep(
        hidden=hidden,
        feed_normed=feed_normed,
        small_feed=small_feed,
        gate_value=gate_value,
        up_value=up_value,
        inner=inner,
        small_out=small_out,
    )
    return feed_part


def feed_backward(grad_out, w, place, s, finish):
    grads = Weights()
    grad_feed = grad_out.astype(BF)
    grad_small_out = mm_t(grad_feed, w.feedout_up)
    grad_inner = mm_t(grad_feed, w.down) + mm(grad_small_out, w.feedout_down)
    gate_value, up_value = s.gate_value, s.up_value
    sigmoid_gate = jax.nn.sigmoid(gate_value)
    grad_gate = grad_inner * up_value * sigmoid_gate * (1.0 + gate_value * (1.0 - sigmoid_gate))
    grad_up = grad_inner * gate_value * sigmoid_gate
    grad_gateup = jnp.concatenate([grad_gate, grad_up], axis=1).astype(BF)
    grad_small_feed = mm_t(grad_gateup, w.feedin_up)
    feed_norm_part = mm_t(grad_gateup, w.gateup) + mm(grad_small_feed, w.feedin_down)
    summed = lax.psum(feed_norm_part.astype(BF), "wt")
    small_all = exchange_sum(
        jnp.concatenate(
            [part.astype(BF) for part in (s.small_mid, s.small_out, grad_small_feed)], axis=1
        ),
        "wt",
    )
    rank = grad_small_feed.shape[1]
    s.small_mid = small_all[:, :rank]
    grads.feedout_up = t_mm(small_all[:, rank : 2 * rank], grad_feed)
    grads.feedout_down = t_mm(grad_small_out, s.inner)
    grads.feedin_up = t_mm(s.small_feed, grad_gateup)
    grads.feedin_down = t_mm(small_all[:, 2 * rank :], s.feed_normed)
    found = finish(grads)
    summed = after(summed, found[2]).astype(F32)
    return grad_out + norm_back(s.hidden, summed, w.feed_gain), found


def mixer_backward(grad_hidden, w, place, s, finish, before, late):
    grads = Weights()
    span = grad_hidden.shape[0]
    grad_mixed = (grad_hidden * place.live[:, None]).astype(BF)
    grad_small_mid = mm_t(grad_mixed, w.mixout_up)
    grad_gated = mm_t(grad_mixed, w.mambaout) + mm(grad_small_mid, w.mambaout_down)
    gate_raw, inputs, scanned = s.gate_raw, s.inputs, s.scanned
    skip = jnp.repeat(w.skip_gain, MHEAD)[None, :]
    sigmoid_raw = jax.nn.sigmoid(gate_raw)
    silu_raw = gate_raw * sigmoid_raw
    dy_low = (grad_gated * silu_raw).astype(BF)
    dy = dy_low.astype(F32)
    grad_gates = (
        grad_gated * (scanned + skip * inputs) * sigmoid_raw * (1.0 + gate_raw * (1.0 - sigmoid_raw))
    )
    cum, step_sizes = s.cum, s.step_sizes
    grown = wide(jnp.exp(cum))
    grown_dy = (grown * dy).astype(BF)
    local_grad = t_mm(s.output_map, grown_dy)
    payload = state_payload(local_grad, cum[-1])
    moved = moved_states(payload, True)
    dy_now, grad_mid, small_now = lax.optimization_barrier(
        (dy_low, grad_mixed, grad_small_mid, payload)
    )[:3]

    grad_attended = (
        mm_t(grad_mid, w.attnout) + mm(small_now, w.attnout_down)
    ).astype(BF)
    grad_query, grad_keyval = attend_backward(
        place.scalars, s.query_rows, s.key_all, s.lse, s.attended, grad_attended
    )
    own = returned_rows(after(grad_keyval, *moved), span, place.ctx)

    z_local, db_local, dc_local = scan_backward(
        inputs, dy_now, s.input_map, s.output_map, step_sizes, cum, cum.T
    )
    grad_inputs, grad_map_in, grad_map_out, grad_step = scan_close(
        inputs,
        dy_low,
        z_local,
        scanned,
        s.input_map,
        s.state_in,
        db_local,
        dc_local,
        step_sizes,
        cum,
        s.step_in,
        place.live[:, None],
        w.decay_rate[None, :],
        skip,
        moved,
    )

    heads = cum.shape[1]
    grad_query_low = rotate(grad_query, place.tables, -1.0).astype(BF)
    grad_keys = rotate(own[:, :HEAD], place.tables, -1.0)
    key_head = s.key_head
    offset = 2 * KVHEADS * HEAD
    keyval = jnp.zeros((span, offset), F32)
    keyval = lax.dynamic_update_slice_in_dim(keyval, grad_keys, key_head * HEAD, 1)
    keyval = lax.dynamic_update_slice_in_dim(
        keyval, own[:, HEAD:], (KVHEADS + key_head) * HEAD, 1
    )
    all_heads = w.shared.shape[1] - offset - 2 * NSTATE
    step_part = lax.dynamic_update_slice_in_dim(
        jnp.zeros((span, all_heads), F32), grad_step, place.wt * heads, 1
    )
    grad_shared = jnp.concatenate(
        [keyval.astype(BF), grad_map_in, grad_map_out, step_part.astype(BF)], axis=1
    )
    grad_mamba = jnp.concatenate([grad_gates.astype(BF), grad_inputs], axis=1)
    grad_small_in = (
        mm_t(grad_query_low, w.query_up)
        + mm_t(grad_mamba, w.mamba_up)
        + mm_t(grad_shared, w.shared_up)
    )
    norm_part = (
        mm_t(grad_query_low, w.query)
        + mm_t(grad_mamba, w.mamba)
        + mm_t(grad_shared, w.shared)
        + mm(grad_small_in, w.mixin_down)
    )
    norm_part = after(norm_part.astype(BF), *before)
    summed = lax.psum(norm_part, "wt")
    grads.mixout_up = t_mm(s.small_mid, grad_mixed)
    grads.attnout_down = t_mm(grad_small_mid, s.attended_low)
    grads.mambaout_down = t_mm(grad_small_mid, s.gated_low)
    grads.query_up = t_mm(s.small_in, grad_query_low)
    grads.mamba_up = t_mm(s.small_in, grad_mamba)
    grads.shared_up = t_mm(s.small_in, grad_shared)
    grads.mixin_down = t_mm(grad_small_in, s.normed)
    found = finish(grads, *((summed,) if late else ()))
    grad_entry = grad_hidden + norm_back(
        s.entry.astype(F32), summed.astype(F32), w.mixer_gain
    )
    return grad_entry, found


FIXED = (
    "mixer_gain",
    "feed_gain",
    "decay_rate",
    "step_bias",
    "skip_gain",
    "query",
    "mamba",
    "shared",
    "attnout",
    "mambaout",
    "gateup",
    "down",
)
ADAPTERS = (
    "mixin_down",
    "query_up",
    "mamba_up",
    "shared_up",
    "attnout_down",
    "mambaout_down",
    "mixout_up",
    "feedin_down",
    "feedin_up",
    "feedout_down",
    "feedout_up",
)
PARTIAL = ("mixin_down", "shared_up")
PACKS = (
    ("mixin_down", "mamba_up", "query_up", "shared_up"),
    ("mixout_up", "mambaout_down", "attnout_down"),
    ("feedin_down", "feedin_up", "feedout_up", "feedout_down"),
)
GROUPS = (
    ("shared", "query", "mamba"),
    ("attnout", "mambaout"),
    ("gateup", "down"),
)


def shards(layer_input, cotangent, seq_lengths, adapter_ids, *params):
    section = lax.axis_index("section")
    ctx_index = lax.axis_index("ctx")
    micro_count, span = layer_input.shape[0], layer_input.shape[1]
    assert micro_count == 2 and lax.axis_size("section") == 2

    place = Weights()
    place.wt = lax.axis_index("wt")
    place.ctx = ctx_index
    length = seq_lengths[section]
    positions = ctx_index * span + jnp.arange(span, dtype=jnp.int32)
    place.live = (positions < length).astype(F32)
    place.tables = rope_tables(positions)
    row = lax.broadcasted_iota(jnp.int32, (span, span), 0)
    col = lax.broadcasted_iota(jnp.int32, (span, span), 1)
    place.lower = (row >= col).astype(F32)
    blocks = jnp.minimum(
        ((ctx_index + 1) * span + KEY_BLOCK - 1) // KEY_BLOCK, (length + KEY_BLOCK - 1) // KEY_BLOCK
    )
    place.scalars = jnp.stack([length, ctx_index, blocks]).astype(jnp.int32)

    own, items, shapes = {}, {}, {}
    for name, item in zip(FIXED, params):
        own[name] = item[0]
    mine, theirs = adapter_ids[section], adapter_ids[1 - section]
    for name, item in zip(ADAPTERS, params[len(FIXED) :]):
        shapes[name] = item.shape[1:]
        items[name] = item[0]
    layers = (Weights(), Weights())

    def place_pack(names, widths, kept, moved):
        for index, w in enumerate(layers):
            value = jnp.where(section == index, kept, moved)
            start = 0
            for name, width in zip(names, widths):
                setattr(w, name, value[..., start : start + width])
                start += width

    def exchange_pack(number, *gates):
        names = PACKS[number]
        widths = [items[name][0, 0].size for name in names]
        packed = jnp.concatenate(
            [items[name].reshape(items[name].shape[:2] + (-1,)) for name in names], axis=2
        )
        packed = lax.optimization_barrier((packed,) + gates)[0]
        moved = swap(lax.dynamic_index_in_dim(packed, theirs, 0, keepdims=False))
        kept = lax.dynamic_index_in_dim(packed, mine, 0, keepdims=False)
        place_pack(names, widths, kept, moved)

    vectors = FIXED[:5]
    joined = jnp.concatenate([own[name].astype(F32) for name in vectors])
    place_pack(vectors, [own[name].size for name in vectors], joined, swap(joined))
    exchange_pack(0)
    done = []
    for group in GROUPS:
        moved = {name: swap(after(own[name], *done)) for name in group}
        done = done or list(moved.values())
        for name in group:
            for index, w in enumerate(layers):
                value = jnp.where(section == index, own[name], moved[name])
                if value.ndim == 3:
                    value = value.reshape(value.shape[0], -1)
                setattr(w, name, lax.optimization_barrier(value))
    exchange_pack(1, *done)

    first, second = layers
    entry = lax.dynamic_index_in_dim(layer_input, section, 0, keepdims=False)
    part, saved_first = mixer_forward(entry, first, place)
    exchange_pack(2, part)
    feed_part = feed_forward(entry, part, first, place, saved_first)
    following = [getattr(second, name) for name in GROUPS[0] + GROUPS[1]]
    fed = after(lax.psum(feed_part, "wt"), *following)
    first_out = (saved_first.hidden + fed.astype(F32)).astype(BF)
    part, saved_second = mixer_forward(first_out, second, place)
    last_part = feed_forward(first_out, part, second, place, saved_second)

    def forth(value):
        return lax.ppermute(value, "section", [(0, 1)])

    def back(value):
        return lax.ppermute(value, "section", [(1, 0)])

    def reduced(found):
        names = list(found)
        packed = jnp.concatenate(
            [found[name].astype(BF).reshape(found[name].shape[0], -1) for name in names], axis=1
        )
        return names, [found[name].shape[1] for name in names], packed

    def summed_grads(grads, *gates):
        found = vars(grads)
        partial = {name: found[name] for name in found if name in PARTIAL}
        whole = {name: found[name] for name in found if name not in PARTIAL}
        names, widths, packed = reduced(whole)
        packed = after(packed, *gates)
        if partial:
            more, extra, part = reduced(partial)
            part = after(part, *gates)
            names, widths = names + more, widths + extra
            packed = jnp.concatenate([packed, exchange_sum(part, "wt")], axis=1)
        return names, widths, exchange_sum(packed, "ctx")

    grad = lax.dynamic_index_in_dim(cotangent, section, 0, keepdims=False).astype(F32)
    grad_hidden, found = feed_backward(grad, second, place, saved_second, summed_grads)
    second_sets = [found]
    last_part = after(last_part, grad_hidden)
    second_out = (saved_second.hidden + low_sum(last_part)).astype(BF)
    grad, found = mixer_backward(
        grad_hidden, second, place, saved_second, summed_grads, (second_out,), True
    )
    second_grad = grad.astype(BF)
    second_sets.append(found)
    grad_hidden, found = feed_backward(
        second_grad.astype(F32), first, place, saved_first, summed_grads
    )
    first_sets = [found]
    grad, found = mixer_backward(
        grad_hidden, first, place, saved_first, summed_grads, (), False
    )
    first_grad = grad.astype(BF)
    first_sets.append(found)

    def stacked(early, late):
        return jnp.where(
            section == 0, jnp.stack([early, back(early)]), jnp.stack([forth(late), late])
        )[None]

    found = {}
    adapters = jnp.arange(params[len(FIXED)].shape[1], dtype=jnp.int32)[:, None, None]
    for first_set, second_set in zip(first_sets, second_sets):
        keep = jnp.where(section == 0, first_set[2], second_set[2])
        moved = jnp.where(section == 0, back(first_set[2]), forth(second_set[2]))
        start = 0
        for name, width in zip(first_set[0], first_set[1]):
            lanes = slice(start, start + width)
            start += width
            total = jnp.where(adapters == mine, keep[None, :, lanes].astype(F32), 0.0)
            total = total + jnp.where(adapters == theirs, moved[None, :, lanes].astype(F32), 0.0)
            found[name] = total.reshape(shapes[name])[None]
    return (
        stacked(first_out, second_out),
        stacked(first_grad, second_grad),
    ) + tuple(found[name] for name in ADAPTERS)


def solution(mesh):
    in_specs = (
        P(None, "ctx", None),
        P(None, "ctx", None),
        P(),
        P(),
        P("section", None),
        P("section", None),
        P("section", "wt"),
        P("section", "wt"),
        P("section", "wt"),
        P("section", None, "wt"),
        P("section", None, None, "wt"),
        P("section", None, None),
        P("section", "wt", None),
        P("section", "wt", None),
        P("section", None, None, "wt"),
        P("section", "wt", None),
        P("section", None, None, None),
        P("section", None, None, "wt"),
        P("section", None, None, None, "wt"),
        P("section", None, None, None),
        P("section", None, None, "wt"),
        P("section", None, None, "wt"),
        P("section", None, None, None),
        P("section", None, None, None),
        P("section", None, None, None, "wt"),
        P("section", None, None, "wt"),
        P("section", None, None, None),
    )
    out_specs = (
        P("section", None, "ctx", None),
        P("section", None, "ctx", None),
    ) + in_specs[16:]
    return jax.shard_map(shards, mesh=mesh, in_specs=in_specs, out_specs=out_specs, check_vma=False)
```
